128 devices in a mesh: slab: 32 (over z, x, core), cross: 4 (over y).
Axes of the slice: x: 4, y: 4, z: 4, core: 2. Of those that a mesh axis runs over, the one named last changes fastest.
Arguments:
- velocity: float32 [3, 512, 256, 256], P(None, 'slab', 'cross'), may hold values from -6 to 6
- shape_weight: float32 [32, 384], replicated, may hold values from -6 to 6
- w_in: bfloat16 [384, 1024], replicated, may hold values from -0.3125 to 0.3125
- w_out: bfloat16 [1024, 4096], replicated, may hold values from -0.1875 to 0.1875
- decay: float32 [1024], replicated, may hold values from 0.1 to 2
- rotor_states: float32 [32, 1024], P('slab'), may hold values from -6 to 6
- slot_of_rotor: int32 [32], replicated, may hold values from 0 to 31, each once
- entry_rotor: int32 [131072, 1], P(('slab', 'cross')), may hold values from 0 to 31; in each aligned block of 1024 rows (0 to 1023, 1024 to 2047, ...) at most 64 rows name the same one
- entry_tile: int32 [131072], P(('slab', 'cross')), may hold values from 0 to 2047
- entry_sub: int32 [131072], P(('slab', 'cross')), may hold values from 0 to 31
Outputs:
- advanced: float32 [3, 512, 256, 256], P(None, 'slab', 'cross')
- new_states: float32 [32, 1024], P('slab')
The draws below stay inside these ranges and needn't reach their ends.
Inputs may be any that keep to these rules, and one draw needn't show every extreme that they name: `entry_rotor`: in the rows of one device no rotor is named more than 64 times, a bound that some block reaches; every rotor is named by some entry. Each slot once; rotor r is owned by slab slot_of_rotor[r].
All inputs are finite; a program needn't handle non-finite values.
Results may differ from the reference program's by a relative error of at most 0.0026.
Values may be sent and summed in bfloat16 or wider, within the bound.
A program may use at most 64 MiB of HBM per device.

```python
import math
import jax
import jax.numpy as jnp
import numpy as np
from jax import lax

CX = 16
CY = 64
NZ = 256
TILE = 128
R = 32
S = 1024
NSRC = 4096
E_DEV = 1024
CAP = 64
NSUB = 32
TILES_DEV = 2048
NX = 512
NY = 256
ENTRIES = 131072
N_CROSS = 4


def set_ends(values, own_key, smallest, high):
    dims = values.shape
    place = [jax.random.randint(jax.random.fold_in(own_key, axis), (), 0, dims[axis]) for axis in range(len(dims))]
    values = values.at[tuple(place)].set(smallest)
    longest = dims.index(max(dims))
    place[longest] = (place[longest] + 1) % dims[longest]
    return values.at[tuple(place)].set(high)


def level_of(stream_key, shape, split, smallest, top_value):
    factor_of, own = 1.0, jax.random.fold_in(stream_key, 6)
    for dim, parts in split:
        heights = jnp.exp(jax.random.uniform(jax.random.fold_in(own, dim), (parts,), jnp.float32, smallest / len(split), top_value / len(split)))
        factor_of = factor_of * jnp.repeat(heights, shape[dim] // parts).reshape([-1 if axis == dim else 1 for axis in range(len(shape))])
    return factor_of


def deal_out(key, own, number, rows, amount, top, limit, skew):
    order = jax.random.permutation(key, amount)
    heavy_load, usual = load_shares(amount, rows * top, limit, skew, True), load_shares(amount, rows * top, limit, skew, False)
    places = jnp.arange(amount)

    def named(lengths, turn):
        used = int((lengths > 0).sum())
        fixed = max(1, used // 4)
        shifted = fixed + (places - fixed + turn * (used - fixed)) % max(1, amount - fixed)
        return jnp.zeros((amount,), jnp.int32).at[order[jnp.where(places < fixed, places, shifted)]].set(jnp.asarray(lengths, jnp.int32))

    lengths = jnp.where(number % 4 == 0, named(heavy_load, number // 4), named(usual, number - number // 4 - 1))
    mixed = jax.random.permutation(jax.random.fold_in(own, 3), amount)
    giver, taker = mixed[0:amount // 2 * 2:2], mixed[1:amount // 2 * 2:2]
    room = jnp.minimum(lengths[giver] - 1, limit - lengths[taker]) // 2
    room = jnp.where((giver == order[0]) | (taker == order[0]) | (lengths[taker] == 0), 0, jnp.maximum(room, 0))
    shifted = jax.random.randint(jax.random.fold_in(own, 4), (amount // 2,), 0, 1 << 20) % (room + 1)
    lengths = lengths.at[giver].add(-shifted).at[taker].add(shifted)
    items = jnp.searchsorted(jnp.cumsum(lengths), jnp.arange(rows * top), side="right").astype(jnp.int32)
    listing = items.reshape(top, rows).T
    listing = listing[jax.random.permutation(jax.random.fold_in(own, 1), rows)]
    turn = jax.random.randint(jax.random.fold_in(own, 2), (rows, 1), 0, top)
    return jnp.take_along_axis(listing, (jnp.arange(top)[None, :] + turn) % top, axis=1)


def load_shares(number_of, total, most, lean, full):
    loads = [(1 << 20) // math.isqrt(rank ** lean) + 1 for rank in range(1, number_of + 1)]
    largest = most if full else min(most, max(-(-total // number_of), total * loads[0] // sum(loads)))
    least = 1 if total - largest >= number_of - 1 else 0
    counts, rest = [largest] + [least] * (number_of - 1), total - largest - least * (number_of - 1)
    while rest > 0:
        candidates = [i for i in range(1, number_of) if counts[i] < largest] or [i for i in range(1, number_of) if counts[i] < most]
        pool, remaining = sum([loads[i] for i in candidates]), rest
        for i in candidates:
            addition = min(most - counts[i], max(1, remaining * loads[i] // pool), rest)
            counts[i] = counts[i] + addition
            rest = rest - addition
    return np.array(counts)


def noise(stream_key, extent, scale, reach, split=(), kind=jnp.bfloat16):
    loudness = level_of(stream_key, extent, split, -0.22, 0.18) if split else 1.0
    values = jax.random.normal(stream_key, extent, jnp.float32) * scale * loudness
    return jnp.minimum(jnp.maximum(values, -reach), reach).astype(kind)


def setup_inputs(seed: int = 0) -> dict:
    key_of = jax.random.split(jax.random.key(seed), 11)
    velocity = noise(key_of[0], (3, NX, NY, NZ), 1.0, 6.0, ((1, 32), (2, 4)), jnp.float32)
    shape_weight = noise(key_of[1], (NSUB, 3 * TILE), 1.0, 6.0, (), jnp.float32)
    w_in = noise(key_of[2], (3 * TILE, S), (3 * TILE) ** -0.5, 0.3125)
    w_out = noise(key_of[3], (S, NSRC), S ** -0.5, 0.1875)
    decay = jnp.clip(jnp.exp(jax.random.uniform(key_of[4], (S,), jnp.float32, math.log(0.1), math.log(2.0))), 0.1, 2.0)
    rotor_states = noise(key_of[5], (R, S), 1.0, 6.0, ((0, 32),), jnp.float32)
    slot_of_rotor = jax.random.permutation(key_of[6], R).astype(jnp.int32)
    entry_rotor_keys = jax.random.split(jax.random.fold_in(key_of[7], 1), ENTRIES // E_DEV)
    entry_rotor_turns = jax.random.permutation(jax.random.fold_in(key_of[7], 3), ENTRIES // E_DEV)
    entry_rotor = jax.vmap(lambda own, number: deal_out(jax.random.fold_in(key_of[7], 2), own, number, E_DEV, R, 1, CAP, 2))(entry_rotor_keys, entry_rotor_turns).reshape((ENTRIES, 1))
    entry_tile = set_ends(jax.random.randint(key_of[8], (ENTRIES,), 0, TILES_DEV), jax.random.fold_in(key_of[8], 1), 0, TILES_DEV - 1).astype(jnp.int32)
    entry_sub = set_ends(jax.random.randint(key_of[9], (ENTRIES,), 0, NSUB), jax.random.fold_in(key_of[9], 1), 0, NSUB - 1).astype(jnp.int32)
    return dict(velocity=velocity, shape_weight=shape_weight, w_in=w_in, w_out=w_out, decay=decay, rotor_states=rotor_states, slot_of_rotor=slot_of_rotor, entry_rotor=entry_rotor, entry_tile=entry_tile, entry_sub=entry_sub)


time_step = 0.1
viscosity = 0.3
pool_scale = 1.0 / 64.0
state_step = 0.5
force_scale = 0.5


def stencil_core(velocity, padded):
    east = padded[:, 2:, 1:-1, 1:-1]
    west = padded[:, :-2, 1:-1, 1:-1]
    north = padded[:, 1:-1, 2:, 1:-1]
    south = padded[:, 1:-1, :-2, 1:-1]
    upper = padded[:, 1:-1, 1:-1, 2:]
    lower = padded[:, 1:-1, 1:-1, :-2]
    laplace = east + west + north + south + upper + lower - 6.0 * velocity
    advect = velocity[0:1] * ((east - west) * 0.5) + velocity[1:2] * ((north - south) * 0.5) + velocity[2:3] * ((upper - lower) * 0.5)
    return velocity + time_step * (viscosity * laplace - advect)


def reference(velocity, shape_weight, w_in, w_out, decay, rotor_states, slot_of_rotor, entry_rotor, entry_tile, entry_sub):
    ztiles = NZ // TILE
    entries = entry_tile.shape[0]
    position = jnp.arange(entries, dtype=jnp.int32)
    device = position // E_DEV
    slab_id = device // N_CROSS
    cross_id = device % N_CROSS
    xpos = slab_id * CX + entry_tile // (CY * ztiles)
    ypos = cross_id * CY + (entry_tile // ztiles) % CY
    zpos = entry_tile % ztiles
    cells = velocity.reshape(3, NX, NY, ztiles, TILE)
    picked = cells[:, xpos, ypos, zpos, :].astype(jnp.bfloat16)
    picked = lax.optimization_barrier(picked).astype(jnp.float32)
    samples = jnp.transpose(picked, (1, 0, 2)).reshape(entries, 3 * TILE)
    weighted = shape_weight[entry_sub] * samples
    slots = slot_of_rotor[entry_rotor[:, 0]]
    pooled = jax.ops.segment_sum(weighted, slots, num_segments=R)
    pooled_b = (pooled * pool_scale).astype(jnp.bfloat16)
    drive = jnp.dot(pooled_b, w_in, preferred_element_type=jnp.float32)
    new_states = rotor_states + state_step * (drive - decay[None, :] * rotor_states)
    sources = jnp.dot(new_states.astype(jnp.bfloat16), w_out, preferred_element_type=jnp.float32).astype(jnp.bfloat16)
    rows = sources.reshape(R * NSUB, TILE)[slots * NSUB + entry_sub].astype(jnp.float32)
    forcing = jnp.zeros((NX, NY, ztiles, TILE), jnp.float32).at[xpos, ypos, zpos].add(rows)
    padded = jnp.pad(velocity, ((0, 0), (1, 1), (1, 1), (1, 1)))
    advanced = stencil_core(velocity, padded)
    advanced = advanced.at[0].add(-force_scale * forcing.reshape(NX, NY, NZ))
    return advanced, new_states
```

```python
import jax
import jax.numpy as jnp
from jax import lax
from jax.sharding import PartitionSpec as P

TILE = 128
R = 32
NSUB = 32


time_step = 0.1
viscosity = 0.3
pool_scale = 1.0 / 64.0
state_step = 0.5
force_scale = 0.5


def ring_perm(size, stride, n, shift):
    pairs = []
    for s in range(size):
        base = (s // (stride * n)) * stride * n + s % stride
        pos = (s // stride) % n
        pairs.append((s, base + ((pos + shift) % n) * stride))
    return pairs


def ring_sum(value, axis, stride, n):
    size = lax.axis_size(axis)
    if n == 2:
        return value + lax.ppermute(value, axis, ring_perm(size, stride, n, 1))
    got = [lax.ppermute(value, axis, ring_perm(size, stride, n, j)) for j in (1, 2, 3)]
    return (value + got[1]) + (got[0] + got[2])


def ring_gather(value, axis, stride, n):
    size = lax.axis_size(axis)
    pos = (lax.axis_index(axis) // stride) % n
    got = [value] + [lax.ppermute(value, axis, ring_perm(size, stride, n, j)) for j in range(1, n)]
    parts = []
    for p in range(n):
        pick = got[0]
        for j in range(1, n):
            pick = jnp.where((pos - j) % n == p, got[j], pick)
        parts.append(jnp.where(pos == p, got[0], pick))
    return jnp.concatenate(parts, axis=0)


def mesh_rings():
    slab = lax.axis_size("slab")
    rings = [("slab", 1, 2), ("slab", 2, 4), ("slab", 8, slab // 8)]
    return rings


def all_sum(value):
    for axis, stride, n in mesh_rings() + [("cross", 1, lax.axis_size("cross"))]:
        value = ring_sum(value, axis, stride, n)
    return value


def slab_gather(value):
    parts = value
    for axis, stride, n in mesh_rings():
        parts = ring_gather(parts, axis, stride, n)
    return parts


def extended(cells, sides, width):
    for axis, dim in sides:
        count = lax.axis_size(axis)
        ends = count - 1
        head = lax.slice_in_dim(cells, 0, width, axis=dim)
        tail = lax.slice_in_dim(cells, cells.shape[dim] - width, cells.shape[dim], axis=dim)
        cells = jnp.concatenate(
            [
                lax.ppermute(tail, axis, [(i, (i + 1) % count) for i in range(ends)]),
                cells,
                lax.ppermute(head, axis, [((i + 1) % count, i) for i in range(ends)]),
            ],
            axis=dim,
        )
    return cells


def combine_terms(velocity, east, west, north, south, upper, lower):
    laplace = east + west + north + south + upper + lower - 6.0 * velocity
    advect = (
        velocity[0:1] * ((east - west) * 0.5)
        + velocity[1:2] * ((north - south) * 0.5)
        + velocity[2:3] * ((upper - lower) * 0.5)
    )
    return velocity + time_step * (viscosity * laplace - advect)


def on_device(
    velocity,
    shape_weight,
    w_in,
    w_out,
    decay,
    rotor_states,
    slot_of_rotor,
    entry_rotor,
    entry_tile,
    entry_sub,
):
    local_x, local_y, local_z = (velocity.shape[1], velocity.shape[2], velocity.shape[3])
    tile_count = local_x * local_y * local_z // TILE
    all_states = slab_gather(rotor_states)
    rotor_hot = (entry_rotor == jnp.arange(R, dtype=jnp.int32)[None, :]).astype(jnp.int32)
    slots = jnp.sum(rotor_hot * slot_of_rotor[None, :], axis=1)
    sub_range = jnp.arange(NSUB, dtype=jnp.int32)
    sub_hot = (entry_sub[:, None] == sub_range[None, :]).astype(jnp.float32)
    gains = jnp.dot(sub_hot, shape_weight, precision=lax.Precision.HIGHEST)
    slot_hot = (slots[:, None] == jnp.arange(R, dtype=jnp.int32)[None, :]).astype(jnp.float32)
    per_rotor = []
    for c in range(3):
        cells = velocity[c].reshape(tile_count, TILE)
        picked = jnp.take(cells, entry_tile, axis=0).astype(jnp.bfloat16).astype(jnp.float32)
        weighted = gains[:, c * TILE:(c + 1) * TILE] * picked
        per_rotor.append(jnp.dot(slot_hot.T, weighted, precision=lax.Precision.HIGHEST))
    per_rotor = jnp.concatenate(per_rotor, axis=1)
    pooled = all_sum(per_rotor)
    pooled_b = (pooled * pool_scale).astype(jnp.bfloat16)
    drive = jnp.dot(pooled_b, w_in, preferred_element_type=jnp.float32)
    all_new = all_states + state_step * (drive - decay[None, :] * all_states)
    all_sources = jnp.dot(
        all_new.astype(jnp.bfloat16), w_out, preferred_element_type=jnp.float32
    ).astype(jnp.bfloat16)
    new_states = lax.dynamic_slice_in_dim(all_new, lax.axis_index("slab"), 1, axis=0)
    rows = all_sources.reshape(R * NSUB, TILE)[slots * NSUB + entry_sub]
    tile_hot = (jnp.arange(tile_count, dtype=jnp.int32)[:, None] == entry_tile[None, :]).astype(jnp.bfloat16)
    forcing = jnp.dot(tile_hot, rows, preferred_element_type=jnp.float32)
    vertical = jnp.pad(velocity, ((0, 0), (0, 0), (0, 0), (1, 1)))
    upper = vertical[:, :, :, 2:]
    lower = vertical[:, :, :, :-2]
    padded = extended(velocity.astype(jnp.bfloat16), (("slab", 1), ("cross", 2)), 1).astype(
        velocity.dtype
    )
    east = padded[:, 2:, 1:-1, :]
    west = padded[:, :-2, 1:-1, :]
    north = padded[:, 1:-1, 2:, :]
    south = padded[:, 1:-1, :-2, :]
    advanced = combine_terms(velocity, east, west, north, south, upper, lower)
    advanced = advanced.at[0].add(-force_scale * forcing.reshape(local_x, local_y, local_z))
    return (advanced, new_states)


def solution(mesh):
    in_specs = (
        P(None, "slab", "cross", None),
        P(),
        P(),
        P(),
        P(),
        P("slab", None),
        P(),
        P(("slab", "cross"), None),
        P(("slab", "cross")),
        P(("slab", "cross")),
    )
    out_specs = (P(None, "slab", "cross", None), P("slab", None))
    return jax.shard_map(
        on_device, mesh=mesh, in_specs=in_specs, out_specs=out_specs, check_vma=False
    )
```

```python
import jax
import jax.numpy as jnp
from jax import lax
from jax.experimental import pallas as pl
from jax.experimental.pallas import tpu as pltpu
from jax.sharding import PartitionSpec as P

MESH = pl.DeviceIdType.MESH

TILE = 128
R = 32
NSUB = 32


time_step = 0.1
viscosity = 0.3
pool_scale = 1.0 / 64.0
state_step = 0.5
force_scale = 0.5


def ring_perm(size, stride, n, shift):
    pairs = []
    for s in range(size):
        base = (s // (stride * n)) * stride * n + s % stride
        pos = (s // stride) % n
        pairs.append((s, base + ((pos + shift) % n) * stride))
    return pairs


def ring_sum(value, axis, stride, n):
    size = lax.axis_size(axis)
    if n == 2:
        return value + lax.ppermute(value, axis, ring_perm(size, stride, n, 1))
    got = [lax.ppermute(value, axis, ring_perm(size, stride, n, j)) for j in (1, 2, 3)]
    return (value + got[1]) + (got[0] + got[2])


def ring_gather(value, axis, stride, n):
    size = lax.axis_size(axis)
    pos = (lax.axis_index(axis) // stride) % n
    got = [value] + [lax.ppermute(value, axis, ring_perm(size, stride, n, j)) for j in range(1, n)]
    parts = []
    for p in range(n):
        pick = got[0]
        for j in range(1, n):
            pick = jnp.where((pos - j) % n == p, got[j], pick)
        parts.append(jnp.where(pos == p, got[0], pick))
    return jnp.concatenate(parts, axis=0)


def mesh_rings():
    slab = lax.axis_size("slab")
    rings = [("slab", 1, 2), ("slab", 2, 4), ("slab", 8, slab // 8)]
    return rings


def all_sum(value):
    for axis, stride, n in mesh_rings() + [("cross", 1, lax.axis_size("cross"))]:
        value = ring_sum(value, axis, stride, n)
    return value


def slab_gather(value):
    parts = value
    for axis, stride, n in mesh_rings():
        parts = ring_gather(parts, axis, stride, n)
    return parts


def ring_rounds(slab, cross):
    return [(0, 1, 2), (0, 2, 4), (0, 8, slab // 8), (1, 1, cross)]


def partner(me, stride, n, shift):
    pos = (me // stride) % n
    return me - pos * stride + ((pos + shift) % n) * stride


def reduce_gather_kernel(rounds, per_ref, st_ref, pooled_ref, states_ref, held, sends, recvs, st_sends, st_recvs):
    here = (lax.axis_index("slab"), lax.axis_index("cross"))

    def device(axis, other):
        return (other, here[1]) if axis == 0 else (here[0], other)

    barrier = pltpu.get_barrier_semaphore()
    count = 0
    for axis, stride, n in rounds:
        for j in range(1, n):
            pl.semaphore_signal(barrier, inc=1, device_id=device(axis, partner(here[axis], stride, n, j)), device_id_type=MESH)
            count += 1
    pl.semaphore_wait(barrier, count)

    me = here[0]
    states_ref[pl.ds(me, 1)] = st_ref[...][None]
    pooled_ref[...] = per_ref[...]
    for r, (axis, stride, n) in enumerate(rounds):
        if n == 1:
            continue
        copies = []
        for j in range(1, n):
            dev = device(axis, partner(here[axis], stride, n, j))
            copy = pltpu.make_async_remote_copy(
                src_ref=pooled_ref,
                dst_ref=held.at[r, j - 1],
                send_sem=sends.at[r, j - 1],
                recv_sem=recvs.at[r, j - 1],
                device_id=dev,
                device_id_type=MESH,
            )
            copy.start()
            copies.append(copy)
            if axis == 0:
                rows = pl.ds(me - me % stride, stride)
                block = pltpu.make_async_remote_copy(
                    src_ref=states_ref.at[rows],
                    dst_ref=states_ref.at[rows],
                    send_sem=st_sends.at[r, j - 1],
                    recv_sem=st_recvs.at[r, j - 1],
                    device_id=dev,
                    device_id_type=MESH,
                )
                block.start()
                copies.append(block)
        for copy in copies:
            copy.wait()
        if n == 2:
            total = pooled_ref[...] + held[r, 0]
        else:
            total = (pooled_ref[...] + held[r, 1]) + (held[r, 0] + held[r, 2])
        pooled_ref[...] = total


def reduce_gather(per_rotor, rotor_states):
    slab, cross = lax.axis_size("slab"), lax.axis_size("cross")
    rounds = ring_rounds(slab, cross)
    vmem = pl.BlockSpec(memory_space=pltpu.VMEM)
    return pl.pallas_call(
        lambda *refs: reduce_gather_kernel(rounds, *refs),
        out_shape=(
            jax.ShapeDtypeStruct(per_rotor.shape, jnp.float32),
            jax.ShapeDtypeStruct((slab,) + rotor_states.shape, jnp.float32),
        ),
        in_specs=[vmem, vmem],
        out_specs=(vmem, vmem),
        scratch_shapes=[
            pltpu.VMEM((len(rounds), 3) + per_rotor.shape, jnp.float32),
            pltpu.SemaphoreType.DMA((len(rounds), 3)),
            pltpu.SemaphoreType.DMA((len(rounds), 3)),
            pltpu.SemaphoreType.DMA((len(rounds), 3)),
            pltpu.SemaphoreType.DMA((len(rounds), 3)),
        ],
        compiler_params=pltpu.CompilerParams(collective_id=0, has_side_effects=True),
    )(per_rotor, rotor_states)


def extended(cells, sides, width):
    for axis, dim in sides:
        count = lax.axis_size(axis)
        ends = count - 1
        head = lax.slice_in_dim(cells, 0, width, axis=dim)
        tail = lax.slice_in_dim(cells, cells.shape[dim] - width, cells.shape[dim], axis=dim)
        cells = jnp.concatenate(
            [
                lax.ppermute(tail, axis, [(i, (i + 1) % count) for i in range(ends)]),
                cells,
                lax.ppermute(head, axis, [((i + 1) % count, i) for i in range(ends)]),
            ],
            axis=dim,
        )
    return cells


def combine_terms(velocity, east, west, north, south, upper, lower):
    laplace = east + west + north + south + upper + lower - 6.0 * velocity
    advect = (
        velocity[0:1] * ((east - west) * 0.5)
        + velocity[1:2] * ((north - south) * 0.5)
        + velocity[2:3] * ((upper - lower) * 0.5)
    )
    return velocity + time_step * (viscosity * laplace - advect)


def on_device(
    velocity,
    shape_weight,
    w_in,
    w_out,
    decay,
    rotor_states,
    slot_of_rotor,
    entry_rotor,
    entry_tile,
    entry_sub,
):
    local_x, local_y, local_z = (velocity.shape[1], velocity.shape[2], velocity.shape[3])
    tile_count = local_x * local_y * local_z // TILE
    rotor_hot = (entry_rotor == jnp.arange(R, dtype=jnp.int32)[None, :]).astype(jnp.int32)
    slots = jnp.sum(rotor_hot * slot_of_rotor[None, :], axis=1)
    sub_range = jnp.arange(NSUB, dtype=jnp.int32)
    sub_hot = (entry_sub[:, None] == sub_range[None, :]).astype(jnp.float32)
    gains = jnp.dot(sub_hot, shape_weight, precision=lax.Precision.HIGHEST)
    slot_hot = (slots[:, None] == jnp.arange(R, dtype=jnp.int32)[None, :]).astype(jnp.float32)
    per_rotor = []
    for c in range(3):
        cells = velocity[c].reshape(tile_count, TILE)
        picked = jnp.take(cells, entry_tile, axis=0).astype(jnp.bfloat16).astype(jnp.float32)
        weighted = gains[:, c * TILE:(c + 1) * TILE] * picked
        per_rotor.append(jnp.dot(slot_hot.T, weighted, precision=lax.Precision.HIGHEST))
    per_rotor = jnp.concatenate(per_rotor, axis=1)
    pooled, all_states = reduce_gather(per_rotor, rotor_states)
    all_states = all_states.reshape(-1, rotor_states.shape[1])
    pooled_b = (pooled * pool_scale).astype(jnp.bfloat16)
    drive = jnp.dot(pooled_b, w_in, preferred_element_type=jnp.float32)
    all_new = all_states + state_step * (drive - decay[None, :] * all_states)
    all_sources = jnp.dot(
        all_new.astype(jnp.bfloat16), w_out, preferred_element_type=jnp.float32
    ).astype(jnp.bfloat16)
    new_states = lax.dynamic_slice_in_dim(all_new, lax.axis_index("slab"), 1, axis=0)
    rows = all_sources.reshape(R * NSUB, TILE)[slots * NSUB + entry_sub]
    tile_hot = (jnp.arange(tile_count, dtype=jnp.int32)[:, None] == entry_tile[None, :]).astype(jnp.bfloat16)
    forcing = jnp.dot(tile_hot, rows, preferred_element_type=jnp.float32)
    vertical = jnp.pad(velocity, ((0, 0), (0, 0), (0, 0), (1, 1)))
    upper = vertical[:, :, :, 2:]
    lower = vertical[:, :, :, :-2]
    padded = extended(velocity.astype(jnp.bfloat16), (("slab", 1), ("cross", 2)), 1).astype(
        velocity.dtype
    )
    east = padded[:, 2:, 1:-1, :]
    west = padded[:, :-2, 1:-1, :]
    north = padded[:, 1:-1, 2:, :]
    south = padded[:, 1:-1, :-2, :]
    advanced = combine_terms(velocity, east, west, north, south, upper, lower)
    advanced = advanced.at[0].add(-force_scale * forcing.reshape(local_x, local_y, local_z))
    return (advanced, new_states)


def solution(mesh):
    in_specs = (
        P(None, "slab", "cross", None),
        P(),
        P(),
        P(),
        P(),
        P("slab", None),
        P(),
        P(("slab", "cross"), None),
        P(("slab", "cross")),
        P(("slab", "cross")),
    )
    out_specs = (P(None, "slab", "cross", None), P("slab", None))
    return jax.shard_map(
        on_device, mesh=mesh, in_specs=in_specs, out_specs=out_specs, check_vma=False
    )
```

```python
import jax
import jax.numpy as jnp
from jax import lax
from jax.experimental import pallas as pl
from jax.experimental.pallas import tpu as pltpu
from jax.sharding import PartitionSpec as P

MESH = pl.DeviceIdType.MESH

TILE = 128
R = 32
NSUB = 32


time_step = 0.1
viscosity = 0.3
pool_scale = 1.0 / 64.0
state_step = 0.5
force_scale = 0.5


def ring_perm(size, stride, n, shift):
    pairs = []
    for s in range(size):
        base = (s // (stride * n)) * stride * n + s % stride
        pos = (s // stride) % n
        pairs.append((s, base + ((pos + shift) % n) * stride))
    return pairs


def ring_sum(value, axis, stride, n):
    size = lax.axis_size(axis)
    if n == 2:
        return value + lax.ppermute(value, axis, ring_perm(size, stride, n, 1))
    got = [lax.ppermute(value, axis, ring_perm(size, stride, n, j)) for j in (1, 2, 3)]
    return (value + got[1]) + (got[0] + got[2])


def ring_gather(value, axis, stride, n):
    size = lax.axis_size(axis)
    pos = (lax.axis_index(axis) // stride) % n
    got = [value] + [lax.ppermute(value, axis, ring_perm(size, stride, n, j)) for j in range(1, n)]
    parts = []
    for p in range(n):
        pick = got[0]
        for j in range(1, n):
            pick = jnp.where((pos - j) % n == p, got[j], pick)
        parts.append(jnp.where(pos == p, got[0], pick))
    return jnp.concatenate(parts, axis=0)


def mesh_rings():
    slab = lax.axis_size("slab")
    rings = [("slab", 1, 2), ("slab", 2, 4), ("slab", 8, slab // 8)]
    return rings


def all_sum(value):
    for axis, stride, n in mesh_rings() + [("cross", 1, lax.axis_size("cross"))]:
        value = ring_sum(value, axis, stride, n)
    return value


def slab_gather(value):
    parts = value
    for axis, stride, n in mesh_rings():
        parts = ring_gather(parts, axis, stride, n)
    return parts


def ring_rounds(slab, cross):
    return [(0, 1, 2), (0, 2, 4), (0, 8, slab // 8), (1, 1, cross)]


def partner(me, stride, n, shift):
    pos = (me // stride) % n
    return me - pos * stride + ((pos + shift) % n) * stride


def reduce_gather_kernel(rounds, per_ref, st_ref, pooled_ref, states_ref, held, sends, recvs, st_sends, st_recvs):
    here = (lax.axis_index("slab"), lax.axis_index("cross"))

    def device(axis, other):
        return (other, here[1]) if axis == 0 else (here[0], other)

    barrier = pltpu.get_barrier_semaphore()
    count = 0
    for axis, stride, n in rounds:
        for j in range(1, n):
            pl.semaphore_signal(barrier, inc=1, device_id=device(axis, partner(here[axis], stride, n, j)), device_id_type=MESH)
            count += 1
    pl.semaphore_wait(barrier, count)

    me = here[0]
    states_ref[pl.ds(me, 1)] = st_ref[...][None]
    pooled_ref[...] = per_ref[...]
    for r, (axis, stride, n) in enumerate(rounds):
        if n == 1:
            continue
        copies = []
        for j in range(1, n):
            dev = device(axis, partner(here[axis], stride, n, j))
            copy = pltpu.make_async_remote_copy(
                src_ref=pooled_ref,
                dst_ref=held.at[r, j - 1],
                send_sem=sends.at[r, j - 1],
                recv_sem=recvs.at[r, j - 1],
                device_id=dev,
                device_id_type=MESH,
            )
            copy.start()
            copies.append(copy)
            if axis == 0:
                rows = pl.ds(me - me % stride, stride)
                block = pltpu.make_async_remote_copy(
                    src_ref=states_ref.at[rows],
                    dst_ref=states_ref.at[rows],
                    send_sem=st_sends.at[r, j - 1],
                    recv_sem=st_recvs.at[r, j - 1],
                    device_id=dev,
                    device_id_type=MESH,
                )
                block.start()
                copies.append(block)
        for copy in copies:
            copy.wait()
        if n == 2:
            total = pooled_ref[...] + held[r, 0]
        else:
            total = (pooled_ref[...] + held[r, 1]) + (held[r, 0] + held[r, 2])
        pooled_ref[...] = total


def reduce_gather(per_rotor, rotor_states):
    slab, cross = lax.axis_size("slab"), lax.axis_size("cross")
    rounds = ring_rounds(slab, cross)
    vmem = pl.BlockSpec(memory_space=pltpu.VMEM)
    return pl.pallas_call(
        lambda *refs: reduce_gather_kernel(rounds, *refs),
        out_shape=(
            jax.ShapeDtypeStruct(per_rotor.shape, jnp.float32),
            jax.ShapeDtypeStruct((slab,) + rotor_states.shape, jnp.float32),
        ),
        in_specs=[vmem, vmem],
        out_specs=(vmem, vmem),
        scratch_shapes=[
            pltpu.VMEM((len(rounds), 3) + per_rotor.shape, jnp.float32),
            pltpu.SemaphoreType.DMA((len(rounds), 3)),
            pltpu.SemaphoreType.DMA((len(rounds), 3)),
            pltpu.SemaphoreType.DMA((len(rounds), 3)),
            pltpu.SemaphoreType.DMA((len(rounds), 3)),
        ],
        compiler_params=pltpu.CompilerParams(collective_id=0, has_side_effects=True),
    )(per_rotor, rotor_states)


def stencil_plane(x, planes, vel_ref, xlo_ref, xhi_ref, ylo_ref, yhi_ref):
    _, _, ny, nz = vel_ref.shape
    rows = lax.broadcasted_iota(jnp.int32, (ny, nz), 0)
    lanes = lax.broadcasted_iota(jnp.int32, (ny, nz), 1)
    here = [vel_ref[c, x] for c in range(3)]
    results = []
    for c in range(3):
        u = here[c]
        west = jnp.where(x == 0, xlo_ref[c].astype(jnp.float32), vel_ref[c, jnp.maximum(x - 1, 0)])
        east = jnp.where(x == planes - 1, xhi_ref[c].astype(jnp.float32), vel_ref[c, jnp.minimum(x + 1, planes - 1)])
        south = jnp.where(rows == 0, ylo_ref[c, x].astype(jnp.float32), pltpu.roll(u, 1, 0))
        north = jnp.where(rows == ny - 1, yhi_ref[c, x].astype(jnp.float32), pltpu.roll(u, ny - 1, 0))
        lower = jnp.where(lanes == 0, 0.0, pltpu.roll(u, 1, 1))
        upper = jnp.where(lanes == nz - 1, 0.0, pltpu.roll(u, nz - 1, 1))
        laplace = east + west + north + south + upper + lower - 6.0 * u
        advect = (
            here[0] * ((east - west) * 0.5)
            + here[1] * ((north - south) * 0.5)
            + here[2] * ((upper - lower) * 0.5)
        )
        results.append(u + time_step * (viscosity * laplace - advect))
    return results


def stencil_kernel(vel_ref, xlo_ref, xhi_ref, ylo_ref, yhi_ref, force_ref, out_ref):
    planes = vel_ref.shape[1]

    def body(x, carry):
        results = stencil_plane(x, planes, vel_ref, xlo_ref, xhi_ref, ylo_ref, yhi_ref)
        out_ref[0, x] = results[0] - force_scale * force_ref[x]
        out_ref[1, x] = results[1]
        out_ref[2, x] = results[2]
        return carry

    lax.fori_loop(0, planes, body, 0)


def stencil(velocity, halos, forcing):
    vmem = pl.BlockSpec(memory_space=pltpu.VMEM)
    return pl.pallas_call(
        stencil_kernel,
        out_shape=jax.ShapeDtypeStruct(velocity.shape, velocity.dtype),
        in_specs=[vmem] * 6,
        out_specs=vmem,
    )(velocity, *halos, forcing)


def halo_faces(velocity):
    faces = []
    for axis, dim in (("slab", 1), ("cross", 2)):
        count = lax.axis_size(axis)
        size = velocity.shape[dim]
        head = lax.slice_in_dim(velocity, 0, 1, axis=dim).astype(jnp.bfloat16)
        tail = lax.slice_in_dim(velocity, size - 1, size, axis=dim).astype(jnp.bfloat16)
        low = lax.ppermute(tail, axis, [(i, i + 1) for i in range(count - 1)])
        high = lax.ppermute(head, axis, [(i + 1, i) for i in range(count - 1)])
        faces += [jnp.squeeze(low, dim), jnp.squeeze(high, dim)] if dim == 1 else [low, high]
    return faces


def extended(cells, sides, width):
    for axis, dim in sides:
        count = lax.axis_size(axis)
        ends = count - 1
        head = lax.slice_in_dim(cells, 0, width, axis=dim)
        tail = lax.slice_in_dim(cells, cells.shape[dim] - width, cells.shape[dim], axis=dim)
        cells = jnp.concatenate(
            [
                lax.ppermute(tail, axis, [(i, (i + 1) % count) for i in range(ends)]),
                cells,
                lax.ppermute(head, axis, [((i + 1) % count, i) for i in range(ends)]),
            ],
            axis=dim,
        )
    return cells


def combine_terms(velocity, east, west, north, south, upper, lower):
    laplace = east + west + north + south + upper + lower - 6.0 * velocity
    advect = (
        velocity[0:1] * ((east - west) * 0.5)
        + velocity[1:2] * ((north - south) * 0.5)
        + velocity[2:3] * ((upper - lower) * 0.5)
    )
    return velocity + time_step * (viscosity * laplace - advect)


def on_device(
    velocity,
    shape_weight,
    w_in,
    w_out,
    decay,
    rotor_states,
    slot_of_rotor,
    entry_rotor,
    entry_tile,
    entry_sub,
):
    local_x, local_y, local_z = (velocity.shape[1], velocity.shape[2], velocity.shape[3])
    tile_count = local_x * local_y * local_z // TILE
    halos = halo_faces(velocity)
    rotor_hot = (entry_rotor == jnp.arange(R, dtype=jnp.int32)[None, :]).astype(jnp.int32)
    slots = jnp.sum(rotor_hot * slot_of_rotor[None, :], axis=1)
    sub_range = jnp.arange(NSUB, dtype=jnp.int32)
    sub_hot = (entry_sub[:, None] == sub_range[None, :]).astype(jnp.float32)
    gains = jnp.dot(sub_hot, shape_weight, precision=lax.Precision.HIGHEST)
    slot_hot = (slots[:, None] == jnp.arange(R, dtype=jnp.int32)[None, :]).astype(jnp.float32)
    per_rotor = []
    for c in range(3):
        cells = velocity[c].reshape(tile_count, TILE)
        picked = jnp.take(cells, entry_tile, axis=0).astype(jnp.bfloat16).astype(jnp.float32)
        weighted = gains[:, c * TILE:(c + 1) * TILE] * picked
        per_rotor.append(jnp.dot(slot_hot.T, weighted, precision=lax.Precision.HIGHEST))
    per_rotor = jnp.concatenate(per_rotor, axis=1)
    pooled, all_states = reduce_gather(per_rotor, rotor_states)
    all_states = all_states.reshape(-1, rotor_states.shape[1])
    pooled_b = (pooled * pool_scale).astype(jnp.bfloat16)
    drive = jnp.dot(pooled_b, w_in, preferred_element_type=jnp.float32)
    all_new = all_states + state_step * (drive - decay[None, :] * all_states)
    all_sources = jnp.dot(
        all_new.astype(jnp.bfloat16), w_out, preferred_element_type=jnp.float32
    ).astype(jnp.bfloat16)
    new_states = lax.dynamic_slice_in_dim(all_new, lax.axis_index("slab"), 1, axis=0)
    rows = all_sources.reshape(R * NSUB, TILE)[slots * NSUB + entry_sub]
    cells_xy = local_x * local_y
    tile_pos = entry_tile // 2
    forcing = jnp.concatenate(
        [
            jnp.dot(
                ((jnp.arange(cells_xy, dtype=jnp.int32)[:, None] == tile_pos[None, :])
                 & (entry_tile % 2 == half)[None, :]).astype(jnp.bfloat16),
                rows,
                preferred_element_type=jnp.float32,
            )
            for half in range(local_z // TILE)
        ],
        axis=1,
    ).reshape(local_x, local_y, local_z)
    advanced = stencil(velocity, halos, forcing)
    return (advanced, new_states)


def solution(mesh):
    in_specs = (
        P(None, "slab", "cross", None),
        P(),
        P(),
        P(),
        P(),
        P("slab", None),
        P(),
        P(("slab", "cross"), None),
        P(("slab", "cross")),
        P(("slab", "cross")),
    )
    out_specs = (P(None, "slab", "cross", None), P("slab", None))
    return jax.shard_map(
        on_device, mesh=mesh, in_specs=in_specs, out_specs=out_specs, check_vma=False
    )
```

```python
import jax
import jax.numpy as jnp
from jax import lax
from jax.experimental import pallas as pl
from jax.experimental.pallas import tpu as pltpu
from jax.sharding import PartitionSpec as P

MESH = pl.DeviceIdType.MESH

TILE = 128
R = 32
NSUB = 32


time_step = 0.1
viscosity = 0.3
pool_scale = 1.0 / 64.0
state_step = 0.5
force_scale = 0.5


def ring_perm(size, stride, n, shift):
    pairs = []
    for s in range(size):
        base = (s // (stride * n)) * stride * n + s % stride
        pos = (s // stride) % n
        pairs.append((s, base + ((pos + shift) % n) * stride))
    return pairs


def ring_sum(value, axis, stride, n):
    size = lax.axis_size(axis)
    if n == 2:
        return value + lax.ppermute(value, axis, ring_perm(size, stride, n, 1))
    got = [lax.ppermute(value, axis, ring_perm(size, stride, n, j)) for j in (1, 2, 3)]
    return (value + got[1]) + (got[0] + got[2])


def ring_gather(value, axis, stride, n):
    size = lax.axis_size(axis)
    pos = (lax.axis_index(axis) // stride) % n
    got = [value] + [lax.ppermute(value, axis, ring_perm(size, stride, n, j)) for j in range(1, n)]
    parts = []
    for p in range(n):
        pick = got[0]
        for j in range(1, n):
            pick = jnp.where((pos - j) % n == p, got[j], pick)
        parts.append(jnp.where(pos == p, got[0], pick))
    return jnp.concatenate(parts, axis=0)


def mesh_rings():
    slab = lax.axis_size("slab")
    rings = [("slab", 1, 2), ("slab", 2, 4), ("slab", 8, slab // 8)]
    return rings


def all_sum(value):
    for axis, stride, n in mesh_rings() + [("cross", 1, lax.axis_size("cross"))]:
        value = ring_sum(value, axis, stride, n)
    return value


def slab_gather(value):
    parts = value
    for axis, stride, n in mesh_rings():
        parts = ring_gather(parts, axis, stride, n)
    return parts


def ring_rounds(slab, cross):
    return [(0, 1, 2), (0, 2, 4), (0, 8, slab // 8), (1, 1, cross)]


def partner(me, stride, n, shift):
    pos = (me // stride) % n
    return me - pos * stride + ((pos + shift) % n) * stride


def reduce_gather_kernel(rounds, per_ref, st_ref, pooled_ref, states_ref, held, sends, recvs, st_sends, st_recvs):
    here = (lax.axis_index("slab"), lax.axis_index("cross"))

    def device(axis, other):
        return (other, here[1]) if axis == 0 else (here[0], other)

    barrier = pltpu.get_barrier_semaphore()
    count = 0
    for axis, stride, n in rounds:
        for j in range(1, n):
            pl.semaphore_signal(barrier, inc=1, device_id=device(axis, partner(here[axis], stride, n, j)), device_id_type=MESH)
            count += 1
    pl.semaphore_wait(barrier, count)

    me = here[0]
    states_ref[pl.ds(me, 1)] = st_ref[...][None]
    pooled_ref[...] = per_ref[...]
    for r, (axis, stride, n) in enumerate(rounds):
        if n == 1:
            continue
        copies = []
        for j in range(1, n):
            dev = device(axis, partner(here[axis], stride, n, j))
            copy = pltpu.make_async_remote_copy(
                src_ref=pooled_ref,
                dst_ref=held.at[r, j - 1],
                send_sem=sends.at[r, j - 1],
                recv_sem=recvs.at[r, j - 1],
                device_id=dev,
                device_id_type=MESH,
            )
            copy.start()
            copies.append(copy)
            if axis == 0:
                rows = pl.ds(me - me % stride, stride)
                block = pltpu.make_async_remote_copy(
                    src_ref=states_ref.at[rows],
                    dst_ref=states_ref.at[rows],
                    send_sem=st_sends.at[r, j - 1],
                    recv_sem=st_recvs.at[r, j - 1],
                    device_id=dev,
                    device_id_type=MESH,
                )
                block.start()
                copies.append(block)
        for copy in copies:
            copy.wait()
        if n == 2:
            total = pooled_ref[...] + held[r, 0]
        else:
            total = (pooled_ref[...] + held[r, 1]) + (held[r, 0] + held[r, 2])
        pooled_ref[...] = total


def reduce_gather(per_rotor, rotor_states):
    slab, cross = lax.axis_size("slab"), lax.axis_size("cross")
    rounds = ring_rounds(slab, cross)
    vmem = pl.BlockSpec(memory_space=pltpu.VMEM)
    return pl.pallas_call(
        lambda *refs: reduce_gather_kernel(rounds, *refs),
        out_shape=(
            jax.ShapeDtypeStruct(per_rotor.shape, jnp.float32),
            jax.ShapeDtypeStruct((slab,) + rotor_states.shape, jnp.float32),
        ),
        in_specs=[vmem, vmem],
        out_specs=(vmem, vmem),
        scratch_shapes=[
            pltpu.VMEM((len(rounds), 3) + per_rotor.shape, jnp.float32),
            pltpu.SemaphoreType.DMA((len(rounds), 3)),
            pltpu.SemaphoreType.DMA((len(rounds), 3)),
            pltpu.SemaphoreType.DMA((len(rounds), 3)),
            pltpu.SemaphoreType.DMA((len(rounds), 3)),
        ],
        compiler_params=pltpu.CompilerParams(collective_id=0, has_side_effects=True),
    )(per_rotor, rotor_states)


def stencil_plane(x, planes, vel_ref, xlo_ref, xhi_ref, ylo_ref, yhi_ref):
    _, _, ny, nz = vel_ref.shape
    rows = lax.broadcasted_iota(jnp.int32, (ny, nz), 0)
    lanes = lax.broadcasted_iota(jnp.int32, (ny, nz), 1)
    here = [vel_ref[c, x] for c in range(3)]
    results = []
    for c in range(3):
        u = here[c]
        west = jnp.where(x == 0, xlo_ref[c].astype(jnp.float32), vel_ref[c, jnp.maximum(x - 1, 0)])
        east = jnp.where(x == planes - 1, xhi_ref[c].astype(jnp.float32), vel_ref[c, jnp.minimum(x + 1, planes - 1)])
        south = jnp.where(rows == 0, ylo_ref[c, x].astype(jnp.float32), pltpu.roll(u, 1, 0))
        north = jnp.where(rows == ny - 1, yhi_ref[c, x].astype(jnp.float32), pltpu.roll(u, ny - 1, 0))
        lower = jnp.where(lanes == 0, 0.0, pltpu.roll(u, 1, 1))
        upper = jnp.where(lanes == nz - 1, 0.0, pltpu.roll(u, nz - 1, 1))
        laplace = east + west + north + south + upper + lower - 6.0 * u
        advect = (
            here[0] * ((east - west) * 0.5)
            + here[1] * ((north - south) * 0.5)
            + here[2] * ((upper - lower) * 0.5)
        )
        results.append(u + time_step * (viscosity * laplace - advect))
    return results


def stencil_kernel(vel_ref, xlo_ref, xhi_ref, ylo_ref, yhi_ref, force_ref, out_ref):
    planes = vel_ref.shape[1]

    def body(x, carry):
        results = stencil_plane(x, planes, vel_ref, xlo_ref, xhi_ref, ylo_ref, yhi_ref)
        out_ref[0, x] = results[0] - force_scale * force_ref[x]
        out_ref[1, x] = results[1]
        out_ref[2, x] = results[2]
        return carry

    lax.fori_loop(0, planes, body, 0)


def stencil(velocity, halos, forcing):
    vmem = pl.BlockSpec(memory_space=pltpu.VMEM)
    return pl.pallas_call(
        stencil_kernel,
        out_shape=jax.ShapeDtypeStruct(velocity.shape, velocity.dtype),
        in_specs=[vmem] * 6,
        out_specs=vmem,
    )(velocity, *halos, forcing)


def halo_faces(velocity):
    faces = []
    for axis, dim in (("slab", 1), ("cross", 2)):
        count = lax.axis_size(axis)
        size = velocity.shape[dim]
        head = lax.slice_in_dim(velocity, 0, 1, axis=dim).astype(jnp.bfloat16)
        tail = lax.slice_in_dim(velocity, size - 1, size, axis=dim).astype(jnp.bfloat16)
        low = lax.ppermute(tail, axis, [(i, i + 1) for i in range(count - 1)])
        high = lax.ppermute(head, axis, [(i + 1, i) for i in range(count - 1)])
        faces += [jnp.squeeze(low, dim), jnp.squeeze(high, dim)] if dim == 1 else [low, high]
    return faces


def extended(cells, sides, width):
    for axis, dim in sides:
        count = lax.axis_size(axis)
        ends = count - 1
        head = lax.slice_in_dim(cells, 0, width, axis=dim)
        tail = lax.slice_in_dim(cells, cells.shape[dim] - width, cells.shape[dim], axis=dim)
        cells = jnp.concatenate(
            [
                lax.ppermute(tail, axis, [(i, (i + 1) % count) for i in range(ends)]),
                cells,
                lax.ppermute(head, axis, [((i + 1) % count, i) for i in range(ends)]),
            ],
            axis=dim,
        )
    return cells


def combine_terms(velocity, east, west, north, south, upper, lower):
    laplace = east + west + north + south + upper + lower - 6.0 * velocity
    advect = (
        velocity[0:1] * ((east - west) * 0.5)
        + velocity[1:2] * ((north - south) * 0.5)
        + velocity[2:3] * ((upper - lower) * 0.5)
    )
    return velocity + time_step * (viscosity * laplace - advect)


def on_device(
    velocity,
    shape_weight,
    w_in,
    w_out,
    decay,
    rotor_states,
    slot_of_rotor,
    entry_rotor,
    entry_tile,
    entry_sub,
):
    local_x, local_y, local_z = (velocity.shape[1], velocity.shape[2], velocity.shape[3])
    tile_count = local_x * local_y * local_z // TILE
    halos = halo_faces(velocity)
    rotor_hot = (entry_rotor == jnp.arange(R, dtype=jnp.int32)[None, :]).astype(jnp.int32)
    slots = jnp.sum(rotor_hot * slot_of_rotor[None, :], axis=1)
    sub_range = jnp.arange(NSUB, dtype=jnp.int32)
    sub_hot = (entry_sub[:, None] == sub_range[None, :]).astype(jnp.float32)
    gains = jnp.dot(sub_hot, shape_weight, precision=lax.Precision.HIGHEST)
    slot_hot = (slots[:, None] == jnp.arange(R, dtype=jnp.int32)[None, :]).astype(jnp.float32)
    per_rotor = []
    pick_hot = (entry_tile[:, None] == jnp.arange(tile_count, dtype=jnp.int32)[None, :]).astype(jnp.bfloat16)
    for c in range(3):
        cells = velocity[c].reshape(tile_count, TILE).astype(jnp.bfloat16)
        picked = jnp.dot(pick_hot, cells, preferred_element_type=jnp.float32)
        weighted = gains[:, c * TILE:(c + 1) * TILE] * picked
        per_rotor.append(jnp.dot(slot_hot.T, weighted, precision=lax.Precision.HIGHEST))
    per_rotor = jnp.concatenate(per_rotor, axis=1)
    pooled, all_states = reduce_gather(per_rotor, rotor_states)
    all_states = all_states.reshape(-1, rotor_states.shape[1])
    pooled_b = (pooled * pool_scale).astype(jnp.bfloat16)
    drive = jnp.dot(pooled_b, w_in, preferred_element_type=jnp.float32)
    all_new = all_states + state_step * (drive - decay[None, :] * all_states)
    all_sources = jnp.dot(
        all_new.astype(jnp.bfloat16), w_out, preferred_element_type=jnp.float32
    ).astype(jnp.bfloat16)
    new_states = lax.dynamic_slice_in_dim(all_new, lax.axis_index("slab"), 1, axis=0)
    rows = all_sources.reshape(R * NSUB, TILE)[slots * NSUB + entry_sub]
    cells_xy = local_x * local_y
    halves = local_z // TILE
    half = (entry_tile % halves)[:, None]
    wide = jnp.concatenate([jnp.where(half == h, rows, jnp.zeros_like(rows)) for h in range(halves)], axis=1)
    place_hot = (jnp.arange(cells_xy, dtype=jnp.int32)[:, None] == (entry_tile // halves)[None, :]).astype(jnp.bfloat16)
    forcing = jnp.dot(place_hot, wide, preferred_element_type=jnp.float32).reshape(local_x, local_y, local_z)
    advanced = stencil(velocity, halos, forcing)
    return (advanced, new_states)


def solution(mesh):
    in_specs = (
        P(None, "slab", "cross", None),
        P(),
        P(),
        P(),
        P(),
        P("slab", None),
        P(),
        P(("slab", "cross"), None),
        P(("slab", "cross")),
        P(("slab", "cross")),
    )
    out_specs = (P(None, "slab", "cross", None), P("slab", None))
    return jax.shard_map(
        on_device, mesh=mesh, in_specs=in_specs, out_specs=out_specs, check_vma=False
    )
```

```python
import jax
import jax.numpy as jnp
from jax import lax
from jax.experimental import pallas as pl
from jax.experimental.pallas import tpu as pltpu
from jax.sharding import PartitionSpec as P

MESH = pl.DeviceIdType.MESH

TILE = 128
R = 32
NSUB = 32


time_step = 0.1
viscosity = 0.3
pool_scale = 1.0 / 64.0
state_step = 0.5
force_scale = 0.5


def ring_perm(size, stride, n, shift):
    pairs = []
    for s in range(size):
        base = (s // (stride * n)) * stride * n + s % stride
        pos = (s // stride) % n
        pairs.append((s, base + ((pos + shift) % n) * stride))
    return pairs


def ring_sum(value, axis, stride, n):
    size = lax.axis_size(axis)
    if n == 2:
        return value + lax.ppermute(value, axis, ring_perm(size, stride, n, 1))
    got = [lax.ppermute(value, axis, ring_perm(size, stride, n, j)) for j in (1, 2, 3)]
    return (value + got[1]) + (got[0] + got[2])


def ring_gather(value, axis, stride, n):
    size = lax.axis_size(axis)
    pos = (lax.axis_index(axis) // stride) % n
    got = [value] + [lax.ppermute(value, axis, ring_perm(size, stride, n, j)) for j in range(1, n)]
    parts = []
    for p in range(n):
        pick = got[0]
        for j in range(1, n):
            pick = jnp.where((pos - j) % n == p, got[j], pick)
        parts.append(jnp.where(pos == p, got[0], pick))
    return jnp.concatenate(parts, axis=0)


def mesh_rings():
    slab = lax.axis_size("slab")
    rings = [("slab", 1, 2), ("slab", 2, 4), ("slab", 8, slab // 8)]
    return rings


def all_sum(value):
    for axis, stride, n in mesh_rings() + [("cross", 1, lax.axis_size("cross"))]:
        value = ring_sum(value, axis, stride, n)
    return value


def slab_gather(value):
    parts = value
    for axis, stride, n in mesh_rings():
        parts = ring_gather(parts, axis, stride, n)
    return parts


def ring_rounds(slab, cross):
    return [(0, 1, 2), (0, 2, 4), (0, 8, slab // 8), (1, 1, cross)]


def partner(me, stride, n, shift):
    pos = (me // stride) % n
    return me - pos * stride + ((pos + shift) % n) * stride


def step_kernel(rounds, per_ref, st_ref, vel_ref, pooled_ref, states_ref, adv_ref, held, sends, recvs,
                st_sends, st_recvs, xlo, xhi, ylo, yhi, face_sends, face_recvs):
    here = (lax.axis_index("slab"), lax.axis_index("cross"))
    slab, cross = lax.axis_size("slab"), lax.axis_size("cross")
    planes = vel_ref.shape[1]
    ny = vel_ref.shape[2]
    s, c = here

    def device(axis, other):
        return (other, here[1]) if axis == 0 else (here[0], other)

    extra = s - 1 + 2 * (s % 2)
    barrier = pltpu.get_barrier_semaphore()
    count = 0
    for axis, stride, n in rounds:
        for j in range(1, n):
            pl.semaphore_signal(barrier, inc=1, device_id=device(axis, partner(here[axis], stride, n, j)), device_id_type=MESH)
            count += 1
    pl.semaphore_signal(barrier, inc=1, device_id=((extra + slab) % slab, c), device_id_type=MESH)
    pl.semaphore_wait(barrier, count + 1)

    faces = [
        (s > 0, s < slab - 1, vel_ref.at[:, 0], xhi, ((s + slab - 1) % slab, c)),
        (s < slab - 1, s > 0, vel_ref.at[:, planes - 1], xlo, ((s + 1) % slab, c)),
        (c > 0, c < cross - 1, vel_ref.at[:, :, pl.ds(0, 1)], yhi, (s, (c + cross - 1) % cross)),
        (c < cross - 1, c > 0, vel_ref.at[:, :, pl.ds(ny - 1, 1)], ylo, (s, (c + 1) % cross)),
    ]
    face_copies = []
    for k, (send_if, recv_if, src, dst, dev) in enumerate(faces):
        copy = pltpu.make_async_remote_copy(
            src_ref=src, dst_ref=dst, send_sem=face_sends.at[k], recv_sem=face_recvs.at[k],
            device_id=dev, device_id_type=MESH,
        )

        @pl.when(send_if)
        def _():
            copy.start()

        @pl.when(jnp.logical_not(recv_if))
        def _():
            dst[...] = jnp.zeros(dst.shape, dst.dtype)

        face_copies.append((send_if, recv_if, copy))

    states_ref[pl.ds(s, 1)] = st_ref[...][None]
    pooled_ref[...] = per_ref[...]
    chunks = [None, (0, 6), (6, 11), (11, planes)]
    for r, (axis, stride, n) in enumerate(rounds):
        copies = []
        for j in range(1, n):
            dev = device(axis, partner(here[axis], stride, n, j))
            copy = pltpu.make_async_remote_copy(
                src_ref=pooled_ref,
                dst_ref=held.at[r, j - 1],
                send_sem=sends.at[r, j - 1],
                recv_sem=recvs.at[r, j - 1],
                device_id=dev,
                device_id_type=MESH,
            )
            copy.start()
            copies.append(copy)
            if axis == 0:
                rows = pl.ds(s - s % stride, stride)
                block = pltpu.make_async_remote_copy(
                    src_ref=states_ref.at[rows],
                    dst_ref=states_ref.at[rows],
                    send_sem=st_sends.at[r, j - 1],
                    recv_sem=st_recvs.at[r, j - 1],
                    device_id=dev,
                    device_id_type=MESH,
                )
                block.start()
                copies.append(block)
        if chunks[r] is not None:
            first, last = chunks[r]

            def body(x, carry):
                results = stencil_plane(x, planes, vel_ref, xlo, xhi, ylo, yhi)
                for k in range(3):
                    adv_ref[k, x] = results[k]
                return carry

            lax.fori_loop(first, last, body, 0)
        for copy in copies:
            copy.wait()
        if n == 2:
            total = pooled_ref[...] + held[r, 0]
        else:
            total = (pooled_ref[...] + held[r, 1]) + (held[r, 0] + held[r, 2])
        pooled_ref[...] = total
        if r == 0:
            for send_if, recv_if, copy in face_copies:

                @pl.when(send_if)
                def _():
                    copy.wait_send()

                @pl.when(recv_if)
                def _():
                    copy.wait_recv()


def reduce_step(per_rotor, rotor_states, velocity):
    slab, cross = lax.axis_size("slab"), lax.axis_size("cross")
    rounds = ring_rounds(slab, cross)
    vmem = pl.BlockSpec(memory_space=pltpu.VMEM)
    _, planes, ny, nz = velocity.shape
    return pl.pallas_call(
        lambda *refs: step_kernel(rounds, *refs),
        out_shape=(
            jax.ShapeDtypeStruct(per_rotor.shape, jnp.float32),
            jax.ShapeDtypeStruct((slab,) + rotor_states.shape, jnp.float32),
            jax.ShapeDtypeStruct(velocity.shape, jnp.float32),
        ),
        in_specs=[vmem, vmem, vmem],
        out_specs=(vmem, vmem, vmem),
        scratch_shapes=[
            pltpu.VMEM((len(rounds), 3) + per_rotor.shape, jnp.float32),
            pltpu.SemaphoreType.DMA((len(rounds), 3)),
            pltpu.SemaphoreType.DMA((len(rounds), 3)),
            pltpu.SemaphoreType.DMA((len(rounds), 3)),
            pltpu.SemaphoreType.DMA((len(rounds), 3)),
            pltpu.VMEM((3, ny, nz), jnp.float32),
            pltpu.VMEM((3, ny, nz), jnp.float32),
            pltpu.VMEM((3, planes, 1, nz), jnp.float32),
            pltpu.VMEM((3, planes, 1, nz), jnp.float32),
            pltpu.SemaphoreType.DMA((4,)),
            pltpu.SemaphoreType.DMA((4,)),
        ],
        compiler_params=pltpu.CompilerParams(collective_id=0, has_side_effects=True),
    )(per_rotor, rotor_states, velocity)


def stencil_plane(x, planes, vel_ref, xlo_ref, xhi_ref, ylo_ref, yhi_ref):
    _, _, ny, nz = vel_ref.shape
    rows = lax.broadcasted_iota(jnp.int32, (ny, nz), 0)
    lanes = lax.broadcasted_iota(jnp.int32, (ny, nz), 1)
    here = [vel_ref[c, x] for c in range(3)]
    results = []
    for c in range(3):
        u = here[c]
        west = jnp.where(x == 0, xlo_ref[c].astype(jnp.float32), vel_ref[c, jnp.maximum(x - 1, 0)])
        east = jnp.where(x == planes - 1, xhi_ref[c].astype(jnp.float32), vel_ref[c, jnp.minimum(x + 1, planes - 1)])
        south = jnp.where(rows == 0, ylo_ref[c, x].astype(jnp.float32), pltpu.roll(u, 1, 0))
        north = jnp.where(rows == ny - 1, yhi_ref[c, x].astype(jnp.float32), pltpu.roll(u, ny - 1, 0))
        lower = jnp.where(lanes == 0, 0.0, pltpu.roll(u, 1, 1))
        upper = jnp.where(lanes == nz - 1, 0.0, pltpu.roll(u, nz - 1, 1))
        laplace = east + west + north + south + upper + lower - 6.0 * u
        advect = (
            here[0] * ((east - west) * 0.5)
            + here[1] * ((north - south) * 0.5)
            + here[2] * ((upper - lower) * 0.5)
        )
        results.append(u + time_step * (viscosity * laplace - advect))
    return results


def stencil_kernel(vel_ref, xlo_ref, xhi_ref, ylo_ref, yhi_ref, force_ref, out_ref):
    planes = vel_ref.shape[1]

    def body(x, carry):
        results = stencil_plane(x, planes, vel_ref, xlo_ref, xhi_ref, ylo_ref, yhi_ref)
        out_ref[0, x] = results[0] - force_scale * force_ref[x]
        out_ref[1, x] = results[1]
        out_ref[2, x] = results[2]
        return carry

    lax.fori_loop(0, planes, body, 0)


def stencil(velocity, halos, forcing):
    vmem = pl.BlockSpec(memory_space=pltpu.VMEM)
    return pl.pallas_call(
        stencil_kernel,
        out_shape=jax.ShapeDtypeStruct(velocity.shape, velocity.dtype),
        in_specs=[vmem] * 6,
        out_specs=vmem,
    )(velocity, *halos, forcing)


def halo_faces(velocity):
    faces = []
    for axis, dim in (("slab", 1), ("cross", 2)):
        count = lax.axis_size(axis)
        size = velocity.shape[dim]
        head = lax.slice_in_dim(velocity, 0, 1, axis=dim).astype(jnp.bfloat16)
        tail = lax.slice_in_dim(velocity, size - 1, size, axis=dim).astype(jnp.bfloat16)
        low = lax.ppermute(tail, axis, [(i, i + 1) for i in range(count - 1)])
        high = lax.ppermute(head, axis, [(i + 1, i) for i in range(count - 1)])
        faces += [jnp.squeeze(low, dim), jnp.squeeze(high, dim)] if dim == 1 else [low, high]
    return faces


def extended(cells, sides, width):
    for axis, dim in sides:
        count = lax.axis_size(axis)
        ends = count - 1
        head = lax.slice_in_dim(cells, 0, width, axis=dim)
        tail = lax.slice_in_dim(cells, cells.shape[dim] - width, cells.shape[dim], axis=dim)
        cells = jnp.concatenate(
            [
                lax.ppermute(tail, axis, [(i, (i + 1) % count) for i in range(ends)]),
                cells,
                lax.ppermute(head, axis, [((i + 1) % count, i) for i in range(ends)]),
            ],
            axis=dim,
        )
    return cells


def combine_terms(velocity, east, west, north, south, upper, lower):
    laplace = east + west + north + south + upper + lower - 6.0 * velocity
    advect = (
        velocity[0:1] * ((east - west) * 0.5)
        + velocity[1:2] * ((north - south) * 0.5)
        + velocity[2:3] * ((upper - lower) * 0.5)
    )
    return velocity + time_step * (viscosity * laplace - advect)


def on_device(
    velocity,
    shape_weight,
    w_in,
    w_out,
    decay,
    rotor_states,
    slot_of_rotor,
    entry_rotor,
    entry_tile,
    entry_sub,
):
    local_x, local_y, local_z = (velocity.shape[1], velocity.shape[2], velocity.shape[3])
    tile_count = local_x * local_y * local_z // TILE
    rotor_hot = (entry_rotor == jnp.arange(R, dtype=jnp.int32)[None, :]).astype(jnp.int32)
    slots = jnp.sum(rotor_hot * slot_of_rotor[None, :], axis=1)
    sub_range = jnp.arange(NSUB, dtype=jnp.int32)
    sub_hot = (entry_sub[:, None] == sub_range[None, :]).astype(jnp.float32)
    gains = jnp.dot(sub_hot, shape_weight, precision=lax.Precision.HIGHEST)
    slot_hot = (slots[:, None] == jnp.arange(R, dtype=jnp.int32)[None, :]).astype(jnp.float32)
    per_rotor = []
    pick_hot = (entry_tile[:, None] == jnp.arange(tile_count, dtype=jnp.int32)[None, :]).astype(jnp.bfloat16)
    for c in range(3):
        cells = velocity[c].reshape(tile_count, TILE).astype(jnp.bfloat16)
        picked = jnp.dot(pick_hot, cells, preferred_element_type=jnp.float32)
        weighted = gains[:, c * TILE:(c + 1) * TILE] * picked
        per_rotor.append(jnp.dot(slot_hot.T, weighted, precision=lax.Precision.HIGHEST))
    per_rotor = jnp.concatenate(per_rotor, axis=1)
    pooled, all_states, advanced = reduce_step(per_rotor, rotor_states, velocity)
    all_states = all_states.reshape(-1, rotor_states.shape[1])
    pooled_b = (pooled * pool_scale).astype(jnp.bfloat16)
    drive = jnp.dot(pooled_b, w_in, preferred_element_type=jnp.float32)
    all_new = all_states + state_step * (drive - decay[None, :] * all_states)
    all_sources = jnp.dot(
        all_new.astype(jnp.bfloat16), w_out, preferred_element_type=jnp.float32
    ).astype(jnp.bfloat16)
    new_states = lax.dynamic_slice_in_dim(all_new, lax.axis_index("slab"), 1, axis=0)
    rows = all_sources.reshape(R * NSUB, TILE)[slots * NSUB + entry_sub]
    cells_xy = local_x * local_y
    halves = local_z // TILE
    half = (entry_tile % halves)[:, None]
    wide = jnp.concatenate([jnp.where(half == h, rows, jnp.zeros_like(rows)) for h in range(halves)], axis=1)
    place_hot = (jnp.arange(cells_xy, dtype=jnp.int32)[:, None] == (entry_tile // halves)[None, :]).astype(jnp.bfloat16)
    forcing = jnp.dot(place_hot, wide, preferred_element_type=jnp.float32).reshape(local_x, local_y, local_z)
    advanced = advanced.at[0].add(-force_scale * forcing)
    return (advanced, new_states)


def solution(mesh):
    in_specs = (
        P(None, "slab", "cross", None),
        P(),
        P(),
        P(),
        P(),
        P("slab", None),
        P(),
        P(("slab", "cross"), None),
        P(("slab", "cross")),
        P(("slab", "cross")),
    )
    out_specs = (P(None, "slab", "cross", None), P("slab", None))
    return jax.shard_map(
        on_device, mesh=mesh, in_specs=in_specs, out_specs=out_specs, check_vma=False
    )
```

```python
import jax
import jax.numpy as jnp
from jax import lax
from jax.experimental import pallas as pl
from jax.experimental.pallas import tpu as pltpu
from jax.sharding import PartitionSpec as P

MESH = pl.DeviceIdType.MESH

TILE = 128
R = 32
NSUB = 32


time_step = 0.1
viscosity = 0.3
pool_scale = 1.0 / 64.0
state_step = 0.5
force_scale = 0.5


def ring_perm(size, stride, n, shift):
    pairs = []
    for s in range(size):
        base = (s // (stride * n)) * stride * n + s % stride
        pos = (s // stride) % n
        pairs.append((s, base + ((pos + shift) % n) * stride))
    return pairs


def ring_sum(value, axis, stride, n):
    size = lax.axis_size(axis)
    if n == 2:
        return value + lax.ppermute(value, axis, ring_perm(size, stride, n, 1))
    got = [lax.ppermute(value, axis, ring_perm(size, stride, n, j)) for j in (1, 2, 3)]
    return (value + got[1]) + (got[0] + got[2])


def ring_gather(value, axis, stride, n):
    size = lax.axis_size(axis)
    pos = (lax.axis_index(axis) // stride) % n
    got = [value] + [lax.ppermute(value, axis, ring_perm(size, stride, n, j)) for j in range(1, n)]
    parts = []
    for p in range(n):
        pick = got[0]
        for j in range(1, n):
            pick = jnp.where((pos - j) % n == p, got[j], pick)
        parts.append(jnp.where(pos == p, got[0], pick))
    return jnp.concatenate(parts, axis=0)


def mesh_rings():
    slab = lax.axis_size("slab")
    rings = [("slab", 1, 2), ("slab", 2, 4), ("slab", 8, slab // 8)]
    return rings


def all_sum(value):
    for axis, stride, n in mesh_rings() + [("cross", 1, lax.axis_size("cross"))]:
        value = ring_sum(value, axis, stride, n)
    return value


def slab_gather(value):
    parts = value
    for axis, stride, n in mesh_rings():
        parts = ring_gather(parts, axis, stride, n)
    return parts


def ring_rounds(slab, cross):
    return [(0, 1, 2), (0, 2, 4), (0, 8, slab // 8), (1, 1, cross)]


def partner(me, stride, n, shift):
    pos = (me // stride) % n
    return me - pos * stride + ((pos + shift) % n) * stride


def step_kernel(rounds, per_ref, st_ref, vel_ref, pooled_ref, states_ref, adv_ref, held, sends, recvs,
                st_sends, st_recvs, xlo, xhi, ylo, yhi, face_sends, face_recvs):
    here = (lax.axis_index("slab"), lax.axis_index("cross"))
    slab, cross = lax.axis_size("slab"), lax.axis_size("cross")
    planes = vel_ref.shape[1]
    ny = vel_ref.shape[2]
    s, c = here

    def device(axis, other):
        return (other, here[1]) if axis == 0 else (here[0], other)

    extra = s - 1 + 2 * (s % 2)
    barrier = pltpu.get_barrier_semaphore()
    count = 0
    for axis, stride, n in rounds:
        for j in range(1, n):
            pl.semaphore_signal(barrier, inc=1, device_id=device(axis, partner(here[axis], stride, n, j)), device_id_type=MESH)
            count += 1
    pl.semaphore_signal(barrier, inc=1, device_id=((extra + slab) % slab, c), device_id_type=MESH)
    pl.semaphore_wait(barrier, count + 1)

    faces = [
        (s > 0, s < slab - 1, vel_ref.at[:, 0], xhi, ((s + slab - 1) % slab, c)),
        (s < slab - 1, s > 0, vel_ref.at[:, planes - 1], xlo, ((s + 1) % slab, c)),
        (c > 0, c < cross - 1, vel_ref.at[:, :, pl.ds(0, 1)], yhi, (s, (c + cross - 1) % cross)),
        (c < cross - 1, c > 0, vel_ref.at[:, :, pl.ds(ny - 1, 1)], ylo, (s, (c + 1) % cross)),
    ]
    face_copies = []
    for k, (send_if, recv_if, src, dst, dev) in enumerate(faces):
        copy = pltpu.make_async_remote_copy(
            src_ref=src, dst_ref=dst, send_sem=face_sends.at[k], recv_sem=face_recvs.at[k],
            device_id=dev, device_id_type=MESH,
        )

        @pl.when(send_if)
        def _():
            copy.start()

        @pl.when(jnp.logical_not(recv_if))
        def _():
            dst[...] = jnp.zeros(dst.shape, dst.dtype)

        face_copies.append((send_if, recv_if, copy))

    states_ref[pl.ds(s, 1)] = st_ref[...][None]
    pooled_ref[...] = per_ref[...]
    chunks = [None, (0, 6), (6, 11), (11, planes)]
    for r, (axis, stride, n) in enumerate(rounds):
        copies = []
        for j in range(1, n):
            dev = device(axis, partner(here[axis], stride, n, j))
            copy = pltpu.make_async_remote_copy(
                src_ref=pooled_ref,
                dst_ref=held.at[r, j - 1],
                send_sem=sends.at[r, j - 1],
                recv_sem=recvs.at[r, j - 1],
                device_id=dev,
                device_id_type=MESH,
            )
            copy.start()
            copies.append(copy)
            if axis == 0:
                rows = pl.ds(s - s % stride, stride)
                block = pltpu.make_async_remote_copy(
                    src_ref=states_ref.at[rows],
                    dst_ref=states_ref.at[rows],
                    send_sem=st_sends.at[r, j - 1],
                    recv_sem=st_recvs.at[r, j - 1],
                    device_id=dev,
                    device_id_type=MESH,
                )
                block.start()
                copies.append(block)
        if chunks[r] is not None:
            first, last = chunks[r]

            def body(x, carry):
                results = stencil_plane(x, planes, vel_ref, xlo, xhi, ylo, yhi)
                for k in range(3):
                    adv_ref[k, x] = results[k]
                return carry

            lax.fori_loop(first, last, body, 0)
        for copy in copies:
            copy.wait()
        if n == 2:
            total = pooled_ref[...] + held[r, 0]
        else:
            total = (pooled_ref[...] + held[r, 1]) + (held[r, 0] + held[r, 2])
        pooled_ref[...] = total
        if r == 0:
            for send_if, recv_if, copy in face_copies:

                @pl.when(send_if)
                def _():
                    copy.wait_send()

                @pl.when(recv_if)
                def _():
                    copy.wait_recv()


def reduce_step(per_rotor, rotor_states, velocity):
    slab, cross = lax.axis_size("slab"), lax.axis_size("cross")
    rounds = ring_rounds(slab, cross)
    vmem = pl.BlockSpec(memory_space=pltpu.VMEM)
    _, planes, ny, nz = velocity.shape
    return pl.pallas_call(
        lambda *refs: step_kernel(rounds, *refs),
        out_shape=(
            jax.ShapeDtypeStruct(per_rotor.shape, jnp.float32),
            jax.ShapeDtypeStruct((slab,) + rotor_states.shape, jnp.float32),
            jax.ShapeDtypeStruct(velocity.shape, jnp.float32),
        ),
        in_specs=[vmem, vmem, vmem],
        out_specs=(vmem, vmem, vmem),
        scratch_shapes=[
            pltpu.VMEM((len(rounds), 3) + per_rotor.shape, jnp.float32),
            pltpu.SemaphoreType.DMA((len(rounds), 3)),
            pltpu.SemaphoreType.DMA((len(rounds), 3)),
            pltpu.SemaphoreType.DMA((len(rounds), 3)),
            pltpu.SemaphoreType.DMA((len(rounds), 3)),
            pltpu.VMEM((3, ny, nz), jnp.float32),
            pltpu.VMEM((3, ny, nz), jnp.float32),
            pltpu.VMEM((3, planes, 1, nz), jnp.float32),
            pltpu.VMEM((3, planes, 1, nz), jnp.float32),
            pltpu.SemaphoreType.DMA((4,)),
            pltpu.SemaphoreType.DMA((4,)),
        ],
        compiler_params=pltpu.CompilerParams(collective_id=0, has_side_effects=True),
    )(per_rotor, rotor_states, velocity)


def stencil_plane(x, planes, vel_ref, xlo_ref, xhi_ref, ylo_ref, yhi_ref):
    _, _, ny, nz = vel_ref.shape
    rows = lax.broadcasted_iota(jnp.int32, (ny, nz), 0)
    lanes = lax.broadcasted_iota(jnp.int32, (ny, nz), 1)
    here = [vel_ref[c, x] for c in range(3)]
    results = []
    for c in range(3):
        u = here[c]
        west = jnp.where(x == 0, xlo_ref[c].astype(jnp.float32), vel_ref[c, jnp.maximum(x - 1, 0)])
        east = jnp.where(x == planes - 1, xhi_ref[c].astype(jnp.float32), vel_ref[c, jnp.minimum(x + 1, planes - 1)])
        south = jnp.where(rows == 0, ylo_ref[c, x].astype(jnp.float32), pltpu.roll(u, 1, 0))
        north = jnp.where(rows == ny - 1, yhi_ref[c, x].astype(jnp.float32), pltpu.roll(u, ny - 1, 0))
        lower = jnp.where(lanes == 0, 0.0, pltpu.roll(u, 1, 1))
        upper = jnp.where(lanes == nz - 1, 0.0, pltpu.roll(u, nz - 1, 1))
        laplace = east + west + north + south + upper + lower - 6.0 * u
        advect = (
            here[0] * ((east - west) * 0.5)
            + here[1] * ((north - south) * 0.5)
            + here[2] * ((upper - lower) * 0.5)
        )
        results.append(u + time_step * (viscosity * laplace - advect))
    return results


def stencil_kernel(vel_ref, xlo_ref, xhi_ref, ylo_ref, yhi_ref, force_ref, out_ref):
    planes = vel_ref.shape[1]

    def body(x, carry):
        results = stencil_plane(x, planes, vel_ref, xlo_ref, xhi_ref, ylo_ref, yhi_ref)
        out_ref[0, x] = results[0] - force_scale * force_ref[x]
        out_ref[1, x] = results[1]
        out_ref[2, x] = results[2]
        return carry

    lax.fori_loop(0, planes, body, 0)


def stencil(velocity, halos, forcing):
    vmem = pl.BlockSpec(memory_space=pltpu.VMEM)
    return pl.pallas_call(
        stencil_kernel,
        out_shape=jax.ShapeDtypeStruct(velocity.shape, velocity.dtype),
        in_specs=[vmem] * 6,
        out_specs=vmem,
    )(velocity, *halos, forcing)


def halo_faces(velocity):
    faces = []
    for axis, dim in (("slab", 1), ("cross", 2)):
        count = lax.axis_size(axis)
        size = velocity.shape[dim]
        head = lax.slice_in_dim(velocity, 0, 1, axis=dim).astype(jnp.bfloat16)
        tail = lax.slice_in_dim(velocity, size - 1, size, axis=dim).astype(jnp.bfloat16)
        low = lax.ppermute(tail, axis, [(i, i + 1) for i in range(count - 1)])
        high = lax.ppermute(head, axis, [(i + 1, i) for i in range(count - 1)])
        faces += [jnp.squeeze(low, dim), jnp.squeeze(high, dim)] if dim == 1 else [low, high]
    return faces


def extended(cells, sides, width):
    for axis, dim in sides:
        count = lax.axis_size(axis)
        ends = count - 1
        head = lax.slice_in_dim(cells, 0, width, axis=dim)
        tail = lax.slice_in_dim(cells, cells.shape[dim] - width, cells.shape[dim], axis=dim)
        cells = jnp.concatenate(
            [
                lax.ppermute(tail, axis, [(i, (i + 1) % count) for i in range(ends)]),
                cells,
                lax.ppermute(head, axis, [((i + 1) % count, i) for i in range(ends)]),
            ],
            axis=dim,
        )
    return cells


def combine_terms(velocity, east, west, north, south, upper, lower):
    laplace = east + west + north + south + upper + lower - 6.0 * velocity
    advect = (
        velocity[0:1] * ((east - west) * 0.5)
        + velocity[1:2] * ((north - south) * 0.5)
        + velocity[2:3] * ((upper - lower) * 0.5)
    )
    return velocity + time_step * (viscosity * laplace - advect)


def on_device(
    velocity,
    shape_weight,
    w_in,
    w_out,
    decay,
    rotor_states,
    slot_of_rotor,
    entry_rotor,
    entry_tile,
    entry_sub,
):
    local_x, local_y, local_z = (velocity.shape[1], velocity.shape[2], velocity.shape[3])
    tile_count = local_x * local_y * local_z // TILE
    rotor_hot = (entry_rotor == jnp.arange(R, dtype=jnp.int32)[None, :]).astype(jnp.int32)
    slots = jnp.sum(rotor_hot * slot_of_rotor[None, :], axis=1)
    sub_range = jnp.arange(NSUB, dtype=jnp.int32)
    sub_hot = (entry_sub[:, None] == sub_range[None, :]).astype(jnp.bfloat16)
    high = shape_weight.astype(jnp.bfloat16)
    rest = shape_weight - high.astype(jnp.float32)
    middle = rest.astype(jnp.bfloat16)
    low = (rest - middle.astype(jnp.float32)).astype(jnp.bfloat16)
    gains = [jnp.dot(sub_hot, part, preferred_element_type=jnp.float32) for part in (high, middle, low)]
    gains = (gains[0] + gains[1]) + gains[2]
    slot_hot = (slots[:, None] == jnp.arange(R, dtype=jnp.int32)[None, :]).astype(jnp.float32)
    cells_xy = local_x * local_y
    halves = local_z // TILE
    half = (entry_tile % halves)[:, None]
    place_hot = (jnp.arange(cells_xy, dtype=jnp.int32)[:, None] == (entry_tile // halves)[None, :]).astype(jnp.bfloat16)
    per_rotor = []
    for c in range(3):
        cells = velocity[c].reshape(cells_xy, local_z).astype(jnp.bfloat16)
        both = jnp.dot(place_hot.T, cells, preferred_element_type=jnp.float32)
        picked = both[:, :TILE]
        for h in range(1, halves):
            picked = jnp.where(half == h, both[:, h * TILE:(h + 1) * TILE], picked)
        weighted = gains[:, c * TILE:(c + 1) * TILE] * picked
        per_rotor.append(jnp.dot(slot_hot.T, weighted, precision=lax.Precision.HIGHEST))
    per_rotor = jnp.concatenate(per_rotor, axis=1)
    pooled, all_states, advanced = reduce_step(per_rotor, rotor_states, velocity)
    all_states = all_states.reshape(-1, rotor_states.shape[1])
    pooled_b = (pooled * pool_scale).astype(jnp.bfloat16)
    drive = jnp.dot(pooled_b, w_in, preferred_element_type=jnp.float32)
    all_new = all_states + state_step * (drive - decay[None, :] * all_states)
    all_sources = jnp.dot(
        all_new.astype(jnp.bfloat16), w_out, preferred_element_type=jnp.float32
    ).astype(jnp.bfloat16)
    new_states = lax.dynamic_slice_in_dim(all_new, lax.axis_index("slab"), 1, axis=0)
    flat = all_sources.reshape(R * NSUB, TILE)
    row_hot = ((slots * NSUB + entry_sub)[:, None] == jnp.arange(R * NSUB, dtype=jnp.int32)[None, :]).astype(jnp.bfloat16)
    rows = jnp.dot(row_hot, flat, preferred_element_type=jnp.float32).astype(jnp.bfloat16)
    wide = jnp.concatenate([jnp.where(half == h, rows, jnp.zeros_like(rows)) for h in range(halves)], axis=1)
    forcing = jnp.dot(place_hot, wide, preferred_element_type=jnp.float32).reshape(local_x, local_y, local_z)
    advanced = advanced.at[0].add(-force_scale * forcing)
    return (advanced, new_states)


def solution(mesh):
    in_specs = (
        P(None, "slab", "cross", None),
        P(),
        P(),
        P(),
        P(),
        P("slab", None),
        P(),
        P(("slab", "cross"), None),
        P(("slab", "cross")),
        P(("slab", "cross")),
    )
    out_specs = (P(None, "slab", "cross", None), P("slab", None))
    return jax.shard_map(
        on_device, mesh=mesh, in_specs=in_specs, out_specs=out_specs, check_vma=False
    )
```

```python
import jax
import jax.numpy as jnp
from jax import lax
from jax.experimental import pallas as pl
from jax.experimental.pallas import tpu as pltpu
from jax.sharding import PartitionSpec as P

MESH = pl.DeviceIdType.MESH

TILE = 128
R = 32
NSUB = 32


time_step = 0.1
viscosity = 0.3
pool_scale = 1.0 / 64.0
state_step = 0.5
force_scale = 0.5


def ring_perm(size, stride, n, shift):
    pairs = []
    for s in range(size):
        base = (s // (stride * n)) * stride * n + s % stride
        pos = (s // stride) % n
        pairs.append((s, base + ((pos + shift) % n) * stride))
    return pairs


def ring_sum(value, axis, stride, n):
    size = lax.axis_size(axis)
    if n == 2:
        return value + lax.ppermute(value, axis, ring_perm(size, stride, n, 1))
    got = [lax.ppermute(value, axis, ring_perm(size, stride, n, j)) for j in (1, 2, 3)]
    return (value + got[1]) + (got[0] + got[2])


def ring_gather(value, axis, stride, n):
    size = lax.axis_size(axis)
    pos = (lax.axis_index(axis) // stride) % n
    got = [value] + [lax.ppermute(value, axis, ring_perm(size, stride, n, j)) for j in range(1, n)]
    parts = []
    for p in range(n):
        pick = got[0]
        for j in range(1, n):
            pick = jnp.where((pos - j) % n == p, got[j], pick)
        parts.append(jnp.where(pos == p, got[0], pick))
    return jnp.concatenate(parts, axis=0)


def mesh_rings():
    slab = lax.axis_size("slab")
    rings = [("slab", 1, 2), ("slab", 2, 4), ("slab", 8, slab // 8)]
    return rings


def all_sum(value):
    for axis, stride, n in mesh_rings() + [("cross", 1, lax.axis_size("cross"))]:
        value = ring_sum(value, axis, stride, n)
    return value


def slab_gather(value):
    parts = value
    for axis, stride, n in mesh_rings():
        parts = ring_gather(parts, axis, stride, n)
    return parts


def ring_rounds(slab, cross):
    return [(0, 1, 2), (0, 2, 4), (0, 8, slab // 8), (1, 1, cross)]


def partner(me, stride, n, shift):
    pos = (me // stride) % n
    return me - pos * stride + ((pos + shift) % n) * stride


def step_kernel(rounds, per_ref, st_ref, vel_ref, pooled_ref, states_ref, adv_ref, held, sends, recvs,
                st_sends, st_recvs, xlo, xhi, ylo, yhi, face_sends, face_recvs):
    here = (lax.axis_index("slab"), lax.axis_index("cross"))
    slab, cross = lax.axis_size("slab"), lax.axis_size("cross")
    planes = vel_ref.shape[1]
    ny = vel_ref.shape[2]
    s, c = here

    def device(axis, other):
        return (other, here[1]) if axis == 0 else (here[0], other)

    extra = s - 1 + 2 * (s % 2)
    barrier = pltpu.get_barrier_semaphore()
    count = 0
    for axis, stride, n in rounds:
        for j in range(1, n):
            pl.semaphore_signal(barrier, inc=1, device_id=device(axis, partner(here[axis], stride, n, j)), device_id_type=MESH)
            count += 1
    pl.semaphore_signal(barrier, inc=1, device_id=((extra + slab) % slab, c), device_id_type=MESH)
    pl.semaphore_wait(barrier, count + 1)

    faces = [
        (s > 0, s < slab - 1, vel_ref.at[:, 0], xhi, ((s + slab - 1) % slab, c)),
        (s < slab - 1, s > 0, vel_ref.at[:, planes - 1], xlo, ((s + 1) % slab, c)),
        (c > 0, c < cross - 1, vel_ref.at[:, :, pl.ds(0, 1)], yhi, (s, (c + cross - 1) % cross)),
        (c < cross - 1, c > 0, vel_ref.at[:, :, pl.ds(ny - 1, 1)], ylo, (s, (c + 1) % cross)),
    ]
    face_copies = []
    for k, (send_if, recv_if, src, dst, dev) in enumerate(faces):
        copy = pltpu.make_async_remote_copy(
            src_ref=src, dst_ref=dst, send_sem=face_sends.at[k], recv_sem=face_recvs.at[k],
            device_id=dev, device_id_type=MESH,
        )

        @pl.when(send_if)
        def _():
            copy.start()

        @pl.when(jnp.logical_not(recv_if))
        def _():
            dst[...] = jnp.zeros(dst.shape, dst.dtype)

        face_copies.append((send_if, recv_if, copy))

    states_ref[pl.ds(s, 1)] = st_ref[...][None]
    pooled_ref[...] = per_ref[...]
    chunks = [None, (0, 6), (6, 11), (11, planes)]
    for r, (axis, stride, n) in enumerate(rounds):
        copies = []
        for j in range(1, n):
            dev = device(axis, partner(here[axis], stride, n, j))
            copy = pltpu.make_async_remote_copy(
                src_ref=pooled_ref,
                dst_ref=held.at[r, j - 1],
                send_sem=sends.at[r, j - 1],
                recv_sem=recvs.at[r, j - 1],
                device_id=dev,
                device_id_type=MESH,
            )
            copy.start()
            copies.append(copy)
            if axis == 0:
                rows = pl.ds(s - s % stride, stride)
                block = pltpu.make_async_remote_copy(
                    src_ref=states_ref.at[rows],
                    dst_ref=states_ref.at[rows],
                    send_sem=st_sends.at[r, j - 1],
                    recv_sem=st_recvs.at[r, j - 1],
                    device_id=dev,
                    device_id_type=MESH,
                )
                block.start()
                copies.append(block)
        if chunks[r] is not None:
            first, last = chunks[r]

            def body(x, carry):
                results = stencil_plane(x, planes, vel_ref, xlo, xhi, ylo, yhi)
                for k in range(3):
                    adv_ref[k, x] = results[k]
                return carry

            lax.fori_loop(first, last, body, 0)
        for copy in copies:
            copy.wait()
        if n == 2:
            total = pooled_ref[...] + held[r, 0]
        else:
            total = (pooled_ref[...] + held[r, 1]) + (held[r, 0] + held[r, 2])
        pooled_ref[...] = total
        if r == 0:
            for send_if, recv_if, copy in face_copies:

                @pl.when(send_if)
                def _():
                    copy.wait_send()

                @pl.when(recv_if)
                def _():
                    copy.wait_recv()


def reduce_step(per_rotor, rotor_states, velocity):
    slab, cross = lax.axis_size("slab"), lax.axis_size("cross")
    rounds = ring_rounds(slab, cross)
    vmem = pl.BlockSpec(memory_space=pltpu.VMEM)
    _, planes, ny, nz = velocity.shape
    return pl.pallas_call(
        lambda *refs: step_kernel(rounds, *refs),
        out_shape=(
            jax.ShapeDtypeStruct(per_rotor.shape, jnp.float32),
            jax.ShapeDtypeStruct((slab,) + rotor_states.shape, jnp.float32),
            jax.ShapeDtypeStruct(velocity.shape, jnp.float32),
        ),
        in_specs=[vmem, vmem, vmem],
        out_specs=(vmem, vmem, vmem),
        scratch_shapes=[
            pltpu.VMEM((len(rounds), 3) + per_rotor.shape, jnp.float32),
            pltpu.SemaphoreType.DMA((len(rounds), 3)),
            pltpu.SemaphoreType.DMA((len(rounds), 3)),
            pltpu.SemaphoreType.DMA((len(rounds), 3)),
            pltpu.SemaphoreType.DMA((len(rounds), 3)),
            pltpu.VMEM((3, ny, nz), jnp.float32),
            pltpu.VMEM((3, ny, nz), jnp.float32),
            pltpu.VMEM((3, planes, 1, nz), jnp.float32),
            pltpu.VMEM((3, planes, 1, nz), jnp.float32),
            pltpu.SemaphoreType.DMA((4,)),
            pltpu.SemaphoreType.DMA((4,)),
        ],
        compiler_params=pltpu.CompilerParams(collective_id=0, has_side_effects=True),
    )(per_rotor, rotor_states, velocity)


def stencil_plane(x, planes, vel_ref, xlo_ref, xhi_ref, ylo_ref, yhi_ref):
    _, _, ny, nz = vel_ref.shape
    rows = lax.broadcasted_iota(jnp.int32, (ny, nz), 0)
    lanes = lax.broadcasted_iota(jnp.int32, (ny, nz), 1)
    here = [vel_ref[c, x] for c in range(3)]
    results = []
    for c in range(3):
        u = here[c]
        west = jnp.where(x == 0, xlo_ref[c].astype(jnp.float32), vel_ref[c, jnp.maximum(x - 1, 0)])
        east = jnp.where(x == planes - 1, xhi_ref[c].astype(jnp.float32), vel_ref[c, jnp.minimum(x + 1, planes - 1)])
        south = jnp.where(rows == 0, ylo_ref[c, x].astype(jnp.float32), pltpu.roll(u, 1, 0))
        north = jnp.where(rows == ny - 1, yhi_ref[c, x].astype(jnp.float32), pltpu.roll(u, ny - 1, 0))
        lower = jnp.where(lanes == 0, 0.0, pltpu.roll(u, 1, 1))
        upper = jnp.where(lanes == nz - 1, 0.0, pltpu.roll(u, nz - 1, 1))
        laplace = east + west + north + south + upper + lower - 6.0 * u
        advect = (
            here[0] * ((east - west) * 0.5)
            + here[1] * ((north - south) * 0.5)
            + here[2] * ((upper - lower) * 0.5)
        )
        results.append(u + time_step * (viscosity * laplace - advect))
    return results


def stencil_kernel(vel_ref, xlo_ref, xhi_ref, ylo_ref, yhi_ref, force_ref, out_ref):
    planes = vel_ref.shape[1]

    def body(x, carry):
        results = stencil_plane(x, planes, vel_ref, xlo_ref, xhi_ref, ylo_ref, yhi_ref)
        out_ref[0, x] = results[0] - force_scale * force_ref[x]
        out_ref[1, x] = results[1]
        out_ref[2, x] = results[2]
        return carry

    lax.fori_loop(0, planes, body, 0)


def stencil(velocity, halos, forcing):
    vmem = pl.BlockSpec(memory_space=pltpu.VMEM)
    return pl.pallas_call(
        stencil_kernel,
        out_shape=jax.ShapeDtypeStruct(velocity.shape, velocity.dtype),
        in_specs=[vmem] * 6,
        out_specs=vmem,
    )(velocity, *halos, forcing)


def halo_faces(velocity):
    faces = []
    for axis, dim in (("slab", 1), ("cross", 2)):
        count = lax.axis_size(axis)
        size = velocity.shape[dim]
        head = lax.slice_in_dim(velocity, 0, 1, axis=dim).astype(jnp.bfloat16)
        tail = lax.slice_in_dim(velocity, size - 1, size, axis=dim).astype(jnp.bfloat16)
        low = lax.ppermute(tail, axis, [(i, i + 1) for i in range(count - 1)])
        high = lax.ppermute(head, axis, [(i + 1, i) for i in range(count - 1)])
        faces += [jnp.squeeze(low, dim), jnp.squeeze(high, dim)] if dim == 1 else [low, high]
    return faces


def extended(cells, sides, width):
    for axis, dim in sides:
        count = lax.axis_size(axis)
        ends = count - 1
        head = lax.slice_in_dim(cells, 0, width, axis=dim)
        tail = lax.slice_in_dim(cells, cells.shape[dim] - width, cells.shape[dim], axis=dim)
        cells = jnp.concatenate(
            [
                lax.ppermute(tail, axis, [(i, (i + 1) % count) for i in range(ends)]),
                cells,
                lax.ppermute(head, axis, [((i + 1) % count, i) for i in range(ends)]),
            ],
            axis=dim,
        )
    return cells


def combine_terms(velocity, east, west, north, south, upper, lower):
    laplace = east + west + north + south + upper + lower - 6.0 * velocity
    advect = (
        velocity[0:1] * ((east - west) * 0.5)
        + velocity[1:2] * ((north - south) * 0.5)
        + velocity[2:3] * ((upper - lower) * 0.5)
    )
    return velocity + time_step * (viscosity * laplace - advect)


def on_device(
    velocity,
    shape_weight,
    w_in,
    w_out,
    decay,
    rotor_states,
    slot_of_rotor,
    entry_rotor,
    entry_tile,
    entry_sub,
):
    local_x, local_y, local_z = (velocity.shape[1], velocity.shape[2], velocity.shape[3])
    tile_count = local_x * local_y * local_z // TILE
    rotor_hot = (entry_rotor == jnp.arange(R, dtype=jnp.int32)[None, :]).astype(jnp.int32)
    slots = jnp.sum(rotor_hot * slot_of_rotor[None, :], axis=1)
    sub_range = jnp.arange(NSUB, dtype=jnp.int32)
    sub_hot = (entry_sub[:, None] == sub_range[None, :]).astype(jnp.bfloat16)
    high = lax.reduce_precision(shape_weight, exponent_bits=8, mantissa_bits=7)
    rest = shape_weight - high
    middle = lax.reduce_precision(rest, exponent_bits=8, mantissa_bits=7)
    low = rest - middle
    gains = [
        jnp.dot(sub_hot, part.astype(jnp.bfloat16), preferred_element_type=jnp.float32)
        for part in (high, middle, low)
    ]
    gains = (gains[0] + gains[1]) + gains[2]
    slot_hot = (slots[:, None] == jnp.arange(R, dtype=jnp.int32)[None, :]).astype(jnp.float32)
    cells_xy = local_x * local_y
    halves = local_z // TILE
    half = (entry_tile % halves)[:, None]
    place_hot = (jnp.arange(cells_xy, dtype=jnp.int32)[:, None] == (entry_tile // halves)[None, :]).astype(jnp.bfloat16)
    per_rotor = []
    for c in range(3):
        cells = velocity[c].reshape(cells_xy, local_z).astype(jnp.bfloat16)
        both = jnp.dot(place_hot.T, cells, preferred_element_type=jnp.float32)
        picked = both[:, :TILE]
        for h in range(1, halves):
            picked = jnp.where(half == h, both[:, h * TILE:(h + 1) * TILE], picked)
        weighted = gains[:, c * TILE:(c + 1) * TILE] * picked
        per_rotor.append(jnp.dot(slot_hot.T, weighted, precision=lax.Precision.HIGHEST))
    per_rotor = jnp.concatenate(per_rotor, axis=1)
    pooled, all_states, advanced = reduce_step(per_rotor, rotor_states, velocity)
    all_states = all_states.reshape(-1, rotor_states.shape[1])
    pooled_b = (pooled * pool_scale).astype(jnp.bfloat16)
    drive = jnp.dot(pooled_b, w_in, preferred_element_type=jnp.float32)
    all_new = all_states + state_step * (drive - decay[None, :] * all_states)
    all_sources = jnp.dot(
        all_new.astype(jnp.bfloat16), w_out, preferred_element_type=jnp.float32
    ).astype(jnp.bfloat16)
    new_states = lax.dynamic_slice_in_dim(all_new, lax.axis_index("slab"), 1, axis=0)
    flat = all_sources.reshape(R * NSUB, TILE)
    row_hot = ((slots * NSUB + entry_sub)[:, None] == jnp.arange(R * NSUB, dtype=jnp.int32)[None, :]).astype(jnp.bfloat16)
    rows = jnp.dot(row_hot, flat, preferred_element_type=jnp.float32).astype(jnp.bfloat16)
    wide = jnp.concatenate([jnp.where(half == h, rows, jnp.zeros_like(rows)) for h in range(halves)], axis=1)
    forcing = jnp.dot(place_hot, wide, preferred_element_type=jnp.float32).reshape(local_x, local_y, local_z)
    advanced = advanced.at[0].add(-force_scale * forcing)
    return (advanced, new_states)


def solution(mesh):
    in_specs = (
        P(None, "slab", "cross", None),
        P(),
        P(),
        P(),
        P(),
        P("slab", None),
        P(),
        P(("slab", "cross"), None),
        P(("slab", "cross")),
        P(("slab", "cross")),
    )
    out_specs = (P(None, "slab", "cross", None), P("slab", None))
    return jax.shard_map(
        on_device, mesh=mesh, in_specs=in_specs, out_specs=out_specs, check_vma=False
    )
```

```python
import jax
import jax.numpy as jnp
from jax import lax
from jax.experimental import pallas as pl
from jax.experimental.pallas import tpu as pltpu
from jax.sharding import PartitionSpec as P

MESH = pl.DeviceIdType.MESH

TILE = 128
R = 32
NSUB = 32


time_step = 0.1
viscosity = 0.3
pool_scale = 1.0 / 64.0
state_step = 0.5
force_scale = 0.5


def ring_perm(size, stride, n, shift):
    pairs = []
    for s in range(size):
        base = (s // (stride * n)) * stride * n + s % stride
        pos = (s // stride) % n
        pairs.append((s, base + ((pos + shift) % n) * stride))
    return pairs


def ring_sum(value, axis, stride, n):
    size = lax.axis_size(axis)
    if n == 2:
        return value + lax.ppermute(value, axis, ring_perm(size, stride, n, 1))
    got = [lax.ppermute(value, axis, ring_perm(size, stride, n, j)) for j in (1, 2, 3)]
    return (value + got[1]) + (got[0] + got[2])


def ring_gather(value, axis, stride, n):
    size = lax.axis_size(axis)
    pos = (lax.axis_index(axis) // stride) % n
    got = [value] + [lax.ppermute(value, axis, ring_perm(size, stride, n, j)) for j in range(1, n)]
    parts = []
    for p in range(n):
        pick = got[0]
        for j in range(1, n):
            pick = jnp.where((pos - j) % n == p, got[j], pick)
        parts.append(jnp.where(pos == p, got[0], pick))
    return jnp.concatenate(parts, axis=0)


def mesh_rings():
    slab = lax.axis_size("slab")
    rings = [("slab", 1, 2), ("slab", 2, 4), ("slab", 8, slab // 8)]
    return rings


def all_sum(value):
    for axis, stride, n in mesh_rings() + [("cross", 1, lax.axis_size("cross"))]:
        value = ring_sum(value, axis, stride, n)
    return value


def slab_gather(value):
    parts = value
    for axis, stride, n in mesh_rings():
        parts = ring_gather(parts, axis, stride, n)
    return parts


def ring_rounds(slab, cross):
    return [(0, 1, 2), (0, 2, 4), (0, 8, slab // 8), (1, 1, cross)]


def partner(me, stride, n, shift):
    pos = (me // stride) % n
    return me - pos * stride + ((pos + shift) % n) * stride


def step_kernel(rounds, per_ref, st_ref, vel_ref, pooled_ref, states_ref, adv_ref, held, sends, recvs,
                st_sends, st_recvs, xlo, xhi, ylo, yhi, face_sends, face_recvs):
    here = (lax.axis_index("slab"), lax.axis_index("cross"))
    slab, cross = lax.axis_size("slab"), lax.axis_size("cross")
    planes = vel_ref.shape[1]
    ny = vel_ref.shape[2]
    s, c = here

    def device(axis, other):
        return (other, here[1]) if axis == 0 else (here[0], other)

    extra = s - 1 + 2 * (s % 2)
    barrier = pltpu.get_barrier_semaphore()
    count = 0
    for axis, stride, n in rounds:
        for j in range(1, n):
            pl.semaphore_signal(barrier, inc=1, device_id=device(axis, partner(here[axis], stride, n, j)), device_id_type=MESH)
            count += 1
    pl.semaphore_signal(barrier, inc=1, device_id=((extra + slab) % slab, c), device_id_type=MESH)
    pl.semaphore_wait(barrier, count + 1)

    faces = [
        (s > 0, s < slab - 1, vel_ref.at[:, 0], xhi, ((s + slab - 1) % slab, c)),
        (s < slab - 1, s > 0, vel_ref.at[:, planes - 1], xlo, ((s + 1) % slab, c)),
        (c > 0, c < cross - 1, vel_ref.at[:, :, pl.ds(0, 1)], yhi, (s, (c + cross - 1) % cross)),
        (c < cross - 1, c > 0, vel_ref.at[:, :, pl.ds(ny - 1, 1)], ylo, (s, (c + 1) % cross)),
    ]
    face_copies = []
    for k, (send_if, recv_if, src, dst, dev) in enumerate(faces):
        copy = pltpu.make_async_remote_copy(
            src_ref=src, dst_ref=dst, send_sem=face_sends.at[k], recv_sem=face_recvs.at[k],
            device_id=dev, device_id_type=MESH,
        )

        @pl.when(send_if)
        def _():
            copy.start()

        @pl.when(jnp.logical_not(recv_if))
        def _():
            dst[...] = jnp.zeros(dst.shape, dst.dtype)

        face_copies.append((send_if, recv_if, copy))

    states_ref[pl.ds(s, 1)] = st_ref[...][None]
    pooled_ref[...] = per_ref[...]
    chunks = [None, (0, 6), (6, 11), (11, planes)]
    for r, (axis, stride, n) in enumerate(rounds):
        copies = []
        for j in range(1, n):
            dev = device(axis, partner(here[axis], stride, n, j))
            copy = pltpu.make_async_remote_copy(
                src_ref=pooled_ref,
                dst_ref=held.at[r, j - 1],
                send_sem=sends.at[r, j - 1],
                recv_sem=recvs.at[r, j - 1],
                device_id=dev,
                device_id_type=MESH,
            )
            copy.start()
            copies.append(copy)
            if axis == 0:
                rows = pl.ds(s - s % stride, stride)
                block = pltpu.make_async_remote_copy(
                    src_ref=states_ref.at[rows],
                    dst_ref=states_ref.at[rows],
                    send_sem=st_sends.at[r, j - 1],
                    recv_sem=st_recvs.at[r, j - 1],
                    device_id=dev,
                    device_id_type=MESH,
                )
                block.start()
                copies.append(block)
        if r == 1:
            for send_if, recv_if, face in face_copies:

                @pl.when(send_if)
                def _():
                    face.wait_send()

                @pl.when(recv_if)
                def _():
                    face.wait_recv()
        if chunks[r] is not None:
            first, last = chunks[r]

            def body(x, carry):
                results = stencil_plane(x, planes, vel_ref, xlo, xhi, ylo, yhi)
                for k in range(3):
                    adv_ref[k, x] = results[k]
                return carry

            lax.fori_loop(first, last, body, 0)
        for copy in copies:
            copy.wait()
        if n == 2:
            total = pooled_ref[...] + held[r, 0]
        else:
            total = (pooled_ref[...] + held[r, 1]) + (held[r, 0] + held[r, 2])
        pooled_ref[...] = total


def reduce_step(per_rotor, rotor_states, velocity):
    slab, cross = lax.axis_size("slab"), lax.axis_size("cross")
    rounds = ring_rounds(slab, cross)
    vmem = pl.BlockSpec(memory_space=pltpu.VMEM)
    _, planes, ny, nz = velocity.shape
    return pl.pallas_call(
        lambda *refs: step_kernel(rounds, *refs),
        out_shape=(
            jax.ShapeDtypeStruct(per_rotor.shape, jnp.float32),
            jax.ShapeDtypeStruct((slab,) + rotor_states.shape, jnp.float32),
            jax.ShapeDtypeStruct(velocity.shape, jnp.float32),
        ),
        in_specs=[vmem, vmem, vmem],
        out_specs=(vmem, vmem, vmem),
        scratch_shapes=[
            pltpu.VMEM((len(rounds), 3) + per_rotor.shape, jnp.float32),
            pltpu.SemaphoreType.DMA((len(rounds), 3)),
            pltpu.SemaphoreType.DMA((len(rounds), 3)),
            pltpu.SemaphoreType.DMA((len(rounds), 3)),
            pltpu.SemaphoreType.DMA((len(rounds), 3)),
            pltpu.VMEM((3, ny, nz), jnp.float32),
            pltpu.VMEM((3, ny, nz), jnp.float32),
            pltpu.VMEM((3, planes, 1, nz), jnp.float32),
            pltpu.VMEM((3, planes, 1, nz), jnp.float32),
            pltpu.SemaphoreType.DMA((4,)),
            pltpu.SemaphoreType.DMA((4,)),
        ],
        compiler_params=pltpu.CompilerParams(collective_id=0, has_side_effects=True),
    )(per_rotor, rotor_states, velocity)


def stencil_plane(x, planes, vel_ref, xlo_ref, xhi_ref, ylo_ref, yhi_ref):
    _, _, ny, nz = vel_ref.shape
    rows = lax.broadcasted_iota(jnp.int32, (ny, nz), 0)
    lanes = lax.broadcasted_iota(jnp.int32, (ny, nz), 1)
    here = [vel_ref[c, x] for c in range(3)]
    results = []
    for c in range(3):
        u = here[c]
        west = jnp.where(x == 0, xlo_ref[c].astype(jnp.float32), vel_ref[c, jnp.maximum(x - 1, 0)])
        east = jnp.where(x == planes - 1, xhi_ref[c].astype(jnp.float32), vel_ref[c, jnp.minimum(x + 1, planes - 1)])
        south = jnp.where(rows == 0, ylo_ref[c, x].astype(jnp.float32), pltpu.roll(u, 1, 0))
        north = jnp.where(rows == ny - 1, yhi_ref[c, x].astype(jnp.float32), pltpu.roll(u, ny - 1, 0))
        lower = jnp.where(lanes == 0, 0.0, pltpu.roll(u, 1, 1))
        upper = jnp.where(lanes == nz - 1, 0.0, pltpu.roll(u, nz - 1, 1))
        laplace = east + west + north + south + upper + lower - 6.0 * u
        advect = (
            here[0] * ((east - west) * 0.5)
            + here[1] * ((north - south) * 0.5)
            + here[2] * ((upper - lower) * 0.5)
        )
        results.append(u + time_step * (viscosity * laplace - advect))
    return results


def stencil_kernel(vel_ref, xlo_ref, xhi_ref, ylo_ref, yhi_ref, force_ref, out_ref):
    planes = vel_ref.shape[1]

    def body(x, carry):
        results = stencil_plane(x, planes, vel_ref, xlo_ref, xhi_ref, ylo_ref, yhi_ref)
        out_ref[0, x] = results[0] - force_scale * force_ref[x]
        out_ref[1, x] = results[1]
        out_ref[2, x] = results[2]
        return carry

    lax.fori_loop(0, planes, body, 0)


def stencil(velocity, halos, forcing):
    vmem = pl.BlockSpec(memory_space=pltpu.VMEM)
    return pl.pallas_call(
        stencil_kernel,
        out_shape=jax.ShapeDtypeStruct(velocity.shape, velocity.dtype),
        in_specs=[vmem] * 6,
        out_specs=vmem,
    )(velocity, *halos, forcing)


def halo_faces(velocity):
    faces = []
    for axis, dim in (("slab", 1), ("cross", 2)):
        count = lax.axis_size(axis)
        size = velocity.shape[dim]
        head = lax.slice_in_dim(velocity, 0, 1, axis=dim).astype(jnp.bfloat16)
        tail = lax.slice_in_dim(velocity, size - 1, size, axis=dim).astype(jnp.bfloat16)
        low = lax.ppermute(tail, axis, [(i, i + 1) for i in range(count - 1)])
        high = lax.ppermute(head, axis, [(i + 1, i) for i in range(count - 1)])
        faces += [jnp.squeeze(low, dim), jnp.squeeze(high, dim)] if dim == 1 else [low, high]
    return faces


def extended(cells, sides, width):
    for axis, dim in sides:
        count = lax.axis_size(axis)
        ends = count - 1
        head = lax.slice_in_dim(cells, 0, width, axis=dim)
        tail = lax.slice_in_dim(cells, cells.shape[dim] - width, cells.shape[dim], axis=dim)
        cells = jnp.concatenate(
            [
                lax.ppermute(tail, axis, [(i, (i + 1) % count) for i in range(ends)]),
                cells,
                lax.ppermute(head, axis, [((i + 1) % count, i) for i in range(ends)]),
            ],
            axis=dim,
        )
    return cells


def combine_terms(velocity, east, west, north, south, upper, lower):
    laplace = east + west + north + south + upper + lower - 6.0 * velocity
    advect = (
        velocity[0:1] * ((east - west) * 0.5)
        + velocity[1:2] * ((north - south) * 0.5)
        + velocity[2:3] * ((upper - lower) * 0.5)
    )
    return velocity + time_step * (viscosity * laplace - advect)


def on_device(
    velocity,
    shape_weight,
    w_in,
    w_out,
    decay,
    rotor_states,
    slot_of_rotor,
    entry_rotor,
    entry_tile,
    entry_sub,
):
    local_x, local_y, local_z = (velocity.shape[1], velocity.shape[2], velocity.shape[3])
    tile_count = local_x * local_y * local_z // TILE
    rotor_hot = (entry_rotor == jnp.arange(R, dtype=jnp.int32)[None, :]).astype(jnp.int32)
    slots = jnp.sum(rotor_hot * slot_of_rotor[None, :], axis=1)
    sub_range = jnp.arange(NSUB, dtype=jnp.int32)
    sub_hot = (entry_sub[:, None] == sub_range[None, :]).astype(jnp.bfloat16)
    high = lax.reduce_precision(shape_weight, exponent_bits=8, mantissa_bits=7)
    rest = shape_weight - high
    middle = lax.reduce_precision(rest, exponent_bits=8, mantissa_bits=7)
    low = rest - middle
    gains = [
        jnp.dot(sub_hot, part.astype(jnp.bfloat16), preferred_element_type=jnp.float32)
        for part in (high, middle, low)
    ]
    gains = (gains[0] + gains[1]) + gains[2]
    slot_hot = (slots[:, None] == jnp.arange(R, dtype=jnp.int32)[None, :]).astype(jnp.float32)
    cells_xy = local_x * local_y
    halves = local_z // TILE
    half = (entry_tile % halves)[:, None]
    place_hot = (jnp.arange(cells_xy, dtype=jnp.int32)[:, None] == (entry_tile // halves)[None, :]).astype(jnp.bfloat16)
    per_rotor = []
    for c in range(3):
        cells = velocity[c].reshape(cells_xy, local_z).astype(jnp.bfloat16)
        both = jnp.dot(place_hot.T, cells, preferred_element_type=jnp.float32)
        picked = both[:, :TILE]
        for h in range(1, halves):
            picked = jnp.where(half == h, both[:, h * TILE:(h + 1) * TILE], picked)
        weighted = gains[:, c * TILE:(c + 1) * TILE] * picked
        per_rotor.append(jnp.dot(slot_hot.T, weighted, precision=lax.Precision.HIGHEST))
    per_rotor = jnp.concatenate(per_rotor, axis=1)
    pooled, all_states, advanced = reduce_step(per_rotor, rotor_states, velocity)
    all_states = all_states.reshape(-1, rotor_states.shape[1])
    pooled_b = (pooled * pool_scale).astype(jnp.bfloat16)
    drive = jnp.dot(pooled_b, w_in, preferred_element_type=jnp.float32)
    all_new = all_states + state_step * (drive - decay[None, :] * all_states)
    all_sources = jnp.dot(
        all_new.astype(jnp.bfloat16), w_out, preferred_element_type=jnp.float32
    ).astype(jnp.bfloat16)
    new_states = lax.dynamic_slice_in_dim(all_new, lax.axis_index("slab"), 1, axis=0)
    flat = all_sources.reshape(R * NSUB, TILE)
    row_hot = ((slots * NSUB + entry_sub)[:, None] == jnp.arange(R * NSUB, dtype=jnp.int32)[None, :]).astype(jnp.bfloat16)
    rows = jnp.dot(row_hot, flat, preferred_element_type=jnp.float32).astype(jnp.bfloat16)
    wide = jnp.concatenate([jnp.where(half == h, rows, jnp.zeros_like(rows)) for h in range(halves)], axis=1)
    forcing = jnp.dot(place_hot, wide, preferred_element_type=jnp.float32).reshape(local_x, local_y, local_z)
    advanced = advanced.at[0].add(-force_scale * forcing)
    return (advanced, new_states)


def solution(mesh):
    in_specs = (
        P(None, "slab", "cross", None),
        P(),
        P(),
        P(),
        P(),
        P("slab", None),
        P(),
        P(("slab", "cross"), None),
        P(("slab", "cross")),
        P(("slab", "cross")),
    )
    out_specs = (P(None, "slab", "cross", None), P("slab", None))
    return jax.shard_map(
        on_device, mesh=mesh, in_specs=in_specs, out_specs=out_specs, check_vma=False
    )
```

```python
import jax
import jax.numpy as jnp
from jax import lax
from jax.experimental import pallas as pl
from jax.experimental.pallas import tpu as pltpu
from jax.sharding import PartitionSpec as P

MESH = pl.DeviceIdType.MESH

TILE = 128
R = 32
NSUB = 32


time_step = 0.1
viscosity = 0.3
pool_scale = 1.0 / 64.0
state_step = 0.5
force_scale = 0.5


def ring_perm(size, stride, n, shift):
    pairs = []
    for s in range(size):
        base = (s // (stride * n)) * stride * n + s % stride
        pos = (s // stride) % n
        pairs.append((s, base + ((pos + shift) % n) * stride))
    return pairs


def ring_sum(value, axis, stride, n):
    size = lax.axis_size(axis)
    if n == 2:
        return value + lax.ppermute(value, axis, ring_perm(size, stride, n, 1))
    got = [lax.ppermute(value, axis, ring_perm(size, stride, n, j)) for j in (1, 2, 3)]
    return (value + got[1]) + (got[0] + got[2])


def ring_gather(value, axis, stride, n):
    size = lax.axis_size(axis)
    pos = (lax.axis_index(axis) // stride) % n
    got = [value] + [lax.ppermute(value, axis, ring_perm(size, stride, n, j)) for j in range(1, n)]
    parts = []
    for p in range(n):
        pick = got[0]
        for j in range(1, n):
            pick = jnp.where((pos - j) % n == p, got[j], pick)
        parts.append(jnp.where(pos == p, got[0], pick))
    return jnp.concatenate(parts, axis=0)


def mesh_rings():
    slab = lax.axis_size("slab")
    rings = [("slab", 1, 2), ("slab", 2, 4), ("slab", 8, slab // 8)]
    return rings


def all_sum(value):
    for axis, stride, n in mesh_rings() + [("cross", 1, lax.axis_size("cross"))]:
        value = ring_sum(value, axis, stride, n)
    return value


def slab_gather(value):
    parts = value
    for axis, stride, n in mesh_rings():
        parts = ring_gather(parts, axis, stride, n)
    return parts


def ring_rounds(slab, cross):
    return [(0, 1, 2), (0, 2, 4), (0, 8, slab // 8), (1, 1, cross)]


def partner(me, stride, n, shift):
    pos = (me // stride) % n
    return me - pos * stride + ((pos + shift) % n) * stride


def step_kernel(rounds, per_ref, st_ref, vel_ref, w_in_ref, decay_ref, w_out_hbm, src_ref, own_ref, adv_ref,
                states_ref, pooled_ref, held, sends, recvs, st_sends, st_recvs, xlo, xhi, ylo, yhi, face_sends,
                face_recvs, w_out_ref, new_ref, w_sem):
    here = (lax.axis_index("slab"), lax.axis_index("cross"))
    slab, cross = lax.axis_size("slab"), lax.axis_size("cross")
    planes = vel_ref.shape[1]
    ny = vel_ref.shape[2]
    s, c = here

    def device(axis, other):
        return (other, here[1]) if axis == 0 else (here[0], other)

    extra = s - 1 + 2 * (s % 2)
    barrier = pltpu.get_barrier_semaphore()
    count = 0
    for axis, stride, n in rounds:
        for j in range(1, n):
            pl.semaphore_signal(barrier, inc=1, device_id=device(axis, partner(here[axis], stride, n, j)), device_id_type=MESH)
            count += 1
    pl.semaphore_signal(barrier, inc=1, device_id=((extra + slab) % slab, c), device_id_type=MESH)
    pl.semaphore_wait(barrier, count + 1)

    faces = [
        (s > 0, s < slab - 1, vel_ref.at[:, 0], xhi, ((s + slab - 1) % slab, c)),
        (s < slab - 1, s > 0, vel_ref.at[:, planes - 1], xlo, ((s + 1) % slab, c)),
        (c > 0, c < cross - 1, vel_ref.at[:, :, pl.ds(0, 1)], yhi, (s, (c + cross - 1) % cross)),
        (c < cross - 1, c > 0, vel_ref.at[:, :, pl.ds(ny - 1, 1)], ylo, (s, (c + 1) % cross)),
    ]
    face_copies = []
    for k, (send_if, recv_if, src, dst, dev) in enumerate(faces):
        copy = pltpu.make_async_remote_copy(
            src_ref=src, dst_ref=dst, send_sem=face_sends.at[k], recv_sem=face_recvs.at[k],
            device_id=dev, device_id_type=MESH,
        )

        @pl.when(send_if)
        def _():
            copy.start()

        @pl.when(jnp.logical_not(recv_if))
        def _():
            dst[...] = jnp.zeros(dst.shape, dst.dtype)

        face_copies.append((send_if, recv_if, copy))

    w_copy = pltpu.make_async_copy(w_out_hbm, w_out_ref, w_sem)
    w_copy.start()
    states_ref[pl.ds(s, 1)] = st_ref[...][None]
    pooled_ref[...] = per_ref[...]
    chunks = [None, (0, 6), (6, 11), (11, planes)]
    for r, (axis, stride, n) in enumerate(rounds):
        copies = []
        for j in range(1, n):
            dev = device(axis, partner(here[axis], stride, n, j))
            copy = pltpu.make_async_remote_copy(
                src_ref=pooled_ref,
                dst_ref=held.at[r, j - 1],
                send_sem=sends.at[r, j - 1],
                recv_sem=recvs.at[r, j - 1],
                device_id=dev,
                device_id_type=MESH,
            )
            copy.start()
            copies.append(copy)
            if axis == 0:
                rows = pl.ds(s - s % stride, stride)
                block = pltpu.make_async_remote_copy(
                    src_ref=states_ref.at[rows],
                    dst_ref=states_ref.at[rows],
                    send_sem=st_sends.at[r, j - 1],
                    recv_sem=st_recvs.at[r, j - 1],
                    device_id=dev,
                    device_id_type=MESH,
                )
                block.start()
                copies.append(block)
        if r == 1:
            for send_if, recv_if, face in face_copies:

                @pl.when(send_if)
                def _():
                    face.wait_send()

                @pl.when(recv_if)
                def _():
                    face.wait_recv()
        if chunks[r] is not None:
            first, last = chunks[r]

            def body(x, carry):
                results = stencil_plane(x, planes, vel_ref, xlo, xhi, ylo, yhi)
                for k in range(3):
                    adv_ref[k, x] = results[k]
                return carry

            lax.fori_loop(first, last, body, 0)
        for copy in copies:
            copy.wait()
        if n == 2:
            total = pooled_ref[...] + held[r, 0]
        else:
            total = (pooled_ref[...] + held[r, 1]) + (held[r, 0] + held[r, 2])
        pooled_ref[...] = total

    pooled_b = (pooled_ref[...] * pool_scale).astype(jnp.bfloat16)
    drive = jnp.dot(pooled_b, w_in_ref[...], preferred_element_type=jnp.float32)
    decay = decay_ref[...]
    for k in range(states_ref.shape[0]):
        row = states_ref[k]
        new_ref[pl.ds(k, 1), :] = row + state_step * (drive[k:k + 1] - decay * row)
    slot_rows = lax.broadcasted_iota(jnp.int32, drive.shape, 0)
    own_drive = jnp.sum(jnp.where(slot_rows == s, drive, 0.0), axis=0, keepdims=True)
    own = st_ref[...]
    own_ref[...] = own + state_step * (own_drive - decay * own)
    w_copy.wait()
    src_ref[...] = jnp.dot(
        new_ref[...].astype(jnp.bfloat16), w_out_ref[...], preferred_element_type=jnp.float32
    ).astype(jnp.bfloat16)

def reduce_step(per_rotor, rotor_states, velocity, w_in, decay, w_out):
    slab, cross = lax.axis_size("slab"), lax.axis_size("cross")
    rounds = ring_rounds(slab, cross)
    vmem = pl.BlockSpec(memory_space=pltpu.VMEM)
    _, planes, ny, nz = velocity.shape
    return pl.pallas_call(
        lambda *refs: step_kernel(rounds, *refs),
        out_shape=(
            jax.ShapeDtypeStruct((slab, w_out.shape[1]), jnp.bfloat16),
            jax.ShapeDtypeStruct(rotor_states.shape, jnp.float32),
            jax.ShapeDtypeStruct(velocity.shape, jnp.float32),
        ),
        in_specs=[vmem] * 5 + [pl.BlockSpec(memory_space=pl.ANY)],
        out_specs=(vmem, vmem, vmem),
        scratch_shapes=[
            pltpu.VMEM((slab,) + rotor_states.shape, jnp.float32),
            pltpu.VMEM(per_rotor.shape, jnp.float32),
            pltpu.VMEM((len(rounds), 3) + per_rotor.shape, jnp.float32),
            pltpu.SemaphoreType.DMA((len(rounds), 3)),
            pltpu.SemaphoreType.DMA((len(rounds), 3)),
            pltpu.SemaphoreType.DMA((len(rounds), 3)),
            pltpu.SemaphoreType.DMA((len(rounds), 3)),
            pltpu.VMEM((3, ny, nz), jnp.float32),
            pltpu.VMEM((3, ny, nz), jnp.float32),
            pltpu.VMEM((3, planes, 1, nz), jnp.float32),
            pltpu.VMEM((3, planes, 1, nz), jnp.float32),
            pltpu.SemaphoreType.DMA((4,)),
            pltpu.SemaphoreType.DMA((4,)),
            pltpu.VMEM(w_out.shape, w_out.dtype),
            pltpu.VMEM((slab, w_out.shape[0]), jnp.float32),
            pltpu.SemaphoreType.DMA(()),
        ],
        compiler_params=pltpu.CompilerParams(collective_id=0, has_side_effects=True),
    )(per_rotor, rotor_states, velocity, w_in, decay.reshape(1, -1), w_out)

def stencil_plane(x, planes, vel_ref, xlo_ref, xhi_ref, ylo_ref, yhi_ref):
    _, _, ny, nz = vel_ref.shape
    rows = lax.broadcasted_iota(jnp.int32, (ny, nz), 0)
    lanes = lax.broadcasted_iota(jnp.int32, (ny, nz), 1)
    here = [vel_ref[c, x] for c in range(3)]
    results = []
    for c in range(3):
        u = here[c]
        west = jnp.where(x == 0, xlo_ref[c].astype(jnp.float32), vel_ref[c, jnp.maximum(x - 1, 0)])
        east = jnp.where(x == planes - 1, xhi_ref[c].astype(jnp.float32), vel_ref[c, jnp.minimum(x + 1, planes - 1)])
        south = jnp.where(rows == 0, ylo_ref[c, x].astype(jnp.float32), pltpu.roll(u, 1, 0))
        north = jnp.where(rows == ny - 1, yhi_ref[c, x].astype(jnp.float32), pltpu.roll(u, ny - 1, 0))
        lower = jnp.where(lanes == 0, 0.0, pltpu.roll(u, 1, 1))
        upper = jnp.where(lanes == nz - 1, 0.0, pltpu.roll(u, nz - 1, 1))
        laplace = east + west + north + south + upper + lower - 6.0 * u
        advect = (
            here[0] * ((east - west) * 0.5)
            + here[1] * ((north - south) * 0.5)
            + here[2] * ((upper - lower) * 0.5)
        )
        results.append(u + time_step * (viscosity * laplace - advect))
    return results


def stencil_kernel(vel_ref, xlo_ref, xhi_ref, ylo_ref, yhi_ref, force_ref, out_ref):
    planes = vel_ref.shape[1]

    def body(x, carry):
        results = stencil_plane(x, planes, vel_ref, xlo_ref, xhi_ref, ylo_ref, yhi_ref)
        out_ref[0, x] = results[0] - force_scale * force_ref[x]
        out_ref[1, x] = results[1]
        out_ref[2, x] = results[2]
        return carry

    lax.fori_loop(0, planes, body, 0)


def stencil(velocity, halos, forcing):
    vmem = pl.BlockSpec(memory_space=pltpu.VMEM)
    return pl.pallas_call(
        stencil_kernel,
        out_shape=jax.ShapeDtypeStruct(velocity.shape, velocity.dtype),
        in_specs=[vmem] * 6,
        out_specs=vmem,
    )(velocity, *halos, forcing)


def halo_faces(velocity):
    faces = []
    for axis, dim in (("slab", 1), ("cross", 2)):
        count = lax.axis_size(axis)
        size = velocity.shape[dim]
        head = lax.slice_in_dim(velocity, 0, 1, axis=dim).astype(jnp.bfloat16)
        tail = lax.slice_in_dim(velocity, size - 1, size, axis=dim).astype(jnp.bfloat16)
        low = lax.ppermute(tail, axis, [(i, i + 1) for i in range(count - 1)])
        high = lax.ppermute(head, axis, [(i + 1, i) for i in range(count - 1)])
        faces += [jnp.squeeze(low, dim), jnp.squeeze(high, dim)] if dim == 1 else [low, high]
    return faces


def extended(cells, sides, width):
    for axis, dim in sides:
        count = lax.axis_size(axis)
        ends = count - 1
        head = lax.slice_in_dim(cells, 0, width, axis=dim)
        tail = lax.slice_in_dim(cells, cells.shape[dim] - width, cells.shape[dim], axis=dim)
        cells = jnp.concatenate(
            [
                lax.ppermute(tail, axis, [(i, (i + 1) % count) for i in range(ends)]),
                cells,
                lax.ppermute(head, axis, [((i + 1) % count, i) for i in range(ends)]),
            ],
            axis=dim,
        )
    return cells


def combine_terms(velocity, east, west, north, south, upper, lower):
    laplace = east + west + north + south + upper + lower - 6.0 * velocity
    advect = (
        velocity[0:1] * ((east - west) * 0.5)
        + velocity[1:2] * ((north - south) * 0.5)
        + velocity[2:3] * ((upper - lower) * 0.5)
    )
    return velocity + time_step * (viscosity * laplace - advect)


def on_device(
    velocity,
    shape_weight,
    w_in,
    w_out,
    decay,
    rotor_states,
    slot_of_rotor,
    entry_rotor,
    entry_tile,
    entry_sub,
):
    local_x, local_y, local_z = (velocity.shape[1], velocity.shape[2], velocity.shape[3])
    tile_count = local_x * local_y * local_z // TILE
    rotor_hot = (entry_rotor == jnp.arange(R, dtype=jnp.int32)[None, :]).astype(jnp.int32)
    slots = jnp.sum(rotor_hot * slot_of_rotor[None, :], axis=1)
    sub_range = jnp.arange(NSUB, dtype=jnp.int32)
    sub_hot = (entry_sub[:, None] == sub_range[None, :]).astype(jnp.bfloat16)
    high = lax.reduce_precision(shape_weight, exponent_bits=8, mantissa_bits=7)
    rest = shape_weight - high
    middle = lax.reduce_precision(rest, exponent_bits=8, mantissa_bits=7)
    low = rest - middle
    gains = [
        jnp.dot(sub_hot, part.astype(jnp.bfloat16), preferred_element_type=jnp.float32)
        for part in (high, middle, low)
    ]
    gains = (gains[0] + gains[1]) + gains[2]
    slot_hot = (slots[:, None] == jnp.arange(R, dtype=jnp.int32)[None, :]).astype(jnp.float32)
    cells_xy = local_x * local_y
    halves = local_z // TILE
    half = (entry_tile % halves)[:, None]
    place_hot = (jnp.arange(cells_xy, dtype=jnp.int32)[:, None] == (entry_tile // halves)[None, :]).astype(jnp.bfloat16)
    per_rotor = []
    for c in range(3):
        cells = velocity[c].reshape(cells_xy, local_z).astype(jnp.bfloat16)
        both = jnp.dot(place_hot.T, cells, preferred_element_type=jnp.float32)
        picked = both[:, :TILE]
        for h in range(1, halves):
            picked = jnp.where(half == h, both[:, h * TILE:(h + 1) * TILE], picked)
        weighted = gains[:, c * TILE:(c + 1) * TILE] * picked
        per_rotor.append(jnp.dot(slot_hot.T, weighted, precision=lax.Precision.HIGHEST))
    per_rotor = jnp.concatenate(per_rotor, axis=1)
    all_sources, new_states, advanced = reduce_step(per_rotor, rotor_states, velocity, w_in, decay, w_out)
    flat = all_sources.reshape(R * NSUB, TILE)
    row_hot = ((slots * NSUB + entry_sub)[:, None] == jnp.arange(R * NSUB, dtype=jnp.int32)[None, :]).astype(jnp.bfloat16)
    rows = jnp.dot(row_hot, flat, preferred_element_type=jnp.float32).astype(jnp.bfloat16)
    wide = jnp.concatenate([jnp.where(half == h, rows, jnp.zeros_like(rows)) for h in range(halves)], axis=1)
    forcing = jnp.dot(place_hot, wide, preferred_element_type=jnp.float32).reshape(local_x, local_y, local_z)
    advanced = advanced.at[0].add(-force_scale * forcing)
    return (advanced, new_states)


def solution(mesh):
    in_specs = (
        P(None, "slab", "cross", None),
        P(),
        P(),
        P(),
        P(),
        P("slab", None),
        P(),
        P(("slab", "cross"), None),
        P(("slab", "cross")),
        P(("slab", "cross")),
    )
    out_specs = (P(None, "slab", "cross", None), P("slab", None))
    return jax.shard_map(
        on_device, mesh=mesh, in_specs=in_specs, out_specs=out_specs, check_vma=False
    )
```

```python
import jax
import jax.numpy as jnp
from jax import lax
from jax.experimental import pallas as pl
from jax.experimental.pallas import tpu as pltpu
from jax.sharding import PartitionSpec as P

MESH = pl.DeviceIdType.MESH

TILE = 128
R = 32
NSUB = 32


time_step = 0.1
viscosity = 0.3
pool_scale = 1.0 / 64.0
state_step = 0.5
force_scale = 0.5


def ring_perm(size, stride, n, shift):
    pairs = []
    for s in range(size):
        base = (s // (stride * n)) * stride * n + s % stride
        pos = (s // stride) % n
        pairs.append((s, base + ((pos + shift) % n) * stride))
    return pairs


def ring_sum(value, axis, stride, n):
    size = lax.axis_size(axis)
    if n == 2:
        return value + lax.ppermute(value, axis, ring_perm(size, stride, n, 1))
    got = [lax.ppermute(value, axis, ring_perm(size, stride, n, j)) for j in (1, 2, 3)]
    return (value + got[1]) + (got[0] + got[2])


def ring_gather(value, axis, stride, n):
    size = lax.axis_size(axis)
    pos = (lax.axis_index(axis) // stride) % n
    got = [value] + [lax.ppermute(value, axis, ring_perm(size, stride, n, j)) for j in range(1, n)]
    parts = []
    for p in range(n):
        pick = got[0]
        for j in range(1, n):
            pick = jnp.where((pos - j) % n == p, got[j], pick)
        parts.append(jnp.where(pos == p, got[0], pick))
    return jnp.concatenate(parts, axis=0)


def mesh_rings():
    slab = lax.axis_size("slab")
    rings = [("slab", 1, 2), ("slab", 2, 4), ("slab", 8, slab // 8)]
    return rings


def all_sum(value):
    for axis, stride, n in mesh_rings() + [("cross", 1, lax.axis_size("cross"))]:
        value = ring_sum(value, axis, stride, n)
    return value


def slab_gather(value):
    parts = value
    for axis, stride, n in mesh_rings():
        parts = ring_gather(parts, axis, stride, n)
    return parts


def ring_rounds(slab, cross):
    return [(0, 1, 2), (0, 2, 4), (0, 8, slab // 8), (1, 1, cross)]


def partner(me, stride, n, shift):
    pos = (me // stride) % n
    return me - pos * stride + ((pos + shift) % n) * stride


def pool_samples(vel_ref, parts_ref, sub_ref, pos_ref, half_ref, slot_ref):
    _, planes, ny, nz = vel_ref.shape
    entries = sub_ref.shape[0]
    cells_xy = planes * ny
    sub_hot = (sub_ref[...] == lax.broadcasted_iota(jnp.int32, (entries, parts_ref.shape[1]), 1)).astype(jnp.bfloat16)
    gains = [jnp.dot(sub_hot, parts_ref[k], preferred_element_type=jnp.float32) for k in range(3)]
    gains = (gains[0] + gains[1]) + gains[2]
    pick_hot = (pos_ref[...] == lax.broadcasted_iota(jnp.int32, (entries, cells_xy), 1)).astype(jnp.bfloat16)
    slot_hot = (slot_ref[...] == lax.broadcasted_iota(jnp.int32, (R, entries), 0)).astype(jnp.float32)
    half = half_ref[...]
    pooled = []
    for c in range(3):
        cells = vel_ref[c].reshape(cells_xy, nz).astype(jnp.bfloat16)
        both = jnp.dot(pick_hot, cells, preferred_element_type=jnp.float32)
        picked = both[:, :TILE]
        for h in range(1, nz // TILE):
            picked = jnp.where(half == h, both[:, h * TILE:(h + 1) * TILE], picked)
        weighted = gains[:, c * TILE:(c + 1) * TILE] * picked
        pooled.append(jnp.dot(slot_hot, weighted, precision=lax.Precision.HIGHEST, preferred_element_type=jnp.float32))
    return pooled


def step_kernel(rounds, parts_ref, sub_ref, pos_ref, half_ref, slot_ref, st_ref, vel_ref, w_in_ref, decay_ref,
                w_out_hbm, src_ref, own_ref, adv_ref,
                states_ref, pooled_ref, held, sends, recvs, st_sends, st_recvs, xlo, xhi, ylo, yhi, face_sends,
                face_recvs, w_out_ref, new_ref, w_sem):
    here = (lax.axis_index("slab"), lax.axis_index("cross"))
    slab, cross = lax.axis_size("slab"), lax.axis_size("cross")
    planes = vel_ref.shape[1]
    ny = vel_ref.shape[2]
    s, c = here

    def device(axis, other):
        return (other, here[1]) if axis == 0 else (here[0], other)

    extra = s - 1 + 2 * (s % 2)
    barrier = pltpu.get_barrier_semaphore()
    count = 0
    for axis, stride, n in rounds:
        for j in range(1, n):
            pl.semaphore_signal(barrier, inc=1, device_id=device(axis, partner(here[axis], stride, n, j)), device_id_type=MESH)
            count += 1
    pl.semaphore_signal(barrier, inc=1, device_id=((extra + slab) % slab, c), device_id_type=MESH)
    w_copy = pltpu.make_async_copy(w_out_hbm, w_out_ref, w_sem)
    w_copy.start()
    pooled = pool_samples(vel_ref, parts_ref, sub_ref, pos_ref, half_ref, slot_ref)
    for k in range(3):
        pooled_ref[:, k * TILE:(k + 1) * TILE] = pooled[k]
    states_ref[pl.ds(s, 1)] = st_ref[...][None]
    pl.semaphore_wait(barrier, count + 1)

    faces = [
        (s > 0, s < slab - 1, vel_ref.at[:, 0], xhi, ((s + slab - 1) % slab, c)),
        (s < slab - 1, s > 0, vel_ref.at[:, planes - 1], xlo, ((s + 1) % slab, c)),
        (c > 0, c < cross - 1, vel_ref.at[:, :, pl.ds(0, 1)], yhi, (s, (c + cross - 1) % cross)),
        (c < cross - 1, c > 0, vel_ref.at[:, :, pl.ds(ny - 1, 1)], ylo, (s, (c + 1) % cross)),
    ]
    face_copies = []
    for k, (send_if, recv_if, src, dst, dev) in enumerate(faces):
        copy = pltpu.make_async_remote_copy(
            src_ref=src, dst_ref=dst, send_sem=face_sends.at[k], recv_sem=face_recvs.at[k],
            device_id=dev, device_id_type=MESH,
        )

        @pl.when(send_if)
        def _():
            copy.start()

        @pl.when(jnp.logical_not(recv_if))
        def _():
            dst[...] = jnp.zeros(dst.shape, dst.dtype)

        face_copies.append((send_if, recv_if, copy))


    chunks = [None, (0, 6), (6, 11), (11, planes)]
    for r, (axis, stride, n) in enumerate(rounds):
        copies = []
        for j in range(1, n):
            dev = device(axis, partner(here[axis], stride, n, j))
            copy = pltpu.make_async_remote_copy(
                src_ref=pooled_ref,
                dst_ref=held.at[r, j - 1],
                send_sem=sends.at[r, j - 1],
                recv_sem=recvs.at[r, j - 1],
                device_id=dev,
                device_id_type=MESH,
            )
            copy.start()
            copies.append(copy)
            if axis == 0:
                rows = pl.ds(s - s % stride, stride)
                block = pltpu.make_async_remote_copy(
                    src_ref=states_ref.at[rows],
                    dst_ref=states_ref.at[rows],
                    send_sem=st_sends.at[r, j - 1],
                    recv_sem=st_recvs.at[r, j - 1],
                    device_id=dev,
                    device_id_type=MESH,
                )
                block.start()
                copies.append(block)
        if r == 1:
            for send_if, recv_if, face in face_copies:

                @pl.when(send_if)
                def _():
                    face.wait_send()

                @pl.when(recv_if)
                def _():
                    face.wait_recv()
        if chunks[r] is not None:
            first, last = chunks[r]

            def body(x, carry):
                results = stencil_plane(x, planes, vel_ref, xlo, xhi, ylo, yhi)
                for k in range(3):
                    adv_ref[k, x] = results[k]
                return carry

            lax.fori_loop(first, last, body, 0)
        for copy in copies:
            copy.wait()
        if n == 2:
            total = pooled_ref[...] + held[r, 0]
        else:
            total = (pooled_ref[...] + held[r, 1]) + (held[r, 0] + held[r, 2])
        pooled_ref[...] = total

    pooled_b = (pooled_ref[...] * pool_scale).astype(jnp.bfloat16)
    drive = jnp.dot(pooled_b, w_in_ref[...], preferred_element_type=jnp.float32)
    decay = decay_ref[...]
    for k in range(states_ref.shape[0]):
        row = states_ref[k]
        new_ref[pl.ds(k, 1), :] = row + state_step * (drive[k:k + 1] - decay * row)
    slot_rows = lax.broadcasted_iota(jnp.int32, drive.shape, 0)
    own_drive = jnp.sum(jnp.where(slot_rows == s, drive, 0.0), axis=0, keepdims=True)
    own = st_ref[...]
    own_ref[...] = own + state_step * (own_drive - decay * own)
    w_copy.wait()
    src_ref[...] = jnp.dot(
        new_ref[...].astype(jnp.bfloat16), w_out_ref[...], preferred_element_type=jnp.float32
    ).astype(jnp.bfloat16)

def reduce_step(index_parts, rotor_states, velocity, w_in, decay, w_out):
    slab, cross = lax.axis_size("slab"), lax.axis_size("cross")
    rounds = ring_rounds(slab, cross)
    vmem = pl.BlockSpec(memory_space=pltpu.VMEM)
    _, planes, ny, nz = velocity.shape
    return pl.pallas_call(
        lambda *refs: step_kernel(rounds, *refs),
        out_shape=(
            jax.ShapeDtypeStruct((slab, w_out.shape[1]), jnp.bfloat16),
            jax.ShapeDtypeStruct(rotor_states.shape, jnp.float32),
            jax.ShapeDtypeStruct(velocity.shape, jnp.float32),
        ),
        in_specs=[vmem] * 9 + [pl.BlockSpec(memory_space=pl.ANY)],
        out_specs=(vmem, vmem, vmem),
        scratch_shapes=[
            pltpu.VMEM((slab,) + rotor_states.shape, jnp.float32),
            pltpu.VMEM((R, 3 * TILE), jnp.float32),
            pltpu.VMEM((len(rounds), 3, R, 3 * TILE), jnp.float32),
            pltpu.SemaphoreType.DMA((len(rounds), 3)),
            pltpu.SemaphoreType.DMA((len(rounds), 3)),
            pltpu.SemaphoreType.DMA((len(rounds), 3)),
            pltpu.SemaphoreType.DMA((len(rounds), 3)),
            pltpu.VMEM((3, ny, nz), jnp.float32),
            pltpu.VMEM((3, ny, nz), jnp.float32),
            pltpu.VMEM((3, planes, 1, nz), jnp.float32),
            pltpu.VMEM((3, planes, 1, nz), jnp.float32),
            pltpu.SemaphoreType.DMA((4,)),
            pltpu.SemaphoreType.DMA((4,)),
            pltpu.VMEM(w_out.shape, w_out.dtype),
            pltpu.VMEM((slab, w_out.shape[0]), jnp.float32),
            pltpu.SemaphoreType.DMA(()),
        ],
        compiler_params=pltpu.CompilerParams(collective_id=0, has_side_effects=True),
    )(*index_parts, rotor_states, velocity, w_in, decay.reshape(1, -1), w_out)

def stencil_plane(x, planes, vel_ref, xlo_ref, xhi_ref, ylo_ref, yhi_ref):
    _, _, ny, nz = vel_ref.shape
    rows = lax.broadcasted_iota(jnp.int32, (ny, nz), 0)
    lanes = lax.broadcasted_iota(jnp.int32, (ny, nz), 1)
    here = [vel_ref[c, x] for c in range(3)]
    results = []
    for c in range(3):
        u = here[c]
        west = jnp.where(x == 0, xlo_ref[c].astype(jnp.float32), vel_ref[c, jnp.maximum(x - 1, 0)])
        east = jnp.where(x == planes - 1, xhi_ref[c].astype(jnp.float32), vel_ref[c, jnp.minimum(x + 1, planes - 1)])
        south = jnp.where(rows == 0, ylo_ref[c, x].astype(jnp.float32), pltpu.roll(u, 1, 0))
        north = jnp.where(rows == ny - 1, yhi_ref[c, x].astype(jnp.float32), pltpu.roll(u, ny - 1, 0))
        lower = jnp.where(lanes == 0, 0.0, pltpu.roll(u, 1, 1))
        upper = jnp.where(lanes == nz - 1, 0.0, pltpu.roll(u, nz - 1, 1))
        laplace = east + west + north + south + upper + lower - 6.0 * u
        advect = (
            here[0] * ((east - west) * 0.5)
            + here[1] * ((north - south) * 0.5)
            + here[2] * ((upper - lower) * 0.5)
        )
        results.append(u + time_step * (viscosity * laplace - advect))
    return results


def stencil_kernel(vel_ref, xlo_ref, xhi_ref, ylo_ref, yhi_ref, force_ref, out_ref):
    planes = vel_ref.shape[1]

    def body(x, carry):
        results = stencil_plane(x, planes, vel_ref, xlo_ref, xhi_ref, ylo_ref, yhi_ref)
        out_ref[0, x] = results[0] - force_scale * force_ref[x]
        out_ref[1, x] = results[1]
        out_ref[2, x] = results[2]
        return carry

    lax.fori_loop(0, planes, body, 0)


def stencil(velocity, halos, forcing):
    vmem = pl.BlockSpec(memory_space=pltpu.VMEM)
    return pl.pallas_call(
        stencil_kernel,
        out_shape=jax.ShapeDtypeStruct(velocity.shape, velocity.dtype),
        in_specs=[vmem] * 6,
        out_specs=vmem,
    )(velocity, *halos, forcing)


def halo_faces(velocity):
    faces = []
    for axis, dim in (("slab", 1), ("cross", 2)):
        count = lax.axis_size(axis)
        size = velocity.shape[dim]
        head = lax.slice_in_dim(velocity, 0, 1, axis=dim).astype(jnp.bfloat16)
        tail = lax.slice_in_dim(velocity, size - 1, size, axis=dim).astype(jnp.bfloat16)
        low = lax.ppermute(tail, axis, [(i, i + 1) for i in range(count - 1)])
        high = lax.ppermute(head, axis, [(i + 1, i) for i in range(count - 1)])
        faces += [jnp.squeeze(low, dim), jnp.squeeze(high, dim)] if dim == 1 else [low, high]
    return faces


def extended(cells, sides, width):
    for axis, dim in sides:
        count = lax.axis_size(axis)
        ends = count - 1
        head = lax.slice_in_dim(cells, 0, width, axis=dim)
        tail = lax.slice_in_dim(cells, cells.shape[dim] - width, cells.shape[dim], axis=dim)
        cells = jnp.concatenate(
            [
                lax.ppermute(tail, axis, [(i, (i + 1) % count) for i in range(ends)]),
                cells,
                lax.ppermute(head, axis, [((i + 1) % count, i) for i in range(ends)]),
            ],
            axis=dim,
        )
    return cells


def combine_terms(velocity, east, west, north, south, upper, lower):
    laplace = east + west + north + south + upper + lower - 6.0 * velocity
    advect = (
        velocity[0:1] * ((east - west) * 0.5)
        + velocity[1:2] * ((north - south) * 0.5)
        + velocity[2:3] * ((upper - lower) * 0.5)
    )
    return velocity + time_step * (viscosity * laplace - advect)


def on_device(
    velocity,
    shape_weight,
    w_in,
    w_out,
    decay,
    rotor_states,
    slot_of_rotor,
    entry_rotor,
    entry_tile,
    entry_sub,
):
    local_x, local_y, local_z = (velocity.shape[1], velocity.shape[2], velocity.shape[3])
    tile_count = local_x * local_y * local_z // TILE
    rotor_hot = (entry_rotor == jnp.arange(R, dtype=jnp.int32)[None, :]).astype(jnp.int32)
    slots = jnp.sum(rotor_hot * slot_of_rotor[None, :], axis=1)
    high = lax.reduce_precision(shape_weight, exponent_bits=8, mantissa_bits=7)
    rest = shape_weight - high
    middle = lax.reduce_precision(rest, exponent_bits=8, mantissa_bits=7)
    low = rest - middle
    parts = jnp.stack([high, middle, low]).astype(jnp.bfloat16)
    cells_xy = local_x * local_y
    halves = local_z // TILE
    half = (entry_tile % halves)[:, None]
    index_parts = (parts, entry_sub[:, None], (entry_tile // halves)[:, None], half, slots[None, :])
    all_sources, new_states, advanced = reduce_step(index_parts, rotor_states, velocity, w_in, decay, w_out)
    flat = all_sources.reshape(R * NSUB, TILE)
    row_hot = ((slots * NSUB + entry_sub)[:, None] == jnp.arange(R * NSUB, dtype=jnp.int32)[None, :]).astype(jnp.bfloat16)
    rows = jnp.dot(row_hot, flat, preferred_element_type=jnp.float32).astype(jnp.bfloat16)
    wide = jnp.concatenate([jnp.where(half == h, rows, jnp.zeros_like(rows)) for h in range(halves)], axis=1)
    place_hot = (jnp.arange(cells_xy, dtype=jnp.int32)[:, None] == (entry_tile // halves)[None, :]).astype(jnp.bfloat16)
    forcing = jnp.dot(place_hot, wide, preferred_element_type=jnp.float32).reshape(local_x, local_y, local_z)
    advanced = advanced.at[0].add(-force_scale * forcing)
    return (advanced, new_states)


def solution(mesh):
    in_specs = (
        P(None, "slab", "cross", None),
        P(),
        P(),
        P(),
        P(),
        P("slab", None),
        P(),
        P(("slab", "cross"), None),
        P(("slab", "cross")),
        P(("slab", "cross")),
    )
    out_specs = (P(None, "slab", "cross", None), P("slab", None))
    return jax.shard_map(
        on_device, mesh=mesh, in_specs=in_specs, out_specs=out_specs, check_vma=False
    )
```

```python
import jax
import jax.numpy as jnp
from jax import lax
from jax.experimental import pallas as pl
from jax.experimental.pallas import tpu as pltpu
from jax.sharding import PartitionSpec as P

MESH = pl.DeviceIdType.MESH

TILE = 128
R = 32
NSUB = 32


time_step = 0.1
viscosity = 0.3
pool_scale = 1.0 / 64.0
state_step = 0.5
force_scale = 0.5


def ring_perm(size, stride, n, shift):
    pairs = []
    for s in range(size):
        base = (s // (stride * n)) * stride * n + s % stride
        pos = (s // stride) % n
        pairs.append((s, base + ((pos + shift) % n) * stride))
    return pairs


def ring_sum(value, axis, stride, n):
    size = lax.axis_size(axis)
    if n == 2:
        return value + lax.ppermute(value, axis, ring_perm(size, stride, n, 1))
    got = [lax.ppermute(value, axis, ring_perm(size, stride, n, j)) for j in (1, 2, 3)]
    return (value + got[1]) + (got[0] + got[2])


def ring_gather(value, axis, stride, n):
    size = lax.axis_size(axis)
    pos = (lax.axis_index(axis) // stride) % n
    got = [value] + [lax.ppermute(value, axis, ring_perm(size, stride, n, j)) for j in range(1, n)]
    parts = []
    for p in range(n):
        pick = got[0]
        for j in range(1, n):
            pick = jnp.where((pos - j) % n == p, got[j], pick)
        parts.append(jnp.where(pos == p, got[0], pick))
    return jnp.concatenate(parts, axis=0)


def mesh_rings():
    slab = lax.axis_size("slab")
    rings = [("slab", 1, 2), ("slab", 2, 4), ("slab", 8, slab // 8)]
    return rings


def all_sum(value):
    for axis, stride, n in mesh_rings() + [("cross", 1, lax.axis_size("cross"))]:
        value = ring_sum(value, axis, stride, n)
    return value


def slab_gather(value):
    parts = value
    for axis, stride, n in mesh_rings():
        parts = ring_gather(parts, axis, stride, n)
    return parts


def ring_rounds(slab, cross):
    return [(0, 1, 2), (0, 2, 4), (0, 8, slab // 8), (1, 1, cross)]


def partner(me, stride, n, shift):
    pos = (me // stride) % n
    return me - pos * stride + ((pos + shift) % n) * stride


def unpack(code_ref):
    code = code_ref[...]
    half = code % 2
    slot = (code // 2) % R
    sub = (code // (2 * R)) % NSUB
    pos = code // (2 * R * NSUB)
    return pos, sub, slot, half


def pool_samples(vel_ref, parts_ref, code_ref):
    _, planes, ny, nz = vel_ref.shape
    entries = code_ref.shape[0]
    cells_xy = planes * ny
    pos, sub, slot, half = unpack(code_ref)
    sub_hot = (sub == lax.broadcasted_iota(jnp.int32, (entries, parts_ref.shape[1]), 1)).astype(jnp.bfloat16)
    gains = [jnp.dot(sub_hot, parts_ref[k], preferred_element_type=jnp.float32) for k in range(3)]
    gains = (gains[0] + gains[1]) + gains[2]
    pick_hot = (pos == lax.broadcasted_iota(jnp.int32, (entries, cells_xy), 1)).astype(jnp.bfloat16)
    slot_hot = (slot == lax.broadcasted_iota(jnp.int32, (entries, R), 1)).astype(jnp.float32)
    pooled = []
    for c in range(3):
        cells = vel_ref[c].reshape(cells_xy, nz).astype(jnp.bfloat16)
        both = jnp.dot(pick_hot, cells, preferred_element_type=jnp.float32)
        picked = both[:, :TILE]
        for h in range(1, nz // TILE):
            picked = jnp.where(half == h, both[:, h * TILE:(h + 1) * TILE], picked)
        weighted = gains[:, c * TILE:(c + 1) * TILE] * picked
        pooled.append(
            lax.dot_general(
                slot_hot, weighted, (((0,), (0,)), ((), ())),
                precision=lax.Precision.HIGHEST, preferred_element_type=jnp.float32,
            )
        )
    return pooled


def place_forcing(src, code_ref, flat_ref, adv_ref):
    _, planes, ny, nz = adv_ref.shape
    entries = code_ref.shape[0]
    pos, sub, slot, half = unpack(code_ref)
    for j in range(NSUB):
        flat_ref[j * R:(j + 1) * R, :] = src[:, j * TILE:(j + 1) * TILE]
    row_hot = ((sub * R + slot) == lax.broadcasted_iota(jnp.int32, (entries, NSUB * R), 1)).astype(jnp.bfloat16)
    rows = jnp.dot(row_hot, flat_ref[...], preferred_element_type=jnp.float32)
    wide = jnp.concatenate(
        [jnp.where(half == h, rows, 0.0) for h in range(nz // TILE)], axis=1
    ).astype(jnp.bfloat16)
    pick_hot = (pos == lax.broadcasted_iota(jnp.int32, (entries, planes * ny), 1)).astype(jnp.bfloat16)
    forcing = lax.dot_general(pick_hot, wide, (((0,), (0,)), ((), ())), preferred_element_type=jnp.float32)
    adv_ref[0] = adv_ref[0] - force_scale * forcing.reshape(planes, ny, nz)

def step_kernel(rounds, parts_ref, code_ref, st_ref, vel_ref, w_in_ref, decay_ref,
                w_out_hbm, own_ref, adv_ref,
                states_ref, pooled_ref, held, sends, recvs, st_sends, st_recvs, xlo, xhi, ylo, yhi, face_sends,
                face_recvs, w_out_ref, new_ref, w_sem, flat_ref):
    here = (lax.axis_index("slab"), lax.axis_index("cross"))
    slab, cross = lax.axis_size("slab"), lax.axis_size("cross")
    planes = vel_ref.shape[1]
    ny = vel_ref.shape[2]
    s, c = here

    def device(axis, other):
        return (other, here[1]) if axis == 0 else (here[0], other)

    extra = s - 1 + 2 * (s % 2)
    barrier = pltpu.get_barrier_semaphore()
    count = 0
    for axis, stride, n in rounds:
        for j in range(1, n):
            pl.semaphore_signal(barrier, inc=1, device_id=device(axis, partner(here[axis], stride, n, j)), device_id_type=MESH)
            count += 1
    pl.semaphore_signal(barrier, inc=1, device_id=((extra + slab) % slab, c), device_id_type=MESH)
    w_copy = pltpu.make_async_copy(w_out_hbm, w_out_ref, w_sem)
    w_copy.start()
    pooled = pool_samples(vel_ref, parts_ref, code_ref)
    for k in range(3):
        pooled_ref[:, k * TILE:(k + 1) * TILE] = pooled[k]
    states_ref[pl.ds(s, 1)] = st_ref[...][None]
    pl.semaphore_wait(barrier, count + 1)

    faces = [
        (s > 0, s < slab - 1, vel_ref.at[:, 0], xhi, ((s + slab - 1) % slab, c)),
        (s < slab - 1, s > 0, vel_ref.at[:, planes - 1], xlo, ((s + 1) % slab, c)),
        (c > 0, c < cross - 1, vel_ref.at[:, :, pl.ds(0, 1)], yhi, (s, (c + cross - 1) % cross)),
        (c < cross - 1, c > 0, vel_ref.at[:, :, pl.ds(ny - 1, 1)], ylo, (s, (c + 1) % cross)),
    ]
    face_copies = []
    for k, (send_if, recv_if, src, dst, dev) in enumerate(faces):
        copy = pltpu.make_async_remote_copy(
            src_ref=src, dst_ref=dst, send_sem=face_sends.at[k], recv_sem=face_recvs.at[k],
            device_id=dev, device_id_type=MESH,
        )

        @pl.when(send_if)
        def _():
            copy.start()

        @pl.when(jnp.logical_not(recv_if))
        def _():
            dst[...] = jnp.zeros(dst.shape, dst.dtype)

        face_copies.append((send_if, recv_if, copy))


    chunks = [None, (0, 6), (6, 11), (11, planes)]
    for r, (axis, stride, n) in enumerate(rounds):
        copies = []
        for j in range(1, n):
            dev = device(axis, partner(here[axis], stride, n, j))
            copy = pltpu.make_async_remote_copy(
                src_ref=pooled_ref,
                dst_ref=held.at[r, j - 1],
                send_sem=sends.at[r, j - 1],
                recv_sem=recvs.at[r, j - 1],
                device_id=dev,
                device_id_type=MESH,
            )
            copy.start()
            copies.append(copy)
            if axis == 0:
                rows = pl.ds(s - s % stride, stride)
                block = pltpu.make_async_remote_copy(
                    src_ref=states_ref.at[rows],
                    dst_ref=states_ref.at[rows],
                    send_sem=st_sends.at[r, j - 1],
                    recv_sem=st_recvs.at[r, j - 1],
                    device_id=dev,
                    device_id_type=MESH,
                )
                block.start()
                copies.append(block)
        if r == 1:
            for send_if, recv_if, face in face_copies:

                @pl.when(send_if)
                def _():
                    face.wait_send()

                @pl.when(recv_if)
                def _():
                    face.wait_recv()
        if chunks[r] is not None:
            first, last = chunks[r]

            def body(x, carry):
                results = stencil_plane(x, planes, vel_ref, xlo, xhi, ylo, yhi)
                for k in range(3):
                    adv_ref[k, x] = results[k]
                return carry

            lax.fori_loop(first, last, body, 0)
        for copy in copies:
            copy.wait()
        if n == 2:
            total = pooled_ref[...] + held[r, 0]
        else:
            total = (pooled_ref[...] + held[r, 1]) + (held[r, 0] + held[r, 2])
        pooled_ref[...] = total

    pooled_b = (pooled_ref[...] * pool_scale).astype(jnp.bfloat16)
    drive = jnp.dot(pooled_b, w_in_ref[...], preferred_element_type=jnp.float32)
    decay = decay_ref[...]
    for k in range(states_ref.shape[0]):
        row = states_ref[k]
        new_ref[pl.ds(k, 1), :] = row + state_step * (drive[k:k + 1] - decay * row)
    slot_rows = lax.broadcasted_iota(jnp.int32, drive.shape, 0)
    own_drive = jnp.sum(jnp.where(slot_rows == s, drive, 0.0), axis=0, keepdims=True)
    own = st_ref[...]
    own_ref[...] = own + state_step * (own_drive - decay * own)
    w_copy.wait()
    src = jnp.dot(
        new_ref[...].astype(jnp.bfloat16), w_out_ref[...], preferred_element_type=jnp.float32
    ).astype(jnp.bfloat16)
    place_forcing(src, code_ref, flat_ref, adv_ref)

def reduce_step(index_parts, rotor_states, velocity, w_in, decay, w_out):
    slab, cross = lax.axis_size("slab"), lax.axis_size("cross")
    rounds = ring_rounds(slab, cross)
    vmem = pl.BlockSpec(memory_space=pltpu.VMEM)
    _, planes, ny, nz = velocity.shape
    return pl.pallas_call(
        lambda *refs: step_kernel(rounds, *refs),
        out_shape=(
            jax.ShapeDtypeStruct(rotor_states.shape, jnp.float32),
            jax.ShapeDtypeStruct(velocity.shape, jnp.float32),
        ),
        in_specs=[vmem] * 6 + [pl.BlockSpec(memory_space=pl.ANY)],
        out_specs=(vmem, vmem),
        scratch_shapes=[
            pltpu.VMEM((slab,) + rotor_states.shape, jnp.float32),
            pltpu.VMEM((R, 3 * TILE), jnp.float32),
            pltpu.VMEM((len(rounds), 3, R, 3 * TILE), jnp.float32),
            pltpu.SemaphoreType.DMA((len(rounds), 3)),
            pltpu.SemaphoreType.DMA((len(rounds), 3)),
            pltpu.SemaphoreType.DMA((len(rounds), 3)),
            pltpu.SemaphoreType.DMA((len(rounds), 3)),
            pltpu.VMEM((3, ny, nz), jnp.float32),
            pltpu.VMEM((3, ny, nz), jnp.float32),
            pltpu.VMEM((3, planes, 1, nz), jnp.float32),
            pltpu.VMEM((3, planes, 1, nz), jnp.float32),
            pltpu.SemaphoreType.DMA((4,)),
            pltpu.SemaphoreType.DMA((4,)),
            pltpu.VMEM(w_out.shape, w_out.dtype),
            pltpu.VMEM((slab, w_out.shape[0]), jnp.float32),
            pltpu.SemaphoreType.DMA(()),
            pltpu.VMEM((NSUB * R, TILE), jnp.bfloat16),
        ],
        compiler_params=pltpu.CompilerParams(collective_id=0, has_side_effects=True),
    )(*index_parts, rotor_states, velocity, w_in, decay.reshape(1, -1), w_out)

def stencil_plane(x, planes, vel_ref, xlo_ref, xhi_ref, ylo_ref, yhi_ref):
    _, _, ny, nz = vel_ref.shape
    rows = lax.broadcasted_iota(jnp.int32, (ny, nz), 0)
    lanes = lax.broadcasted_iota(jnp.int32, (ny, nz), 1)
    here = [vel_ref[c, x] for c in range(3)]
    results = []
    for c in range(3):
        u = here[c]
        west = jnp.where(x == 0, xlo_ref[c].astype(jnp.float32), vel_ref[c, jnp.maximum(x - 1, 0)])
        east = jnp.where(x == planes - 1, xhi_ref[c].astype(jnp.float32), vel_ref[c, jnp.minimum(x + 1, planes - 1)])
        south = jnp.where(rows == 0, ylo_ref[c, x].astype(jnp.float32), pltpu.roll(u, 1, 0))
        north = jnp.where(rows == ny - 1, yhi_ref[c, x].astype(jnp.float32), pltpu.roll(u, ny - 1, 0))
        lower = jnp.where(lanes == 0, 0.0, pltpu.roll(u, 1, 1))
        upper = jnp.where(lanes == nz - 1, 0.0, pltpu.roll(u, nz - 1, 1))
        laplace = east + west + north + south + upper + lower - 6.0 * u
        advect = (
            here[0] * ((east - west) * 0.5)
            + here[1] * ((north - south) * 0.5)
            + here[2] * ((upper - lower) * 0.5)
        )
        results.append(u + time_step * (viscosity * laplace - advect))
    return results


def stencil_kernel(vel_ref, xlo_ref, xhi_ref, ylo_ref, yhi_ref, force_ref, out_ref):
    planes = vel_ref.shape[1]

    def body(x, carry):
        results = stencil_plane(x, planes, vel_ref, xlo_ref, xhi_ref, ylo_ref, yhi_ref)
        out_ref[0, x] = results[0] - force_scale * force_ref[x]
        out_ref[1, x] = results[1]
        out_ref[2, x] = results[2]
        return carry

    lax.fori_loop(0, planes, body, 0)


def stencil(velocity, halos, forcing):
    vmem = pl.BlockSpec(memory_space=pltpu.VMEM)
    return pl.pallas_call(
        stencil_kernel,
        out_shape=jax.ShapeDtypeStruct(velocity.shape, velocity.dtype),
        in_specs=[vmem] * 6,
        out_specs=vmem,
    )(velocity, *halos, forcing)


def halo_faces(velocity):
    faces = []
    for axis, dim in (("slab", 1), ("cross", 2)):
        count = lax.axis_size(axis)
        size = velocity.shape[dim]
        head = lax.slice_in_dim(velocity, 0, 1, axis=dim).astype(jnp.bfloat16)
        tail = lax.slice_in_dim(velocity, size - 1, size, axis=dim).astype(jnp.bfloat16)
        low = lax.ppermute(tail, axis, [(i, i + 1) for i in range(count - 1)])
        high = lax.ppermute(head, axis, [(i + 1, i) for i in range(count - 1)])
        faces += [jnp.squeeze(low, dim), jnp.squeeze(high, dim)] if dim == 1 else [low, high]
    return faces


def extended(cells, sides, width):
    for axis, dim in sides:
        count = lax.axis_size(axis)
        ends = count - 1
        head = lax.slice_in_dim(cells, 0, width, axis=dim)
        tail = lax.slice_in_dim(cells, cells.shape[dim] - width, cells.shape[dim], axis=dim)
        cells = jnp.concatenate(
            [
                lax.ppermute(tail, axis, [(i, (i + 1) % count) for i in range(ends)]),
                cells,
                lax.ppermute(head, axis, [((i + 1) % count, i) for i in range(ends)]),
            ],
            axis=dim,
        )
    return cells


def combine_terms(velocity, east, west, north, south, upper, lower):
    laplace = east + west + north + south + upper + lower - 6.0 * velocity
    advect = (
        velocity[0:1] * ((east - west) * 0.5)
        + velocity[1:2] * ((north - south) * 0.5)
        + velocity[2:3] * ((upper - lower) * 0.5)
    )
    return velocity + time_step * (viscosity * laplace - advect)


def on_device(
    velocity,
    shape_weight,
    w_in,
    w_out,
    decay,
    rotor_states,
    slot_of_rotor,
    entry_rotor,
    entry_tile,
    entry_sub,
):
    local_x, local_y, local_z = (velocity.shape[1], velocity.shape[2], velocity.shape[3])
    tile_count = local_x * local_y * local_z // TILE
    rotor_hot = (entry_rotor == jnp.arange(R, dtype=jnp.int32)[None, :]).astype(jnp.int32)
    slots = jnp.sum(rotor_hot * slot_of_rotor[None, :], axis=1)
    high = lax.reduce_precision(shape_weight, exponent_bits=8, mantissa_bits=7)
    rest = shape_weight - high
    middle = lax.reduce_precision(rest, exponent_bits=8, mantissa_bits=7)
    low = rest - middle
    parts = jnp.stack([high, middle, low]).astype(jnp.bfloat16)
    halves = local_z // TILE
    code = (((entry_tile // halves) * NSUB + entry_sub) * R + slots) * halves + entry_tile % halves
    new_states, advanced = reduce_step((parts, code[:, None]), rotor_states, velocity, w_in, decay, w_out)
    return (advanced, new_states)


def solution(mesh):
    in_specs = (
        P(None, "slab", "cross", None),
        P(),
        P(),
        P(),
        P(),
        P("slab", None),
        P(),
        P(("slab", "cross"), None),
        P(("slab", "cross")),
        P(("slab", "cross")),
    )
    out_specs = (P(None, "slab", "cross", None), P("slab", None))
    return jax.shard_map(
        on_device, mesh=mesh, in_specs=in_specs, out_specs=out_specs, check_vma=False
    )
```

```python
import jax
import jax.numpy as jnp
from jax import lax
from jax.experimental import pallas as pl
from jax.experimental.pallas import tpu as pltpu
from jax.sharding import PartitionSpec as P

MESH = pl.DeviceIdType.MESH

TILE = 128
R = 32
NSUB = 32


time_step = 0.1
viscosity = 0.3
pool_scale = 1.0 / 64.0
state_step = 0.5
force_scale = 0.5


def ring_perm(size, stride, n, shift):
    pairs = []
    for s in range(size):
        base = (s // (stride * n)) * stride * n + s % stride
        pos = (s // stride) % n
        pairs.append((s, base + ((pos + shift) % n) * stride))
    return pairs


def ring_sum(value, axis, stride, n):
    size = lax.axis_size(axis)
    if n == 2:
        return value + lax.ppermute(value, axis, ring_perm(size, stride, n, 1))
    got = [lax.ppermute(value, axis, ring_perm(size, stride, n, j)) for j in (1, 2, 3)]
    return (value + got[1]) + (got[0] + got[2])


def ring_gather(value, axis, stride, n):
    size = lax.axis_size(axis)
    pos = (lax.axis_index(axis) // stride) % n
    got = [value] + [lax.ppermute(value, axis, ring_perm(size, stride, n, j)) for j in range(1, n)]
    parts = []
    for p in range(n):
        pick = got[0]
        for j in range(1, n):
            pick = jnp.where((pos - j) % n == p, got[j], pick)
        parts.append(jnp.where(pos == p, got[0], pick))
    return jnp.concatenate(parts, axis=0)


def mesh_rings():
    slab = lax.axis_size("slab")
    rings = [("slab", 1, 2), ("slab", 2, 4), ("slab", 8, slab // 8)]
    return rings


def all_sum(value):
    for axis, stride, n in mesh_rings() + [("cross", 1, lax.axis_size("cross"))]:
        value = ring_sum(value, axis, stride, n)
    return value


def slab_gather(value):
    parts = value
    for axis, stride, n in mesh_rings():
        parts = ring_gather(parts, axis, stride, n)
    return parts


def ring_rounds(slab, cross):
    return [(0, 1, 2), (0, 2, 4), (0, 8, slab // 8), (1, 1, cross)]


def partner(me, stride, n, shift):
    pos = (me // stride) % n
    return me - pos * stride + ((pos + shift) % n) * stride


def unpack(code_ref):
    code = code_ref[...]
    half = code % 2
    slot = (code // 2) % R
    sub = (code // (2 * R)) % NSUB
    pos = code // (2 * R * NSUB)
    return pos, sub, slot, half


def pool_samples(vel_ref, parts_ref, code_ref):
    _, planes, ny, nz = vel_ref.shape
    entries = code_ref.shape[0]
    cells_xy = planes * ny
    pos, sub, slot, half = unpack(code_ref)
    sub_hot = (sub == lax.broadcasted_iota(jnp.int32, (entries, parts_ref.shape[1]), 1)).astype(jnp.bfloat16)
    gains = [jnp.dot(sub_hot, parts_ref[k], preferred_element_type=jnp.float32) for k in range(3)]
    gains = (gains[0] + gains[1]) + gains[2]
    pick_hot = (pos == lax.broadcasted_iota(jnp.int32, (entries, cells_xy), 1)).astype(jnp.bfloat16)
    slot_hot = (slot == lax.broadcasted_iota(jnp.int32, (entries, R), 1)).astype(jnp.float32)
    pooled = []
    for c in range(3):
        cells = vel_ref[c].reshape(cells_xy, nz).astype(jnp.bfloat16)
        both = jnp.dot(pick_hot, cells, preferred_element_type=jnp.float32)
        picked = both[:, :TILE]
        for h in range(1, nz // TILE):
            picked = jnp.where(half == h, both[:, h * TILE:(h + 1) * TILE], picked)
        weighted = gains[:, c * TILE:(c + 1) * TILE] * picked
        pooled.append(
            lax.dot_general(
                slot_hot, weighted, (((0,), (0,)), ((), ())),
                precision=lax.Precision.HIGHEST, preferred_element_type=jnp.float32,
            )
        )
    return pooled


def place_forcing(src, code_ref, flat_ref, adv_ref):
    _, planes, ny, nz = adv_ref.shape
    entries = code_ref.shape[0]
    pos, sub, slot, half = unpack(code_ref)
    for j in range(NSUB):
        flat_ref[j * R:(j + 1) * R, :] = src[:, j * TILE:(j + 1) * TILE]
    row_hot = ((sub * R + slot) == lax.broadcasted_iota(jnp.int32, (entries, NSUB * R), 1)).astype(jnp.bfloat16)
    rows = jnp.dot(row_hot, flat_ref[...], preferred_element_type=jnp.float32)
    wide = jnp.concatenate(
        [jnp.where(half == h, rows, 0.0) for h in range(nz // TILE)], axis=1
    ).astype(jnp.bfloat16)
    pick_hot = (pos == lax.broadcasted_iota(jnp.int32, (entries, planes * ny), 1)).astype(jnp.bfloat16)
    forcing = lax.dot_general(pick_hot, wide, (((0,), (0,)), ((), ())), preferred_element_type=jnp.float32)
    adv_ref[0] = adv_ref[0] - force_scale * forcing.reshape(planes, ny, nz)

def step_kernel(rounds, parts_ref, code_ref, st_ref, vel_ref, w_in_ref, decay_ref,
                w_out_hbm, own_ref, adv_ref,
                states_ref, pooled_ref, held, sends, recvs, st_sends, st_recvs, xlo, xhi, ylo, yhi, face_sends,
                face_recvs, w_out_ref, new_ref, w_sem, flat_ref, swap_sems, swap_ref):
    here = (lax.axis_index("slab"), lax.axis_index("cross"))
    slab, cross = lax.axis_size("slab"), lax.axis_size("cross")
    planes = vel_ref.shape[1]
    ny = vel_ref.shape[2]
    s, c = here

    def device(axis, other):
        return (other, here[1]) if axis == 0 else (here[0], other)

    extra = s - 1 + 2 * (s % 2)
    barrier = pltpu.get_barrier_semaphore()
    count = 0
    for axis, stride, n in rounds:
        for j in range(1, n):
            pl.semaphore_signal(barrier, inc=1, device_id=device(axis, partner(here[axis], stride, n, j)), device_id_type=MESH)
            count += 1
    pl.semaphore_signal(barrier, inc=1, device_id=((extra + slab) % slab, c), device_id_type=MESH)
    w_copy = pltpu.make_async_copy(w_out_hbm, w_out_ref, w_sem)
    w_copy.start()
    pooled = pool_samples(vel_ref, parts_ref, code_ref)
    for k in range(3):
        pooled_ref[:, k * TILE:(k + 1) * TILE] = pooled[k]
    states_ref[pl.ds(s, 1)] = st_ref[...][None]
    pl.semaphore_wait(barrier, count + 1)

    faces = [
        (s > 0, s < slab - 1, vel_ref.at[:, 0], xhi, ((s + slab - 1) % slab, c)),
        (s < slab - 1, s > 0, vel_ref.at[:, planes - 1], xlo, ((s + 1) % slab, c)),
        (c > 0, c < cross - 1, vel_ref.at[:, :, pl.ds(0, 1)], yhi, (s, (c + cross - 1) % cross)),
        (c < cross - 1, c > 0, vel_ref.at[:, :, pl.ds(ny - 1, 1)], ylo, (s, (c + 1) % cross)),
    ]
    face_copies = []
    for k, (send_if, recv_if, src, dst, dev) in enumerate(faces):
        copy = pltpu.make_async_remote_copy(
            src_ref=src, dst_ref=dst, send_sem=face_sends.at[k], recv_sem=face_recvs.at[k],
            device_id=dev, device_id_type=MESH,
        )

        @pl.when(send_if)
        def _():
            copy.start()

        @pl.when(jnp.logical_not(recv_if))
        def _():
            dst[...] = jnp.zeros(dst.shape, dst.dtype)

        face_copies.append((send_if, recv_if, copy))


    chunks = [None, (0, 6), (6, 11), (11, planes)]
    share = R // 2
    mine = pl.ds(pl.multiple_of((s % 2) * share, share), share)
    for r, (axis, stride, n) in enumerate(rounds):
        copies = []
        for j in range(1, n):
            dev = device(axis, partner(here[axis], stride, n, j))
            copy = pltpu.make_async_remote_copy(
                src_ref=pooled_ref if r == 0 else pooled_ref.at[mine],
                dst_ref=held.at[r, j - 1] if r == 0 else held.at[r, j - 1, pl.ds(0, share)],
                send_sem=sends.at[r, j - 1],
                recv_sem=recvs.at[r, j - 1],
                device_id=dev,
                device_id_type=MESH,
            )
            copy.start()
            copies.append(copy)
            if axis == 0:
                rows = pl.ds(s - s % stride, stride)
                block = pltpu.make_async_remote_copy(
                    src_ref=states_ref.at[rows],
                    dst_ref=states_ref.at[rows],
                    send_sem=st_sends.at[r, j - 1],
                    recv_sem=st_recvs.at[r, j - 1],
                    device_id=dev,
                    device_id_type=MESH,
                )
                block.start()
                copies.append(block)
        if r == 1:
            for send_if, recv_if, face in face_copies:

                @pl.when(send_if)
                def _():
                    face.wait_send()

                @pl.when(recv_if)
                def _():
                    face.wait_recv()
        if chunks[r] is not None:
            first, last = chunks[r]

            def body(x, carry):
                results = stencil_plane(x, planes, vel_ref, xlo, xhi, ylo, yhi)
                for k in range(3):
                    adv_ref[k, x] = results[k]
                return carry

            lax.fori_loop(first, last, body, 0)
        for copy in copies:
            copy.wait()
        if r == 0:
            pooled_ref[mine, :] = pooled_ref[mine, :] + held[r, 0, mine, :]
        elif n == 2:
            pooled_ref[mine, :] = pooled_ref[mine, :] + held[r, 0, pl.ds(0, share)]
        else:
            got = [held[r, k, pl.ds(0, share)] for k in range(3)]
            pooled_ref[mine, :] = (pooled_ref[mine, :] + got[1]) + (got[0] + got[2])
    swap = pltpu.make_async_remote_copy(
        src_ref=pooled_ref.at[mine],
        dst_ref=swap_ref,
        send_sem=swap_sems.at[0],
        recv_sem=swap_sems.at[1],
        device_id=(s + 1 - 2 * (s % 2), c),
        device_id_type=MESH,
    )
    swap.start()
    swap.wait()
    pooled_ref[pl.ds(pl.multiple_of((1 - s % 2) * share, share), share), :] = swap_ref[...]

    pooled_b = (pooled_ref[...] * pool_scale).astype(jnp.bfloat16)
    drive = jnp.dot(pooled_b, w_in_ref[...], preferred_element_type=jnp.float32)
    decay = decay_ref[...]
    for k in range(states_ref.shape[0]):
        row = states_ref[k]
        new_ref[pl.ds(k, 1), :] = row + state_step * (drive[k:k + 1] - decay * row)
    slot_rows = lax.broadcasted_iota(jnp.int32, drive.shape, 0)
    own_drive = jnp.sum(jnp.where(slot_rows == s, drive, 0.0), axis=0, keepdims=True)
    own = st_ref[...]
    own_ref[...] = own + state_step * (own_drive - decay * own)
    w_copy.wait()
    src = jnp.dot(
        new_ref[...].astype(jnp.bfloat16), w_out_ref[...], preferred_element_type=jnp.float32
    ).astype(jnp.bfloat16)
    place_forcing(src, code_ref, flat_ref, adv_ref)

def reduce_step(index_parts, rotor_states, velocity, w_in, decay, w_out):
    slab, cross = lax.axis_size("slab"), lax.axis_size("cross")
    rounds = ring_rounds(slab, cross)
    vmem = pl.BlockSpec(memory_space=pltpu.VMEM)
    _, planes, ny, nz = velocity.shape
    return pl.pallas_call(
        lambda *refs: step_kernel(rounds, *refs),
        out_shape=(
            jax.ShapeDtypeStruct(rotor_states.shape, jnp.float32),
            jax.ShapeDtypeStruct(velocity.shape, jnp.float32),
        ),
        in_specs=[vmem] * 6 + [pl.BlockSpec(memory_space=pl.ANY)],
        out_specs=(vmem, vmem),
        scratch_shapes=[
            pltpu.VMEM((slab,) + rotor_states.shape, jnp.float32),
            pltpu.VMEM((R, 3 * TILE), jnp.float32),
            pltpu.VMEM((len(rounds), 3, R, 3 * TILE), jnp.float32),
            pltpu.SemaphoreType.DMA((len(rounds), 3)),
            pltpu.SemaphoreType.DMA((len(rounds), 3)),
            pltpu.SemaphoreType.DMA((len(rounds), 3)),
            pltpu.SemaphoreType.DMA((len(rounds), 3)),
            pltpu.VMEM((3, ny, nz), jnp.float32),
            pltpu.VMEM((3, ny, nz), jnp.float32),
            pltpu.VMEM((3, planes, 1, nz), jnp.float32),
            pltpu.VMEM((3, planes, 1, nz), jnp.float32),
            pltpu.SemaphoreType.DMA((4,)),
            pltpu.SemaphoreType.DMA((4,)),
            pltpu.VMEM(w_out.shape, w_out.dtype),
            pltpu.VMEM((slab, w_out.shape[0]), jnp.float32),
            pltpu.SemaphoreType.DMA(()),
            pltpu.VMEM((NSUB * R, TILE), jnp.bfloat16),
            pltpu.SemaphoreType.DMA((2,)),
            pltpu.VMEM((R // 2, 3 * TILE), jnp.float32),
        ],
        compiler_params=pltpu.CompilerParams(collective_id=0, has_side_effects=True),
    )(*index_parts, rotor_states, velocity, w_in, decay.reshape(1, -1), w_out)

def stencil_plane(x, planes, vel_ref, xlo_ref, xhi_ref, ylo_ref, yhi_ref):
    _, _, ny, nz = vel_ref.shape
    rows = lax.broadcasted_iota(jnp.int32, (ny, nz), 0)
    lanes = lax.broadcasted_iota(jnp.int32, (ny, nz), 1)
    here = [vel_ref[c, x] for c in range(3)]
    results = []
    for c in range(3):
        u = here[c]
        west = jnp.where(x == 0, xlo_ref[c].astype(jnp.float32), vel_ref[c, jnp.maximum(x - 1, 0)])
        east = jnp.where(x == planes - 1, xhi_ref[c].astype(jnp.float32), vel_ref[c, jnp.minimum(x + 1, planes - 1)])
        south = jnp.where(rows == 0, ylo_ref[c, x].astype(jnp.float32), pltpu.roll(u, 1, 0))
        north = jnp.where(rows == ny - 1, yhi_ref[c, x].astype(jnp.float32), pltpu.roll(u, ny - 1, 0))
        lower = jnp.where(lanes == 0, 0.0, pltpu.roll(u, 1, 1))
        upper = jnp.where(lanes == nz - 1, 0.0, pltpu.roll(u, nz - 1, 1))
        laplace = east + west + north + south + upper + lower - 6.0 * u
        advect = (
            here[0] * ((east - west) * 0.5)
            + here[1] * ((north - south) * 0.5)
            + here[2] * ((upper - lower) * 0.5)
        )
        results.append(u + time_step * (viscosity * laplace - advect))
    return results


def stencil_kernel(vel_ref, xlo_ref, xhi_ref, ylo_ref, yhi_ref, force_ref, out_ref):
    planes = vel_ref.shape[1]

    def body(x, carry):
        results = stencil_plane(x, planes, vel_ref, xlo_ref, xhi_ref, ylo_ref, yhi_ref)
        out_ref[0, x] = results[0] - force_scale * force_ref[x]
        out_ref[1, x] = results[1]
        out_ref[2, x] = results[2]
        return carry

    lax.fori_loop(0, planes, body, 0)


def stencil(velocity, halos, forcing):
    vmem = pl.BlockSpec(memory_space=pltpu.VMEM)
    return pl.pallas_call(
        stencil_kernel,
        out_shape=jax.ShapeDtypeStruct(velocity.shape, velocity.dtype),
        in_specs=[vmem] * 6,
        out_specs=vmem,
    )(velocity, *halos, forcing)


def halo_faces(velocity):
    faces = []
    for axis, dim in (("slab", 1), ("cross", 2)):
        count = lax.axis_size(axis)
        size = velocity.shape[dim]
        head = lax.slice_in_dim(velocity, 0, 1, axis=dim).astype(jnp.bfloat16)
        tail = lax.slice_in_dim(velocity, size - 1, size, axis=dim).astype(jnp.bfloat16)
        low = lax.ppermute(tail, axis, [(i, i + 1) for i in range(count - 1)])
        high = lax.ppermute(head, axis, [(i + 1, i) for i in range(count - 1)])
        faces += [jnp.squeeze(low, dim), jnp.squeeze(high, dim)] if dim == 1 else [low, high]
    return faces


def extended(cells, sides, width):
    for axis, dim in sides:
        count = lax.axis_size(axis)
        ends = count - 1
        head = lax.slice_in_dim(cells, 0, width, axis=dim)
        tail = lax.slice_in_dim(cells, cells.shape[dim] - width, cells.shape[dim], axis=dim)
        cells = jnp.concatenate(
            [
                lax.ppermute(tail, axis, [(i, (i + 1) % count) for i in range(ends)]),
                cells,
                lax.ppermute(head, axis, [((i + 1) % count, i) for i in range(ends)]),
            ],
            axis=dim,
        )
    return cells


def combine_terms(velocity, east, west, north, south, upper, lower):
    laplace = east + west + north + south + upper + lower - 6.0 * velocity
    advect = (
        velocity[0:1] * ((east - west) * 0.5)
        + velocity[1:2] * ((north - south) * 0.5)
        + velocity[2:3] * ((upper - lower) * 0.5)
    )
    return velocity + time_step * (viscosity * laplace - advect)


def on_device(
    velocity,
    shape_weight,
    w_in,
    w_out,
    decay,
    rotor_states,
    slot_of_rotor,
    entry_rotor,
    entry_tile,
    entry_sub,
):
    local_x, local_y, local_z = (velocity.shape[1], velocity.shape[2], velocity.shape[3])
    tile_count = local_x * local_y * local_z // TILE
    rotor_hot = (entry_rotor == jnp.arange(R, dtype=jnp.int32)[None, :]).astype(jnp.int32)
    slots = jnp.sum(rotor_hot * slot_of_rotor[None, :], axis=1)
    high = lax.reduce_precision(shape_weight, exponent_bits=8, mantissa_bits=7)
    rest = shape_weight - high
    middle = lax.reduce_precision(rest, exponent_bits=8, mantissa_bits=7)
    low = rest - middle
    parts = jnp.stack([high, middle, low]).astype(jnp.bfloat16)
    halves = local_z // TILE
    code = (((entry_tile // halves) * NSUB + entry_sub) * R + slots) * halves + entry_tile % halves
    new_states, advanced = reduce_step((parts, code[:, None]), rotor_states, velocity, w_in, decay, w_out)
    return (advanced, new_states)


def solution(mesh):
    in_specs = (
        P(None, "slab", "cross", None),
        P(),
        P(),
        P(),
        P(),
        P("slab", None),
        P(),
        P(("slab", "cross"), None),
        P(("slab", "cross")),
        P(("slab", "cross")),
    )
    out_specs = (P(None, "slab", "cross", None), P("slab", None))
    return jax.shard_map(
        on_device, mesh=mesh, in_specs=in_specs, out_specs=out_specs, check_vma=False
    )
```

```python
import jax
import jax.numpy as jnp
from jax import lax
from jax.experimental import pallas as pl
from jax.experimental.pallas import tpu as pltpu
from jax.sharding import PartitionSpec as P

MESH = pl.DeviceIdType.MESH

TILE = 128
R = 32
NSUB = 32


time_step = 0.1
viscosity = 0.3
pool_scale = 1.0 / 64.0
state_step = 0.5
force_scale = 0.5


def ring_perm(size, stride, n, shift):
    pairs = []
    for s in range(size):
        base = (s // (stride * n)) * stride * n + s % stride
        pos = (s // stride) % n
        pairs.append((s, base + ((pos + shift) % n) * stride))
    return pairs


def ring_sum(value, axis, stride, n):
    size = lax.axis_size(axis)
    if n == 2:
        return value + lax.ppermute(value, axis, ring_perm(size, stride, n, 1))
    got = [lax.ppermute(value, axis, ring_perm(size, stride, n, j)) for j in (1, 2, 3)]
    return (value + got[1]) + (got[0] + got[2])


def ring_gather(value, axis, stride, n):
    size = lax.axis_size(axis)
    pos = (lax.axis_index(axis) // stride) % n
    got = [value] + [lax.ppermute(value, axis, ring_perm(size, stride, n, j)) for j in range(1, n)]
    parts = []
    for p in range(n):
        pick = got[0]
        for j in range(1, n):
            pick = jnp.where((pos - j) % n == p, got[j], pick)
        parts.append(jnp.where(pos == p, got[0], pick))
    return jnp.concatenate(parts, axis=0)


def mesh_rings():
    slab = lax.axis_size("slab")
    rings = [("slab", 1, 2), ("slab", 2, 4), ("slab", 8, slab // 8)]
    return rings


def all_sum(value):
    for axis, stride, n in mesh_rings() + [("cross", 1, lax.axis_size("cross"))]:
        value = ring_sum(value, axis, stride, n)
    return value


def slab_gather(value):
    parts = value
    for axis, stride, n in mesh_rings():
        parts = ring_gather(parts, axis, stride, n)
    return parts


def ring_rounds(slab, cross):
    return [(0, 1, 2), (0, 2, 4), (0, 8, slab // 8), (1, 1, cross)]


def partner(me, stride, n, shift):
    pos = (me // stride) % n
    return me - pos * stride + ((pos + shift) % n) * stride


def unpack(code_ref):
    code = code_ref[...]
    half = code % 2
    slot = (code // 2) % R
    sub = (code // (2 * R)) % NSUB
    pos = code // (2 * R * NSUB)
    return pos, sub, slot, half


def pool_samples(vel_ref, parts_ref, code_ref):
    _, planes, ny, nz = vel_ref.shape
    entries = code_ref.shape[0]
    cells_xy = planes * ny
    pos, sub, slot, half = unpack(code_ref)
    sub_hot = (sub == lax.broadcasted_iota(jnp.int32, (entries, parts_ref.shape[1]), 1)).astype(jnp.bfloat16)
    gains = [jnp.dot(sub_hot, parts_ref[k], preferred_element_type=jnp.float32) for k in range(3)]
    gains = (gains[0] + gains[1]) + gains[2]
    pick_hot = (pos == lax.broadcasted_iota(jnp.int32, (entries, cells_xy), 1)).astype(jnp.bfloat16)
    slot_hot = (slot == lax.broadcasted_iota(jnp.int32, (entries, R), 1)).astype(jnp.float32)
    pooled = []
    for c in range(3):
        cells = vel_ref[c].reshape(cells_xy, nz).astype(jnp.bfloat16)
        both = jnp.dot(pick_hot, cells, preferred_element_type=jnp.float32)
        picked = both[:, :TILE]
        for h in range(1, nz // TILE):
            picked = jnp.where(half == h, both[:, h * TILE:(h + 1) * TILE], picked)
        weighted = gains[:, c * TILE:(c + 1) * TILE] * picked
        pooled.append(
            lax.dot_general(
                slot_hot, weighted, (((0,), (0,)), ((), ())),
                precision=lax.Precision.HIGHEST, preferred_element_type=jnp.float32,
            )
        )
    return pooled


def place_forcing(src, code_ref, flat_ref, adv_ref):
    _, planes, ny, nz = adv_ref.shape
    entries = code_ref.shape[0]
    pos, sub, slot, half = unpack(code_ref)
    for j in range(NSUB):
        flat_ref[j * R:(j + 1) * R, :] = src[:, j * TILE:(j + 1) * TILE]
    row_hot = ((sub * R + slot) == lax.broadcasted_iota(jnp.int32, (entries, NSUB * R), 1)).astype(jnp.bfloat16)
    rows = jnp.dot(row_hot, flat_ref[...], preferred_element_type=jnp.float32)
    wide = jnp.concatenate(
        [jnp.where(half == h, rows, 0.0) for h in range(nz // TILE)], axis=1
    ).astype(jnp.bfloat16)
    pick_hot = (pos == lax.broadcasted_iota(jnp.int32, (entries, planes * ny), 1)).astype(jnp.bfloat16)
    forcing = lax.dot_general(pick_hot, wide, (((0,), (0,)), ((), ())), preferred_element_type=jnp.float32)
    adv_ref[0] = adv_ref[0] - force_scale * forcing.reshape(planes, ny, nz)

def step_kernel(rounds, parts_ref, code_ref, st_ref, vel_ref, w_in_ref, decay_ref,
                w_out_hbm, own_ref, adv_ref,
                states_ref, p0, p1, p2, p3, p4, held, sends, recvs, st_sends, st_recvs, xlo, xhi, ylo, yhi, face_sends,
                face_recvs, w_out_ref, new_ref, w_sem, flat_ref, swap_sems, swap_ref):
    here = (lax.axis_index("slab"), lax.axis_index("cross"))
    slab, cross = lax.axis_size("slab"), lax.axis_size("cross")
    planes = vel_ref.shape[1]
    ny = vel_ref.shape[2]
    s, c = here

    def device(axis, other):
        return (other, here[1]) if axis == 0 else (here[0], other)

    extra = s - 1 + 2 * (s % 2)
    barrier = pltpu.get_barrier_semaphore()
    count = 0
    for axis, stride, n in rounds:
        for j in range(1, n):
            pl.semaphore_signal(barrier, inc=1, device_id=device(axis, partner(here[axis], stride, n, j)), device_id_type=MESH)
            count += 1
    pl.semaphore_signal(barrier, inc=1, device_id=((extra + slab) % slab, c), device_id_type=MESH)
    w_copy = pltpu.make_async_copy(w_out_hbm, w_out_ref, w_sem)
    w_copy.start()
    pooled = pool_samples(vel_ref, parts_ref, code_ref)
    for k in range(3):
        p0[:, k * TILE:(k + 1) * TILE] = pooled[k]
    states_ref[pl.ds(s, 1)] = st_ref[...][None]
    pl.semaphore_wait(barrier, count + 1)

    faces = [
        (s > 0, s < slab - 1, vel_ref.at[:, 0], xhi, ((s + slab - 1) % slab, c)),
        (s < slab - 1, s > 0, vel_ref.at[:, planes - 1], xlo, ((s + 1) % slab, c)),
        (c > 0, c < cross - 1, vel_ref.at[:, :, pl.ds(0, 1)], yhi, (s, (c + cross - 1) % cross)),
        (c < cross - 1, c > 0, vel_ref.at[:, :, pl.ds(ny - 1, 1)], ylo, (s, (c + 1) % cross)),
    ]
    face_copies = []
    for k, (send_if, recv_if, src, dst, dev) in enumerate(faces):
        copy = pltpu.make_async_remote_copy(
            src_ref=src, dst_ref=dst, send_sem=face_sends.at[k], recv_sem=face_recvs.at[k],
            device_id=dev, device_id_type=MESH,
        )

        @pl.when(send_if)
        def _():
            copy.start()

        @pl.when(jnp.logical_not(recv_if))
        def _():
            dst[...] = jnp.zeros(dst.shape, dst.dtype)

        face_copies.append((send_if, recv_if, copy))


    chunks = [None, (0, 6), (6, 11), (11, planes)]
    share = R // 2
    mine = pl.ds(pl.multiple_of((s % 2) * share, share), share)
    final = len(rounds)
    bufs = [p0, p1, p2, p3, p4]
    sent = []
    for r, (axis, stride, n) in enumerate(rounds):
        copies = []
        for j in range(1, n):
            dev = device(axis, partner(here[axis], stride, n, j))
            copy = pltpu.make_async_remote_copy(
                src_ref=bufs[0] if r == 0 else bufs[r].at[mine],
                dst_ref=held.at[r, j - 1] if r == 0 else held.at[r, j - 1, pl.ds(0, share)],
                send_sem=sends.at[r, j - 1],
                recv_sem=recvs.at[r, j - 1],
                device_id=dev,
                device_id_type=MESH,
            )
            copy.start()
            copies.append(copy)
            if axis == 0:
                rows = pl.ds(s - s % stride, stride)
                block = pltpu.make_async_remote_copy(
                    src_ref=states_ref.at[rows],
                    dst_ref=states_ref.at[rows],
                    send_sem=st_sends.at[r, j - 1],
                    recv_sem=st_recvs.at[r, j - 1],
                    device_id=dev,
                    device_id_type=MESH,
                )
                block.start()
                copies.append(block)
        if r == 1:
            for send_if, recv_if, face in face_copies:


                @pl.when(recv_if)
                def _():
                    face.wait_recv()
        if chunks[r] is not None:
            first, last = chunks[r]

            def body(x, carry):
                results = stencil_plane(x, planes, vel_ref, xlo, xhi, ylo, yhi)
                for k in range(3):
                    adv_ref[k, x] = results[k]
                return carry

            lax.fori_loop(first, last, body, 0)
        for copy in copies:
            copy.wait_recv()
        sent += copies
        if r == 0:
            bufs[r + 1][mine, :] = bufs[r][mine, :] + held[r, 0, mine, :]
        elif n == 2:
            bufs[r + 1][mine, :] = bufs[r][mine, :] + held[r, 0, pl.ds(0, share)]
        else:
            got = [held[r, k, pl.ds(0, share)] for k in range(3)]
            bufs[r + 1][mine, :] = (bufs[r][mine, :] + got[1]) + (got[0] + got[2])
    swap = pltpu.make_async_remote_copy(
        src_ref=bufs[final].at[mine],
        dst_ref=swap_ref,
        send_sem=swap_sems.at[0],
        recv_sem=swap_sems.at[1],
        device_id=(s + 1 - 2 * (s % 2), c),
        device_id_type=MESH,
    )
    swap.start()
    swap.wait()
    bufs[final][pl.ds(pl.multiple_of((1 - s % 2) * share, share), share), :] = swap_ref[...]

    pooled_b = (bufs[final][...] * pool_scale).astype(jnp.bfloat16)
    drive = jnp.dot(pooled_b, w_in_ref[...], preferred_element_type=jnp.float32)
    decay = decay_ref[...]
    for k in range(states_ref.shape[0]):
        row = states_ref[k]
        new_ref[pl.ds(k, 1), :] = row + state_step * (drive[k:k + 1] - decay * row)
    slot_rows = lax.broadcasted_iota(jnp.int32, drive.shape, 0)
    own_drive = jnp.sum(jnp.where(slot_rows == s, drive, 0.0), axis=0, keepdims=True)
    own = st_ref[...]
    own_ref[...] = own + state_step * (own_drive - decay * own)
    w_copy.wait()
    src = jnp.dot(
        new_ref[...].astype(jnp.bfloat16), w_out_ref[...], preferred_element_type=jnp.float32
    ).astype(jnp.bfloat16)
    place_forcing(src, code_ref, flat_ref, adv_ref)
    for copy in sent:
        copy.wait_send()
    for send_if, recv_if, face in face_copies:

        @pl.when(send_if)
        def _():
            face.wait_send()

def reduce_step(index_parts, rotor_states, velocity, w_in, decay, w_out):
    slab, cross = lax.axis_size("slab"), lax.axis_size("cross")
    rounds = ring_rounds(slab, cross)
    vmem = pl.BlockSpec(memory_space=pltpu.VMEM)
    _, planes, ny, nz = velocity.shape
    return pl.pallas_call(
        lambda *refs: step_kernel(rounds, *refs),
        out_shape=(
            jax.ShapeDtypeStruct(rotor_states.shape, jnp.float32),
            jax.ShapeDtypeStruct(velocity.shape, jnp.float32),
        ),
        in_specs=[vmem] * 6 + [pl.BlockSpec(memory_space=pl.ANY)],
        out_specs=(vmem, vmem),
        scratch_shapes=[
            pltpu.VMEM((slab,) + rotor_states.shape, jnp.float32),
            *[pltpu.VMEM((R, 3 * TILE), jnp.float32) for _ in range(len(rounds) + 1)],
            pltpu.VMEM((len(rounds), 3, R, 3 * TILE), jnp.float32),
            pltpu.SemaphoreType.DMA((len(rounds), 3)),
            pltpu.SemaphoreType.DMA((len(rounds), 3)),
            pltpu.SemaphoreType.DMA((len(rounds), 3)),
            pltpu.SemaphoreType.DMA((len(rounds), 3)),
            pltpu.VMEM((3, ny, nz), jnp.float32),
            pltpu.VMEM((3, ny, nz), jnp.float32),
            pltpu.VMEM((3, planes, 1, nz), jnp.float32),
            pltpu.VMEM((3, planes, 1, nz), jnp.float32),
            pltpu.SemaphoreType.DMA((4,)),
            pltpu.SemaphoreType.DMA((4,)),
            pltpu.VMEM(w_out.shape, w_out.dtype),
            pltpu.VMEM((slab, w_out.shape[0]), jnp.float32),
            pltpu.SemaphoreType.DMA(()),
            pltpu.VMEM((NSUB * R, TILE), jnp.bfloat16),
            pltpu.SemaphoreType.DMA((2,)),
            pltpu.VMEM((R // 2, 3 * TILE), jnp.float32),
        ],
        compiler_params=pltpu.CompilerParams(collective_id=0, has_side_effects=True),
    )(*index_parts, rotor_states, velocity, w_in, decay.reshape(1, -1), w_out)

def stencil_plane(x, planes, vel_ref, xlo_ref, xhi_ref, ylo_ref, yhi_ref):
    _, _, ny, nz = vel_ref.shape
    rows = lax.broadcasted_iota(jnp.int32, (ny, nz), 0)
    lanes = lax.broadcasted_iota(jnp.int32, (ny, nz), 1)
    here = [vel_ref[c, x] for c in range(3)]
    results = []
    for c in range(3):
        u = here[c]
        west = jnp.where(x == 0, xlo_ref[c].astype(jnp.float32), vel_ref[c, jnp.maximum(x - 1, 0)])
        east = jnp.where(x == planes - 1, xhi_ref[c].astype(jnp.float32), vel_ref[c, jnp.minimum(x + 1, planes - 1)])
        south = jnp.where(rows == 0, ylo_ref[c, x].astype(jnp.float32), pltpu.roll(u, 1, 0))
        north = jnp.where(rows == ny - 1, yhi_ref[c, x].astype(jnp.float32), pltpu.roll(u, ny - 1, 0))
        lower = jnp.where(lanes == 0, 0.0, pltpu.roll(u, 1, 1))
        upper = jnp.where(lanes == nz - 1, 0.0, pltpu.roll(u, nz - 1, 1))
        laplace = east + west + north + south + upper + lower - 6.0 * u
        advect = (
            here[0] * ((east - west) * 0.5)
            + here[1] * ((north - south) * 0.5)
            + here[2] * ((upper - lower) * 0.5)
        )
        results.append(u + time_step * (viscosity * laplace - advect))
    return results


def stencil_kernel(vel_ref, xlo_ref, xhi_ref, ylo_ref, yhi_ref, force_ref, out_ref):
    planes = vel_ref.shape[1]

    def body(x, carry):
        results = stencil_plane(x, planes, vel_ref, xlo_ref, xhi_ref, ylo_ref, yhi_ref)
        out_ref[0, x] = results[0] - force_scale * force_ref[x]
        out_ref[1, x] = results[1]
        out_ref[2, x] = results[2]
        return carry

    lax.fori_loop(0, planes, body, 0)


def stencil(velocity, halos, forcing):
    vmem = pl.BlockSpec(memory_space=pltpu.VMEM)
    return pl.pallas_call(
        stencil_kernel,
        out_shape=jax.ShapeDtypeStruct(velocity.shape, velocity.dtype),
        in_specs=[vmem] * 6,
        out_specs=vmem,
    )(velocity, *halos, forcing)


def halo_faces(velocity):
    faces = []
    for axis, dim in (("slab", 1), ("cross", 2)):
        count = lax.axis_size(axis)
        size = velocity.shape[dim]
        head = lax.slice_in_dim(velocity, 0, 1, axis=dim).astype(jnp.bfloat16)
        tail = lax.slice_in_dim(velocity, size - 1, size, axis=dim).astype(jnp.bfloat16)
        low = lax.ppermute(tail, axis, [(i, i + 1) for i in range(count - 1)])
        high = lax.ppermute(head, axis, [(i + 1, i) for i in range(count - 1)])
        faces += [jnp.squeeze(low, dim), jnp.squeeze(high, dim)] if dim == 1 else [low, high]
    return faces


def extended(cells, sides, width):
    for axis, dim in sides:
        count = lax.axis_size(axis)
        ends = count - 1
        head = lax.slice_in_dim(cells, 0, width, axis=dim)
        tail = lax.slice_in_dim(cells, cells.shape[dim] - width, cells.shape[dim], axis=dim)
        cells = jnp.concatenate(
            [
                lax.ppermute(tail, axis, [(i, (i + 1) % count) for i in range(ends)]),
                cells,
                lax.ppermute(head, axis, [((i + 1) % count, i) for i in range(ends)]),
            ],
            axis=dim,
        )
    return cells


def combine_terms(velocity, east, west, north, south, upper, lower):
    laplace = east + west + north + south + upper + lower - 6.0 * velocity
    advect = (
        velocity[0:1] * ((east - west) * 0.5)
        + velocity[1:2] * ((north - south) * 0.5)
        + velocity[2:3] * ((upper - lower) * 0.5)
    )
    return velocity + time_step * (viscosity * laplace - advect)


def on_device(
    velocity,
    shape_weight,
    w_in,
    w_out,
    decay,
    rotor_states,
    slot_of_rotor,
    entry_rotor,
    entry_tile,
    entry_sub,
):
    local_x, local_y, local_z = (velocity.shape[1], velocity.shape[2], velocity.shape[3])
    tile_count = local_x * local_y * local_z // TILE
    rotor_hot = (entry_rotor == jnp.arange(R, dtype=jnp.int32)[None, :]).astype(jnp.int32)
    slots = jnp.sum(rotor_hot * slot_of_rotor[None, :], axis=1)
    high = lax.reduce_precision(shape_weight, exponent_bits=8, mantissa_bits=7)
    rest = shape_weight - high
    middle = lax.reduce_precision(rest, exponent_bits=8, mantissa_bits=7)
    low = rest - middle
    parts = jnp.stack([high, middle, low]).astype(jnp.bfloat16)
    halves = local_z // TILE
    code = (((entry_tile // halves) * NSUB + entry_sub) * R + slots) * halves + entry_tile % halves
    new_states, advanced = reduce_step((parts, code[:, None]), rotor_states, velocity, w_in, decay, w_out)
    return (advanced, new_states)


def solution(mesh):
    in_specs = (
        P(None, "slab", "cross", None),
        P(),
        P(),
        P(),
        P(),
        P("slab", None),
        P(),
        P(("slab", "cross"), None),
        P(("slab", "cross")),
        P(("slab", "cross")),
    )
    out_specs = (P(None, "slab", "cross", None), P("slab", None))
    return jax.shard_map(
        on_device, mesh=mesh, in_specs=in_specs, out_specs=out_specs, check_vma=False
    )
```

```python
import jax
import jax.numpy as jnp
from jax import lax
from jax.experimental import pallas as pl
from jax.experimental.pallas import tpu as pltpu
from jax.sharding import PartitionSpec as P

MESH = pl.DeviceIdType.MESH

TILE = 128
R = 32
NSUB = 32


time_step = 0.1
viscosity = 0.3
pool_scale = 1.0 / 64.0
state_step = 0.5
force_scale = 0.5


def ring_perm(size, stride, n, shift):
    pairs = []
    for s in range(size):
        base = (s // (stride * n)) * stride * n + s % stride
        pos = (s // stride) % n
        pairs.append((s, base + ((pos + shift) % n) * stride))
    return pairs


def ring_sum(value, axis, stride, n):
    size = lax.axis_size(axis)
    if n == 2:
        return value + lax.ppermute(value, axis, ring_perm(size, stride, n, 1))
    got = [lax.ppermute(value, axis, ring_perm(size, stride, n, j)) for j in (1, 2, 3)]
    return (value + got[1]) + (got[0] + got[2])


def ring_gather(value, axis, stride, n):
    size = lax.axis_size(axis)
    pos = (lax.axis_index(axis) // stride) % n
    got = [value] + [lax.ppermute(value, axis, ring_perm(size, stride, n, j)) for j in range(1, n)]
    parts = []
    for p in range(n):
        pick = got[0]
        for j in range(1, n):
            pick = jnp.where((pos - j) % n == p, got[j], pick)
        parts.append(jnp.where(pos == p, got[0], pick))
    return jnp.concatenate(parts, axis=0)


def mesh_rings():
    slab = lax.axis_size("slab")
    rings = [("slab", 1, 2), ("slab", 2, 4), ("slab", 8, slab // 8)]
    return rings


def all_sum(value):
    for axis, stride, n in mesh_rings() + [("cross", 1, lax.axis_size("cross"))]:
        value = ring_sum(value, axis, stride, n)
    return value


def slab_gather(value):
    parts = value
    for axis, stride, n in mesh_rings():
        parts = ring_gather(parts, axis, stride, n)
    return parts


def ring_rounds(slab, cross):
    return [(0, 1, 2), (0, 2, 4), (0, 8, slab // 8), (1, 1, cross)]


def partner(me, stride, n, shift):
    pos = (me // stride) % n
    return me - pos * stride + ((pos + shift) % n) * stride


def unpack(code_ref):
    code = code_ref[...]
    half = code % 2
    slot = (code // 2) % R
    sub = (code // (2 * R)) % NSUB
    pos = code // (2 * R * NSUB)
    return pos, sub, slot, half


def pool_samples(vel_ref, parts_ref, code_ref):
    _, planes, ny, nz = vel_ref.shape
    entries = code_ref.shape[0]
    cells_xy = planes * ny
    pos, sub, slot, half = unpack(code_ref)
    sub_hot = (sub == lax.broadcasted_iota(jnp.int32, (entries, parts_ref.shape[1]), 1)).astype(jnp.bfloat16)
    gains = [jnp.dot(sub_hot, parts_ref[k], preferred_element_type=jnp.float32) for k in range(3)]
    gains = (gains[0] + gains[1]) + gains[2]
    pick_hot = (pos == lax.broadcasted_iota(jnp.int32, (entries, cells_xy), 1)).astype(jnp.bfloat16)
    slot_hot = (slot == lax.broadcasted_iota(jnp.int32, (entries, R), 1)).astype(jnp.float32)
    pooled = []
    for c in range(3):
        cells = vel_ref[c].reshape(cells_xy, nz).astype(jnp.bfloat16)
        both = jnp.dot(pick_hot, cells, preferred_element_type=jnp.float32)
        picked = both[:, :TILE]
        for h in range(1, nz // TILE):
            picked = jnp.where(half == h, both[:, h * TILE:(h + 1) * TILE], picked)
        weighted = gains[:, c * TILE:(c + 1) * TILE] * picked
        pooled.append(
            lax.dot_general(
                slot_hot, weighted, (((0,), (0,)), ((), ())),
                precision=lax.Precision.HIGHEST, preferred_element_type=jnp.float32,
            )
        )
    return pooled


def place_forcing(src, code_ref, flat_ref, adv_ref):
    _, planes, ny, nz = adv_ref.shape
    entries = code_ref.shape[0]
    pos, sub, slot, half = unpack(code_ref)
    for j in range(NSUB):
        flat_ref[j * R:(j + 1) * R, :] = src[:, j * TILE:(j + 1) * TILE]
    row_hot = ((sub * R + slot) == lax.broadcasted_iota(jnp.int32, (entries, NSUB * R), 1)).astype(jnp.bfloat16)
    rows = jnp.dot(row_hot, flat_ref[...], preferred_element_type=jnp.float32)
    wide = jnp.concatenate(
        [jnp.where(half == h, rows, 0.0) for h in range(nz // TILE)], axis=1
    ).astype(jnp.bfloat16)
    pick_hot = (pos == lax.broadcasted_iota(jnp.int32, (entries, planes * ny), 1)).astype(jnp.bfloat16)
    forcing = lax.dot_general(pick_hot, wide, (((0,), (0,)), ((), ())), preferred_element_type=jnp.float32)
    adv_ref[0] = adv_ref[0] - force_scale * forcing.reshape(planes, ny, nz)

def step_kernel(rounds, parts_ref, code_ref, st_ref, vel_ref, w_in_ref, decay_ref,
                w_out_hbm, own_ref, adv_hbm,
                states_ref, p0, p1, p2, p3, p4, held, sends, recvs, st_sends, st_recvs, xlo, xhi, ylo, yhi, face_sends,
                face_recvs, w_out_ref, new_ref, w_sem, flat_ref, swap_sems, swap_ref, adv_ref, adv_sems):
    here = (lax.axis_index("slab"), lax.axis_index("cross"))
    slab, cross = lax.axis_size("slab"), lax.axis_size("cross")
    planes = vel_ref.shape[1]
    ny = vel_ref.shape[2]
    s, c = here

    def device(axis, other):
        return (other, here[1]) if axis == 0 else (here[0], other)

    extra = s - 1 + 2 * (s % 2)
    barrier = pltpu.get_barrier_semaphore()
    count = 0
    for axis, stride, n in rounds:
        for j in range(1, n):
            pl.semaphore_signal(barrier, inc=1, device_id=device(axis, partner(here[axis], stride, n, j)), device_id_type=MESH)
            count += 1
    pl.semaphore_signal(barrier, inc=1, device_id=((extra + slab) % slab, c), device_id_type=MESH)
    w_copy = pltpu.make_async_copy(w_out_hbm, w_out_ref, w_sem)
    w_copy.start()
    pooled = pool_samples(vel_ref, parts_ref, code_ref)
    for k in range(3):
        p0[:, k * TILE:(k + 1) * TILE] = pooled[k]
    states_ref[pl.ds(s, 1)] = st_ref[...][None]
    pl.semaphore_wait(barrier, count + 1)

    faces = [
        (s > 0, s < slab - 1, vel_ref.at[:, 0], xhi, ((s + slab - 1) % slab, c)),
        (s < slab - 1, s > 0, vel_ref.at[:, planes - 1], xlo, ((s + 1) % slab, c)),
        (c > 0, c < cross - 1, vel_ref.at[:, :, pl.ds(0, 1)], yhi, (s, (c + cross - 1) % cross)),
        (c < cross - 1, c > 0, vel_ref.at[:, :, pl.ds(ny - 1, 1)], ylo, (s, (c + 1) % cross)),
    ]
    face_copies = []
    for k, (send_if, recv_if, src, dst, dev) in enumerate(faces):
        copy = pltpu.make_async_remote_copy(
            src_ref=src, dst_ref=dst, send_sem=face_sends.at[k], recv_sem=face_recvs.at[k],
            device_id=dev, device_id_type=MESH,
        )

        @pl.when(send_if)
        def _():
            copy.start()

        @pl.when(jnp.logical_not(recv_if))
        def _():
            dst[...] = jnp.zeros(dst.shape, dst.dtype)

        face_copies.append((send_if, recv_if, copy))


    chunks = [None, (0, 6), (6, 11), (11, planes)]
    share = R // 2
    mine = pl.ds(pl.multiple_of((s % 2) * share, share), share)
    final = len(rounds)
    bufs = [p0, p1, p2, p3, p4]
    outs = []
    sent = []
    for r, (axis, stride, n) in enumerate(rounds):
        copies = []
        for j in range(1, n):
            dev = device(axis, partner(here[axis], stride, n, j))
            copy = pltpu.make_async_remote_copy(
                src_ref=bufs[0] if r == 0 else bufs[r].at[mine],
                dst_ref=held.at[r, j - 1] if r == 0 else held.at[r, j - 1, pl.ds(0, share)],
                send_sem=sends.at[r, j - 1],
                recv_sem=recvs.at[r, j - 1],
                device_id=dev,
                device_id_type=MESH,
            )
            copy.start()
            copies.append(copy)
            if axis == 0:
                rows = pl.ds(s - s % stride, stride)
                block = pltpu.make_async_remote_copy(
                    src_ref=states_ref.at[rows],
                    dst_ref=states_ref.at[rows],
                    send_sem=st_sends.at[r, j - 1],
                    recv_sem=st_recvs.at[r, j - 1],
                    device_id=dev,
                    device_id_type=MESH,
                )
                block.start()
                copies.append(block)
        if r == 1:
            for send_if, recv_if, face in face_copies:


                @pl.when(recv_if)
                def _():
                    face.wait_recv()
        if chunks[r] is not None:
            first, last = chunks[r]

            def body(x, carry):
                results = stencil_plane(x, planes, vel_ref, xlo, xhi, ylo, yhi)
                for k in range(3):
                    adv_ref[k, x] = results[k]
                return carry

            lax.fori_loop(first, last, body, 0)
            out = pltpu.make_async_copy(
                adv_ref.at[pl.ds(1, 2), pl.ds(first, last - first)],
                adv_hbm.at[pl.ds(1, 2), pl.ds(first, last - first)],
                adv_sems.at[r - 1],
            )
            out.start()
            outs.append(out)
        for copy in copies:
            copy.wait_recv()
        sent += copies
        if r == 0:
            bufs[r + 1][mine, :] = bufs[r][mine, :] + held[r, 0, mine, :]
        elif n == 2:
            bufs[r + 1][mine, :] = bufs[r][mine, :] + held[r, 0, pl.ds(0, share)]
        else:
            got = [held[r, k, pl.ds(0, share)] for k in range(3)]
            bufs[r + 1][mine, :] = (bufs[r][mine, :] + got[1]) + (got[0] + got[2])
    swap = pltpu.make_async_remote_copy(
        src_ref=bufs[final].at[mine],
        dst_ref=swap_ref,
        send_sem=swap_sems.at[0],
        recv_sem=swap_sems.at[1],
        device_id=(s + 1 - 2 * (s % 2), c),
        device_id_type=MESH,
    )
    swap.start()
    swap.wait()
    bufs[final][pl.ds(pl.multiple_of((1 - s % 2) * share, share), share), :] = swap_ref[...]

    pooled_b = (bufs[final][...] * pool_scale).astype(jnp.bfloat16)
    drive = jnp.dot(pooled_b, w_in_ref[...], preferred_element_type=jnp.float32)
    decay = decay_ref[...]
    for k in range(states_ref.shape[0]):
        row = states_ref[k]
        new_ref[pl.ds(k, 1), :] = row + state_step * (drive[k:k + 1] - decay * row)
    slot_rows = lax.broadcasted_iota(jnp.int32, drive.shape, 0)
    own_drive = jnp.sum(jnp.where(slot_rows == s, drive, 0.0), axis=0, keepdims=True)
    own = st_ref[...]
    own_ref[...] = own + state_step * (own_drive - decay * own)
    w_copy.wait()
    src = jnp.dot(
        new_ref[...].astype(jnp.bfloat16), w_out_ref[...], preferred_element_type=jnp.float32
    ).astype(jnp.bfloat16)
    place_forcing(src, code_ref, flat_ref, adv_ref)
    out = pltpu.make_async_copy(adv_ref.at[0], adv_hbm.at[0], adv_sems.at[len(rounds) - 1])
    out.start()
    outs.append(out)
    for out in outs:
        out.wait()
    for copy in sent:
        copy.wait_send()
    for send_if, recv_if, face in face_copies:

        @pl.when(send_if)
        def _():
            face.wait_send()

def reduce_step(index_parts, rotor_states, velocity, w_in, decay, w_out):
    slab, cross = lax.axis_size("slab"), lax.axis_size("cross")
    rounds = ring_rounds(slab, cross)
    vmem = pl.BlockSpec(memory_space=pltpu.VMEM)
    _, planes, ny, nz = velocity.shape
    return pl.pallas_call(
        lambda *refs: step_kernel(rounds, *refs),
        out_shape=(
            jax.ShapeDtypeStruct(rotor_states.shape, jnp.float32),
            jax.ShapeDtypeStruct(velocity.shape, jnp.float32),
        ),
        in_specs=[vmem] * 6 + [pl.BlockSpec(memory_space=pl.ANY)],
        out_specs=(vmem, pl.BlockSpec(memory_space=pl.ANY)),
        scratch_shapes=[
            pltpu.VMEM((slab,) + rotor_states.shape, jnp.float32),
            *[pltpu.VMEM((R, 3 * TILE), jnp.float32) for _ in range(len(rounds) + 1)],
            pltpu.VMEM((len(rounds), 3, R, 3 * TILE), jnp.float32),
            pltpu.SemaphoreType.DMA((len(rounds), 3)),
            pltpu.SemaphoreType.DMA((len(rounds), 3)),
            pltpu.SemaphoreType.DMA((len(rounds), 3)),
            pltpu.SemaphoreType.DMA((len(rounds), 3)),
            pltpu.VMEM((3, ny, nz), jnp.float32),
            pltpu.VMEM((3, ny, nz), jnp.float32),
            pltpu.VMEM((3, planes, 1, nz), jnp.float32),
            pltpu.VMEM((3, planes, 1, nz), jnp.float32),
            pltpu.SemaphoreType.DMA((4,)),
            pltpu.SemaphoreType.DMA((4,)),
            pltpu.VMEM(w_out.shape, w_out.dtype),
            pltpu.VMEM((slab, w_out.shape[0]), jnp.float32),
            pltpu.SemaphoreType.DMA(()),
            pltpu.VMEM((NSUB * R, TILE), jnp.bfloat16),
            pltpu.SemaphoreType.DMA((2,)),
            pltpu.VMEM((R // 2, 3 * TILE), jnp.float32),
            pltpu.VMEM(velocity.shape, jnp.float32),
            pltpu.SemaphoreType.DMA((len(rounds),)),
        ],
        compiler_params=pltpu.CompilerParams(collective_id=0, has_side_effects=True),
    )(*index_parts, rotor_states, velocity, w_in, decay.reshape(1, -1), w_out)

def stencil_plane(x, planes, vel_ref, xlo_ref, xhi_ref, ylo_ref, yhi_ref):
    _, _, ny, nz = vel_ref.shape
    rows = lax.broadcasted_iota(jnp.int32, (ny, nz), 0)
    lanes = lax.broadcasted_iota(jnp.int32, (ny, nz), 1)
    here = [vel_ref[c, x] for c in range(3)]
    results = []
    for c in range(3):
        u = here[c]
        west = jnp.where(x == 0, xlo_ref[c].astype(jnp.float32), vel_ref[c, jnp.maximum(x - 1, 0)])
        east = jnp.where(x == planes - 1, xhi_ref[c].astype(jnp.float32), vel_ref[c, jnp.minimum(x + 1, planes - 1)])
        south = jnp.where(rows == 0, ylo_ref[c, x].astype(jnp.float32), pltpu.roll(u, 1, 0))
        north = jnp.where(rows == ny - 1, yhi_ref[c, x].astype(jnp.float32), pltpu.roll(u, ny - 1, 0))
        lower = jnp.where(lanes == 0, 0.0, pltpu.roll(u, 1, 1))
        upper = jnp.where(lanes == nz - 1, 0.0, pltpu.roll(u, nz - 1, 1))
        laplace = east + west + north + south + upper + lower - 6.0 * u
        advect = (
            here[0] * ((east - west) * 0.5)
            + here[1] * ((north - south) * 0.5)
            + here[2] * ((upper - lower) * 0.5)
        )
        results.append(u + time_step * (viscosity * laplace - advect))
    return results


def stencil_kernel(vel_ref, xlo_ref, xhi_ref, ylo_ref, yhi_ref, force_ref, out_ref):
    planes = vel_ref.shape[1]

    def body(x, carry):
        results = stencil_plane(x, planes, vel_ref, xlo_ref, xhi_ref, ylo_ref, yhi_ref)
        out_ref[0, x] = results[0] - force_scale * force_ref[x]
        out_ref[1, x] = results[1]
        out_ref[2, x] = results[2]
        return carry

    lax.fori_loop(0, planes, body, 0)


def stencil(velocity, halos, forcing):
    vmem = pl.BlockSpec(memory_space=pltpu.VMEM)
    return pl.pallas_call(
        stencil_kernel,
        out_shape=jax.ShapeDtypeStruct(velocity.shape, velocity.dtype),
        in_specs=[vmem] * 6,
        out_specs=vmem,
    )(velocity, *halos, forcing)


def halo_faces(velocity):
    faces = []
    for axis, dim in (("slab", 1), ("cross", 2)):
        count = lax.axis_size(axis)
        size = velocity.shape[dim]
        head = lax.slice_in_dim(velocity, 0, 1, axis=dim).astype(jnp.bfloat16)
        tail = lax.slice_in_dim(velocity, size - 1, size, axis=dim).astype(jnp.bfloat16)
        low = lax.ppermute(tail, axis, [(i, i + 1) for i in range(count - 1)])
        high = lax.ppermute(head, axis, [(i + 1, i) for i in range(count - 1)])
        faces += [jnp.squeeze(low, dim), jnp.squeeze(high, dim)] if dim == 1 else [low, high]
    return faces


def extended(cells, sides, width):
    for axis, dim in sides:
        count = lax.axis_size(axis)
        ends = count - 1
        head = lax.slice_in_dim(cells, 0, width, axis=dim)
        tail = lax.slice_in_dim(cells, cells.shape[dim] - width, cells.shape[dim], axis=dim)
        cells = jnp.concatenate(
            [
                lax.ppermute(tail, axis, [(i, (i + 1) % count) for i in range(ends)]),
                cells,
                lax.ppermute(head, axis, [((i + 1) % count, i) for i in range(ends)]),
            ],
            axis=dim,
        )
    return cells


def combine_terms(velocity, east, west, north, south, upper, lower):
    laplace = east + west + north + south + upper + lower - 6.0 * velocity
    advect = (
        velocity[0:1] * ((east - west) * 0.5)
        + velocity[1:2] * ((north - south) * 0.5)
        + velocity[2:3] * ((upper - lower) * 0.5)
    )
    return velocity + time_step * (viscosity * laplace - advect)


def on_device(
    velocity,
    shape_weight,
    w_in,
    w_out,
    decay,
    rotor_states,
    slot_of_rotor,
    entry_rotor,
    entry_tile,
    entry_sub,
):
    local_x, local_y, local_z = (velocity.shape[1], velocity.shape[2], velocity.shape[3])
    tile_count = local_x * local_y * local_z // TILE
    rotor_hot = (entry_rotor == jnp.arange(R, dtype=jnp.int32)[None, :]).astype(jnp.int32)
    slots = jnp.sum(rotor_hot * slot_of_rotor[None, :], axis=1)
    high = lax.reduce_precision(shape_weight, exponent_bits=8, mantissa_bits=7)
    rest = shape_weight - high
    middle = lax.reduce_precision(rest, exponent_bits=8, mantissa_bits=7)
    low = rest - middle
    parts = jnp.stack([high, middle, low]).astype(jnp.bfloat16)
    halves = local_z // TILE
    code = (((entry_tile // halves) * NSUB + entry_sub) * R + slots) * halves + entry_tile % halves
    new_states, advanced = reduce_step((parts, code[:, None]), rotor_states, velocity, w_in, decay, w_out)
    return (advanced, new_states)


def solution(mesh):
    in_specs = (
        P(None, "slab", "cross", None),
        P(),
        P(),
        P(),
        P(),
        P("slab", None),
        P(),
        P(("slab", "cross"), None),
        P(("slab", "cross")),
        P(("slab", "cross")),
    )
    out_specs = (P(None, "slab", "cross", None), P("slab", None))
    return jax.shard_map(
        on_device, mesh=mesh, in_specs=in_specs, out_specs=out_specs, check_vma=False
    )
```

```python
import jax
import jax.numpy as jnp
from jax import lax
from jax.experimental import pallas as pl
from jax.experimental.pallas import tpu as pltpu
from jax.sharding import PartitionSpec as P

MESH = pl.DeviceIdType.MESH

TILE = 128
R = 32
NSUB = 32


time_step = 0.1
viscosity = 0.3
pool_scale = 1.0 / 64.0
state_step = 0.5
force_scale = 0.5


def ring_perm(size, stride, n, shift):
    pairs = []
    for s in range(size):
        base = (s // (stride * n)) * stride * n + s % stride
        pos = (s // stride) % n
        pairs.append((s, base + ((pos + shift) % n) * stride))
    return pairs


def ring_sum(value, axis, stride, n):
    size = lax.axis_size(axis)
    if n == 2:
        return value + lax.ppermute(value, axis, ring_perm(size, stride, n, 1))
    got = [lax.ppermute(value, axis, ring_perm(size, stride, n, j)) for j in (1, 2, 3)]
    return (value + got[1]) + (got[0] + got[2])


def ring_gather(value, axis, stride, n):
    size = lax.axis_size(axis)
    pos = (lax.axis_index(axis) // stride) % n
    got = [value] + [lax.ppermute(value, axis, ring_perm(size, stride, n, j)) for j in range(1, n)]
    parts = []
    for p in range(n):
        pick = got[0]
        for j in range(1, n):
            pick = jnp.where((pos - j) % n == p, got[j], pick)
        parts.append(jnp.where(pos == p, got[0], pick))
    return jnp.concatenate(parts, axis=0)


def mesh_rings():
    slab = lax.axis_size("slab")
    rings = [("slab", 1, 2), ("slab", 2, 4), ("slab", 8, slab // 8)]
    return rings


def all_sum(value):
    for axis, stride, n in mesh_rings() + [("cross", 1, lax.axis_size("cross"))]:
        value = ring_sum(value, axis, stride, n)
    return value


def slab_gather(value):
    parts = value
    for axis, stride, n in mesh_rings():
        parts = ring_gather(parts, axis, stride, n)
    return parts


def ring_rounds(slab, cross):
    return [(0, 1, 2), (0, 2, 4), (0, 8, slab // 8), (1, 1, cross)]


def partner(me, stride, n, shift):
    pos = (me // stride) % n
    return me - pos * stride + ((pos + shift) % n) * stride


def unpack(code_ref):
    code = code_ref[...]
    half = code % 2
    slot = (code // 2) % R
    sub = (code // (2 * R)) % NSUB
    pos = code // (2 * R * NSUB)
    return pos, sub, slot, half


def pool_samples(vel_ref, parts_ref, code_ref):
    _, planes, ny, nz = vel_ref.shape
    entries = code_ref.shape[0]
    cells_xy = planes * ny
    pos, sub, slot, half = unpack(code_ref)
    sub_hot = (sub == lax.broadcasted_iota(jnp.int32, (entries, parts_ref.shape[1]), 1)).astype(jnp.bfloat16)
    gains = [jnp.dot(sub_hot, parts_ref[k], preferred_element_type=jnp.float32) for k in range(3)]
    gains = (gains[0] + gains[1]) + gains[2]
    pick_hot = (pos == lax.broadcasted_iota(jnp.int32, (entries, cells_xy), 1)).astype(jnp.bfloat16)
    slot_hot = (slot == lax.broadcasted_iota(jnp.int32, (entries, R), 1)).astype(jnp.float32)
    pooled = []
    for c in range(3):
        cells = vel_ref[c].reshape(cells_xy, nz).astype(jnp.bfloat16)
        both = jnp.dot(pick_hot, cells, preferred_element_type=jnp.float32)
        picked = both[:, :TILE]
        for h in range(1, nz // TILE):
            picked = jnp.where(half == h, both[:, h * TILE:(h + 1) * TILE], picked)
        weighted = gains[:, c * TILE:(c + 1) * TILE] * picked
        pooled.append(
            lax.dot_general(
                slot_hot, weighted, (((0,), (0,)), ((), ())),
                precision=lax.Precision.HIGHEST, preferred_element_type=jnp.float32,
            )
        )
    return pooled


def place_forcing(src, code_ref, flat_ref, adv_ref, row_hot_ref, pick_ref):
    _, planes, ny, nz = adv_ref.shape
    pos, sub, slot, half = unpack(code_ref)
    for j in range(NSUB):
        flat_ref[j * R:(j + 1) * R, :] = src[:, j * TILE:(j + 1) * TILE]
    rows = jnp.dot(row_hot_ref[...], flat_ref[...], preferred_element_type=jnp.float32)
    wide = jnp.concatenate(
        [jnp.where(half == h, rows, 0.0) for h in range(nz // TILE)], axis=1
    ).astype(jnp.bfloat16)
    pick_hot = pick_ref[...]
    forcing = lax.dot_general(pick_hot, wide, (((0,), (0,)), ((), ())), preferred_element_type=jnp.float32)
    adv_ref[0] = adv_ref[0] - force_scale * forcing.reshape(planes, ny, nz)

def step_kernel(rounds, parts_ref, code_ref, st_ref, vel_ref, w_in_ref, decay_ref,
                w_out_hbm, own_ref, adv_hbm,
                states_ref, p0, p1, p2, p3, p4, held, sends, recvs, st_sends, st_recvs, xlo, xhi, ylo, yhi, face_sends,
                face_recvs, w_out_ref, new_ref, w_sem, flat_ref, swap_sems, swap_ref, adv_ref, adv_sems, row_hot_ref, pick_ref):
    here = (lax.axis_index("slab"), lax.axis_index("cross"))
    slab, cross = lax.axis_size("slab"), lax.axis_size("cross")
    planes = vel_ref.shape[1]
    ny = vel_ref.shape[2]
    s, c = here

    def device(axis, other):
        return (other, here[1]) if axis == 0 else (here[0], other)

    extra = s - 1 + 2 * (s % 2)
    barrier = pltpu.get_barrier_semaphore()
    count = 0
    for axis, stride, n in rounds:
        for j in range(1, n):
            pl.semaphore_signal(barrier, inc=1, device_id=device(axis, partner(here[axis], stride, n, j)), device_id_type=MESH)
            count += 1
    pl.semaphore_signal(barrier, inc=1, device_id=((extra + slab) % slab, c), device_id_type=MESH)
    w_copy = pltpu.make_async_copy(w_out_hbm, w_out_ref, w_sem)
    w_copy.start()
    pooled = pool_samples(vel_ref, parts_ref, code_ref)
    for k in range(3):
        p0[:, k * TILE:(k + 1) * TILE] = pooled[k]
    states_ref[pl.ds(s, 1)] = st_ref[...][None]
    pl.semaphore_wait(barrier, count + 1)

    faces = [
        (s > 0, s < slab - 1, vel_ref.at[:, 0], xhi, ((s + slab - 1) % slab, c)),
        (s < slab - 1, s > 0, vel_ref.at[:, planes - 1], xlo, ((s + 1) % slab, c)),
        (c > 0, c < cross - 1, vel_ref.at[:, :, pl.ds(0, 1)], yhi, (s, (c + cross - 1) % cross)),
        (c < cross - 1, c > 0, vel_ref.at[:, :, pl.ds(ny - 1, 1)], ylo, (s, (c + 1) % cross)),
    ]
    face_copies = []
    for k, (send_if, recv_if, src, dst, dev) in enumerate(faces):
        copy = pltpu.make_async_remote_copy(
            src_ref=src, dst_ref=dst, send_sem=face_sends.at[k], recv_sem=face_recvs.at[k],
            device_id=dev, device_id_type=MESH,
        )

        @pl.when(send_if)
        def _():
            copy.start()

        @pl.when(jnp.logical_not(recv_if))
        def _():
            dst[...] = jnp.zeros(dst.shape, dst.dtype)

        face_copies.append((send_if, recv_if, copy))


    chunks = [None, (0, 6), (6, 11), (11, planes)]
    share = R // 2
    mine = pl.ds(pl.multiple_of((s % 2) * share, share), share)
    final = len(rounds)
    bufs = [p0, p1, p2, p3, p4]
    outs = []
    sent = []
    for r, (axis, stride, n) in enumerate(rounds):
        copies = []
        for j in range(1, n):
            dev = device(axis, partner(here[axis], stride, n, j))
            copy = pltpu.make_async_remote_copy(
                src_ref=bufs[0] if r == 0 else bufs[r].at[mine],
                dst_ref=held.at[r, j - 1] if r == 0 else held.at[r, j - 1, pl.ds(0, share)],
                send_sem=sends.at[r, j - 1],
                recv_sem=recvs.at[r, j - 1],
                device_id=dev,
                device_id_type=MESH,
            )
            copy.start()
            copies.append(copy)
            if axis == 0:
                rows = pl.ds(s - s % stride, stride)
                block = pltpu.make_async_remote_copy(
                    src_ref=states_ref.at[rows],
                    dst_ref=states_ref.at[rows],
                    send_sem=st_sends.at[r, j - 1],
                    recv_sem=st_recvs.at[r, j - 1],
                    device_id=dev,
                    device_id_type=MESH,
                )
                block.start()
                copies.append(block)
        if r == 1:
            for send_if, recv_if, face in face_copies:


                @pl.when(recv_if)
                def _():
                    face.wait_recv()
        if chunks[r] is not None:
            first, last = chunks[r]

            def body(x, carry):
                results = stencil_plane(x, planes, vel_ref, xlo, xhi, ylo, yhi)
                for k in range(3):
                    adv_ref[k, x] = results[k]
                return carry

            lax.fori_loop(first, last, body, 0)
            out = pltpu.make_async_copy(
                adv_ref.at[pl.ds(1, 2), pl.ds(first, last - first)],
                adv_hbm.at[pl.ds(1, 2), pl.ds(first, last - first)],
                adv_sems.at[r - 1],
            )
            out.start()
            outs.append(out)
            if r == len(rounds) - 1:
                pos, sub, slot, half = unpack(code_ref)
                entries = code_ref.shape[0]
                row_hot_ref[...] = (
                    (sub * R + slot) == lax.broadcasted_iota(jnp.int32, (entries, NSUB * R), 1)
                ).astype(jnp.bfloat16)
                pick_ref[...] = (pos == lax.broadcasted_iota(jnp.int32, (entries, planes * ny), 1)).astype(jnp.bfloat16)
        for copy in copies:
            copy.wait_recv()
        sent += copies
        if r == 0:
            bufs[r + 1][mine, :] = bufs[r][mine, :] + held[r, 0, mine, :]
        elif n == 2:
            bufs[r + 1][mine, :] = bufs[r][mine, :] + held[r, 0, pl.ds(0, share)]
        else:
            got = [held[r, k, pl.ds(0, share)] for k in range(3)]
            bufs[r + 1][mine, :] = (bufs[r][mine, :] + got[1]) + (got[0] + got[2])
    swap = pltpu.make_async_remote_copy(
        src_ref=bufs[final].at[mine],
        dst_ref=swap_ref,
        send_sem=swap_sems.at[0],
        recv_sem=swap_sems.at[1],
        device_id=(s + 1 - 2 * (s % 2), c),
        device_id_type=MESH,
    )
    swap.start()
    swap.wait()
    bufs[final][pl.ds(pl.multiple_of((1 - s % 2) * share, share), share), :] = swap_ref[...]

    pooled_b = (bufs[final][...] * pool_scale).astype(jnp.bfloat16)
    drive = jnp.dot(pooled_b, w_in_ref[...], preferred_element_type=jnp.float32)
    decay = decay_ref[...]
    for k in range(states_ref.shape[0]):
        row = states_ref[k]
        new_ref[pl.ds(k, 1), :] = row + state_step * (drive[k:k + 1] - decay * row)
    slot_rows = lax.broadcasted_iota(jnp.int32, drive.shape, 0)
    own_drive = jnp.sum(jnp.where(slot_rows == s, drive, 0.0), axis=0, keepdims=True)
    own = st_ref[...]
    own_ref[...] = own + state_step * (own_drive - decay * own)
    w_copy.wait()
    src = jnp.dot(
        new_ref[...].astype(jnp.bfloat16), w_out_ref[...], preferred_element_type=jnp.float32
    ).astype(jnp.bfloat16)
    place_forcing(src, code_ref, flat_ref, adv_ref, row_hot_ref, pick_ref)
    out = pltpu.make_async_copy(adv_ref.at[0], adv_hbm.at[0], adv_sems.at[len(rounds) - 1])
    out.start()
    outs.append(out)
    for out in outs:
        out.wait()
    for copy in sent:
        copy.wait_send()
    for send_if, recv_if, face in face_copies:

        @pl.when(send_if)
        def _():
            face.wait_send()

def reduce_step(code_parts, rotor_states, velocity, w_in, decay, w_out):
    slab, cross = lax.axis_size("slab"), lax.axis_size("cross")
    rounds = ring_rounds(slab, cross)
    vmem = pl.BlockSpec(memory_space=pltpu.VMEM)
    _, planes, ny, nz = velocity.shape
    return pl.pallas_call(
        lambda *refs: step_kernel(rounds, *refs),
        out_shape=(
            jax.ShapeDtypeStruct(rotor_states.shape, jnp.float32),
            jax.ShapeDtypeStruct(velocity.shape, jnp.float32),
        ),
        in_specs=[vmem] * 6 + [pl.BlockSpec(memory_space=pl.ANY)],
        out_specs=(vmem, pl.BlockSpec(memory_space=pl.ANY)),
        scratch_shapes=[
            pltpu.VMEM((slab,) + rotor_states.shape, jnp.float32),
            *[pltpu.VMEM((R, 3 * TILE), jnp.float32) for _ in range(len(rounds) + 1)],
            pltpu.VMEM((len(rounds), 3, R, 3 * TILE), jnp.float32),
            pltpu.SemaphoreType.DMA((len(rounds), 3)),
            pltpu.SemaphoreType.DMA((len(rounds), 3)),
            pltpu.SemaphoreType.DMA((len(rounds), 3)),
            pltpu.SemaphoreType.DMA((len(rounds), 3)),
            pltpu.VMEM((3, ny, nz), jnp.float32),
            pltpu.VMEM((3, ny, nz), jnp.float32),
            pltpu.VMEM((3, planes, 1, nz), jnp.float32),
            pltpu.VMEM((3, planes, 1, nz), jnp.float32),
            pltpu.SemaphoreType.DMA((4,)),
            pltpu.SemaphoreType.DMA((4,)),
            pltpu.VMEM(w_out.shape, w_out.dtype),
            pltpu.VMEM((slab, w_out.shape[0]), jnp.float32),
            pltpu.SemaphoreType.DMA(()),
            pltpu.VMEM((NSUB * R, TILE), jnp.bfloat16),
            pltpu.SemaphoreType.DMA((2,)),
            pltpu.VMEM((R // 2, 3 * TILE), jnp.float32),
            pltpu.VMEM(velocity.shape, jnp.float32),
            pltpu.SemaphoreType.DMA((len(rounds),)),
            pltpu.VMEM((code_parts[1].shape[0], NSUB * R), jnp.bfloat16),
            pltpu.VMEM((code_parts[1].shape[0], planes * ny), jnp.bfloat16),
        ],
        compiler_params=pltpu.CompilerParams(collective_id=0, has_side_effects=True),
    )(*code_parts, rotor_states, velocity, w_in, decay.reshape(1, -1), w_out)

def stencil_plane(x, planes, vel_ref, xlo_ref, xhi_ref, ylo_ref, yhi_ref):
    _, _, ny, nz = vel_ref.shape
    rows = lax.broadcasted_iota(jnp.int32, (ny, nz), 0)
    lanes = lax.broadcasted_iota(jnp.int32, (ny, nz), 1)
    here = [vel_ref[c, x] for c in range(3)]
    results = []
    for c in range(3):
        u = here[c]
        west = jnp.where(x == 0, xlo_ref[c].astype(jnp.float32), vel_ref[c, jnp.maximum(x - 1, 0)])
        east = jnp.where(x == planes - 1, xhi_ref[c].astype(jnp.float32), vel_ref[c, jnp.minimum(x + 1, planes - 1)])
        south = jnp.where(rows == 0, ylo_ref[c, x].astype(jnp.float32), pltpu.roll(u, 1, 0))
        north = jnp.where(rows == ny - 1, yhi_ref[c, x].astype(jnp.float32), pltpu.roll(u, ny - 1, 0))
        lower = jnp.where(lanes == 0, 0.0, pltpu.roll(u, 1, 1))
        upper = jnp.where(lanes == nz - 1, 0.0, pltpu.roll(u, nz - 1, 1))
        laplace = east + west + north + south + upper + lower - 6.0 * u
        advect = (
            here[0] * ((east - west) * 0.5)
            + here[1] * ((north - south) * 0.5)
            + here[2] * ((upper - lower) * 0.5)
        )
        results.append(u + time_step * (viscosity * laplace - advect))
    return results


def stencil_kernel(vel_ref, xlo_ref, xhi_ref, ylo_ref, yhi_ref, force_ref, out_ref):
    planes = vel_ref.shape[1]

    def body(x, carry):
        results = stencil_plane(x, planes, vel_ref, xlo_ref, xhi_ref, ylo_ref, yhi_ref)
        out_ref[0, x] = results[0] - force_scale * force_ref[x]
        out_ref[1, x] = results[1]
        out_ref[2, x] = results[2]
        return carry

    lax.fori_loop(0, planes, body, 0)


def stencil(velocity, halos, forcing):
    vmem = pl.BlockSpec(memory_space=pltpu.VMEM)
    return pl.pallas_call(
        stencil_kernel,
        out_shape=jax.ShapeDtypeStruct(velocity.shape, velocity.dtype),
        in_specs=[vmem] * 6,
        out_specs=vmem,
    )(velocity, *halos, forcing)


def halo_faces(velocity):
    faces = []
    for axis, dim in (("slab", 1), ("cross", 2)):
        count = lax.axis_size(axis)
        size = velocity.shape[dim]
        head = lax.slice_in_dim(velocity, 0, 1, axis=dim).astype(jnp.bfloat16)
        tail = lax.slice_in_dim(velocity, size - 1, size, axis=dim).astype(jnp.bfloat16)
        low = lax.ppermute(tail, axis, [(i, i + 1) for i in range(count - 1)])
        high = lax.ppermute(head, axis, [(i + 1, i) for i in range(count - 1)])
        faces += [jnp.squeeze(low, dim), jnp.squeeze(high, dim)] if dim == 1 else [low, high]
    return faces


def extended(cells, sides, width):
    for axis, dim in sides:
        count = lax.axis_size(axis)
        ends = count - 1
        head = lax.slice_in_dim(cells, 0, width, axis=dim)
        tail = lax.slice_in_dim(cells, cells.shape[dim] - width, cells.shape[dim], axis=dim)
        cells = jnp.concatenate(
            [
                lax.ppermute(tail, axis, [(i, (i + 1) % count) for i in range(ends)]),
                cells,
                lax.ppermute(head, axis, [((i + 1) % count, i) for i in range(ends)]),
            ],
            axis=dim,
        )
    return cells


def combine_terms(velocity, east, west, north, south, upper, lower):
    laplace = east + west + north + south + upper + lower - 6.0 * velocity
    advect = (
        velocity[0:1] * ((east - west) * 0.5)
        + velocity[1:2] * ((north - south) * 0.5)
        + velocity[2:3] * ((upper - lower) * 0.5)
    )
    return velocity + time_step * (viscosity * laplace - advect)


def on_device(
    velocity,
    shape_weight,
    w_in,
    w_out,
    decay,
    rotor_states,
    slot_of_rotor,
    entry_rotor,
    entry_tile,
    entry_sub,
):
    local_x, local_y, local_z = (velocity.shape[1], velocity.shape[2], velocity.shape[3])
    tile_count = local_x * local_y * local_z // TILE
    rotor_hot = (entry_rotor == jnp.arange(R, dtype=jnp.int32)[None, :]).astype(jnp.int32)
    slots = jnp.sum(rotor_hot * slot_of_rotor[None, :], axis=1)
    high = lax.reduce_precision(shape_weight, exponent_bits=8, mantissa_bits=7)
    rest = shape_weight - high
    middle = lax.reduce_precision(rest, exponent_bits=8, mantissa_bits=7)
    low = rest - middle
    parts = jnp.stack([high, middle, low]).astype(jnp.bfloat16)
    halves = local_z // TILE
    code = (((entry_tile // halves) * NSUB + entry_sub) * R + slots) * halves + entry_tile % halves
    new_states, advanced = reduce_step((parts, code[:, None]), rotor_states, velocity, w_in, decay, w_out)
    return (advanced, new_states)


def solution(mesh):
    in_specs = (
        P(None, "slab", "cross", None),
        P(),
        P(),
        P(),
        P(),
        P("slab", None),
        P(),
        P(("slab", "cross"), None),
        P(("slab", "cross")),
        P(("slab", "cross")),
    )
    out_specs = (P(None, "slab", "cross", None), P("slab", None))
    return jax.shard_map(
        on_device, mesh=mesh, in_specs=in_specs, out_specs=out_specs, check_vma=False
    )
```

```python
import jax
import jax.numpy as jnp
from jax import lax
from jax.experimental import pallas as pl
from jax.experimental.pallas import tpu as pltpu
from jax.sharding import PartitionSpec as P

MESH = pl.DeviceIdType.MESH

TILE = 128
R = 32
NSUB = 32


time_step = 0.1
viscosity = 0.3
pool_scale = 1.0 / 64.0
state_step = 0.5
force_scale = 0.5


def ring_perm(size, stride, n, shift):
    pairs = []
    for s in range(size):
        base = (s // (stride * n)) * stride * n + s % stride
        pos = (s // stride) % n
        pairs.append((s, base + ((pos + shift) % n) * stride))
    return pairs


def ring_sum(value, axis, stride, n):
    size = lax.axis_size(axis)
    if n == 2:
        return value + lax.ppermute(value, axis, ring_perm(size, stride, n, 1))
    got = [lax.ppermute(value, axis, ring_perm(size, stride, n, j)) for j in (1, 2, 3)]
    return (value + got[1]) + (got[0] + got[2])


def ring_gather(value, axis, stride, n):
    size = lax.axis_size(axis)
    pos = (lax.axis_index(axis) // stride) % n
    got = [value] + [lax.ppermute(value, axis, ring_perm(size, stride, n, j)) for j in range(1, n)]
    parts = []
    for p in range(n):
        pick = got[0]
        for j in range(1, n):
            pick = jnp.where((pos - j) % n == p, got[j], pick)
        parts.append(jnp.where(pos == p, got[0], pick))
    return jnp.concatenate(parts, axis=0)


def mesh_rings():
    slab = lax.axis_size("slab")
    rings = [("slab", 1, 2), ("slab", 2, 4), ("slab", 8, slab // 8)]
    return rings


def all_sum(value):
    for axis, stride, n in mesh_rings() + [("cross", 1, lax.axis_size("cross"))]:
        value = ring_sum(value, axis, stride, n)
    return value


def slab_gather(value):
    parts = value
    for axis, stride, n in mesh_rings():
        parts = ring_gather(parts, axis, stride, n)
    return parts


def ring_rounds(slab, cross):
    return [(0, 1, 2), (0, 2, 4), (0, 8, slab // 8), (1, 1, cross)]


def partner(me, stride, n, shift):
    pos = (me // stride) % n
    return me - pos * stride + ((pos + shift) % n) * stride


def unpack(code_ref):
    code = code_ref[...]
    half = code % 2
    slot = (code // 2) % R
    sub = (code // (2 * R)) % NSUB
    pos = code // (2 * R * NSUB)
    return pos, sub, slot, half


def pool_samples(vel_ref, parts, code_ref):
    _, planes, ny, nz = vel_ref.shape
    entries = code_ref.shape[0]
    cells_xy = planes * ny
    pos, sub, slot, half = unpack(code_ref)
    sub_hot = (sub == lax.broadcasted_iota(jnp.int32, (entries, parts[0].shape[0]), 1)).astype(jnp.bfloat16)
    gains = [jnp.dot(sub_hot, part[...], preferred_element_type=jnp.float32) for part in parts]
    gains = (gains[0] + gains[1]) + gains[2]
    pick_hot = (pos == lax.broadcasted_iota(jnp.int32, (entries, cells_xy), 1)).astype(jnp.bfloat16)
    slot_hot = (slot == lax.broadcasted_iota(jnp.int32, (entries, R), 1)).astype(jnp.float32)
    pooled = []
    for c in range(3):
        cells = vel_ref[c].reshape(cells_xy, nz).astype(jnp.bfloat16)
        both = jnp.dot(pick_hot, cells, preferred_element_type=jnp.float32)
        picked = both[:, :TILE]
        for h in range(1, nz // TILE):
            picked = jnp.where(half == h, both[:, h * TILE:(h + 1) * TILE], picked)
        weighted = gains[:, c * TILE:(c + 1) * TILE] * picked
        pooled.append(
            lax.dot_general(
                slot_hot, weighted, (((0,), (0,)), ((), ())),
                precision=lax.Precision.HIGHEST, preferred_element_type=jnp.float32,
            )
        )
    return pooled


def place_forcing(src, code_ref, flat_ref, adv_ref, row_hot_ref, pick_ref):
    _, planes, ny, nz = adv_ref.shape
    pos, sub, slot, half = unpack(code_ref)
    for j in range(NSUB):
        flat_ref[j * R:(j + 1) * R, :] = src[:, j * TILE:(j + 1) * TILE]
    rows = jnp.dot(row_hot_ref[...], flat_ref[...], preferred_element_type=jnp.float32)
    wide = jnp.concatenate(
        [jnp.where(half == h, rows, 0.0) for h in range(nz // TILE)], axis=1
    ).astype(jnp.bfloat16)
    pick_hot = pick_ref[...]
    forcing = lax.dot_general(pick_hot, wide, (((0,), (0,)), ((), ())), preferred_element_type=jnp.float32)
    adv_ref[0] = adv_ref[0] - force_scale * forcing.reshape(planes, ny, nz)

def step_kernel(rounds, high_ref, middle_ref, low_ref, code_ref, st_ref, vel_ref, w_in_ref, decay_ref,
                w_out_hbm, own_ref, adv_hbm,
                states_ref, p0, p1, p2, p3, p4, held, sends, recvs, st_sends, st_recvs, xlo, xhi, ylo, yhi, face_sends,
                face_recvs, w_out_ref, new_ref, w_sem, flat_ref, swap_sems, swap_ref, adv_ref, adv_sems, row_hot_ref, pick_ref):
    here = (lax.axis_index("slab"), lax.axis_index("cross"))
    slab, cross = lax.axis_size("slab"), lax.axis_size("cross")
    planes = vel_ref.shape[1]
    ny = vel_ref.shape[2]
    s, c = here

    def device(axis, other):
        return (other, here[1]) if axis == 0 else (here[0], other)

    extra = s - 1 + 2 * (s % 2)
    barrier = pltpu.get_barrier_semaphore()
    count = 0
    for axis, stride, n in rounds:
        for j in range(1, n):
            pl.semaphore_signal(barrier, inc=1, device_id=device(axis, partner(here[axis], stride, n, j)), device_id_type=MESH)
            count += 1
    pl.semaphore_signal(barrier, inc=1, device_id=((extra + slab) % slab, c), device_id_type=MESH)
    w_copy = pltpu.make_async_copy(w_out_hbm, w_out_ref, w_sem)
    w_copy.start()
    pooled = pool_samples(vel_ref, (high_ref, middle_ref, low_ref), code_ref)
    for k in range(3):
        p0[:, k * TILE:(k + 1) * TILE] = pooled[k]
    states_ref[pl.ds(s, 1)] = st_ref[...][None]
    pl.semaphore_wait(barrier, count + 1)

    faces = [
        (s > 0, s < slab - 1, vel_ref.at[:, 0], xhi, ((s + slab - 1) % slab, c)),
        (s < slab - 1, s > 0, vel_ref.at[:, planes - 1], xlo, ((s + 1) % slab, c)),
        (c > 0, c < cross - 1, vel_ref.at[:, :, pl.ds(0, 1)], yhi, (s, (c + cross - 1) % cross)),
        (c < cross - 1, c > 0, vel_ref.at[:, :, pl.ds(ny - 1, 1)], ylo, (s, (c + 1) % cross)),
    ]
    face_copies = []
    for k, (send_if, recv_if, src, dst, dev) in enumerate(faces):
        copy = pltpu.make_async_remote_copy(
            src_ref=src, dst_ref=dst, send_sem=face_sends.at[k], recv_sem=face_recvs.at[k],
            device_id=dev, device_id_type=MESH,
        )

        @pl.when(send_if)
        def _():
            copy.start()

        @pl.when(jnp.logical_not(recv_if))
        def _():
            dst[...] = jnp.zeros(dst.shape, dst.dtype)

        face_copies.append((send_if, recv_if, copy))


    chunks = [None, (0, 6), (6, 11), (11, planes)]
    share = R // 2
    mine = pl.ds(pl.multiple_of((s % 2) * share, share), share)
    final = len(rounds)
    bufs = [p0, p1, p2, p3, p4]
    outs = []
    sent = []
    for r, (axis, stride, n) in enumerate(rounds):
        copies = []
        for j in range(1, n):
            dev = device(axis, partner(here[axis], stride, n, j))
            copy = pltpu.make_async_remote_copy(
                src_ref=bufs[0] if r == 0 else bufs[r].at[mine],
                dst_ref=held.at[r, j - 1] if r == 0 else held.at[r, j - 1, pl.ds(0, share)],
                send_sem=sends.at[r, j - 1],
                recv_sem=recvs.at[r, j - 1],
                device_id=dev,
                device_id_type=MESH,
            )
            copy.start()
            copies.append(copy)
            if axis == 0:
                rows = pl.ds(s - s % stride, stride)
                block = pltpu.make_async_remote_copy(
                    src_ref=states_ref.at[rows],
                    dst_ref=states_ref.at[rows],
                    send_sem=st_sends.at[r, j - 1],
                    recv_sem=st_recvs.at[r, j - 1],
                    device_id=dev,
                    device_id_type=MESH,
                )
                block.start()
                copies.append(block)
        if r == 1:
            for send_if, recv_if, face in face_copies:


                @pl.when(recv_if)
                def _():
                    face.wait_recv()
        if chunks[r] is not None:
            first, last = chunks[r]

            def body(x, carry):
                results = stencil_plane(x, planes, vel_ref, xlo, xhi, ylo, yhi)
                for k in range(3):
                    adv_ref[k, x] = results[k]
                return carry

            lax.fori_loop(first, last, body, 0)
            out = pltpu.make_async_copy(
                adv_ref.at[pl.ds(1, 2), pl.ds(first, last - first)],
                adv_hbm.at[pl.ds(1, 2), pl.ds(first, last - first)],
                adv_sems.at[r - 1],
            )
            out.start()
            outs.append(out)
            if r == len(rounds) - 1:
                pos, sub, slot, half = unpack(code_ref)
                entries = code_ref.shape[0]
                row_hot_ref[...] = (
                    (sub * R + slot) == lax.broadcasted_iota(jnp.int32, (entries, NSUB * R), 1)
                ).astype(jnp.bfloat16)
                pick_ref[...] = (pos == lax.broadcasted_iota(jnp.int32, (entries, planes * ny), 1)).astype(jnp.bfloat16)
        for copy in copies:
            copy.wait_recv()
        sent += copies
        if r == 0:
            bufs[r + 1][mine, :] = bufs[r][mine, :] + held[r, 0, mine, :]
        elif n == 2:
            bufs[r + 1][mine, :] = bufs[r][mine, :] + held[r, 0, pl.ds(0, share)]
        else:
            got = [held[r, k, pl.ds(0, share)] for k in range(3)]
            bufs[r + 1][mine, :] = (bufs[r][mine, :] + got[1]) + (got[0] + got[2])
    swap = pltpu.make_async_remote_copy(
        src_ref=bufs[final].at[mine],
        dst_ref=swap_ref,
        send_sem=swap_sems.at[0],
        recv_sem=swap_sems.at[1],
        device_id=(s + 1 - 2 * (s % 2), c),
        device_id_type=MESH,
    )
    swap.start()
    swap.wait()
    bufs[final][pl.ds(pl.multiple_of((1 - s % 2) * share, share), share), :] = swap_ref[...]

    pooled_b = (bufs[final][...] * pool_scale).astype(jnp.bfloat16)
    drive = jnp.dot(pooled_b, w_in_ref[...], preferred_element_type=jnp.float32)
    decay = decay_ref[...]
    for k in range(states_ref.shape[0]):
        row = states_ref[k]
        new_ref[pl.ds(k, 1), :] = row + state_step * (drive[k:k + 1] - decay * row)
    slot_rows = lax.broadcasted_iota(jnp.int32, drive.shape, 0)
    own_drive = jnp.sum(jnp.where(slot_rows == s, drive, 0.0), axis=0, keepdims=True)
    own = st_ref[...]
    own_ref[...] = own + state_step * (own_drive - decay * own)
    w_copy.wait()
    src = jnp.dot(
        new_ref[...].astype(jnp.bfloat16), w_out_ref[...], preferred_element_type=jnp.float32
    ).astype(jnp.bfloat16)
    place_forcing(src, code_ref, flat_ref, adv_ref, row_hot_ref, pick_ref)
    out = pltpu.make_async_copy(adv_ref.at[0], adv_hbm.at[0], adv_sems.at[len(rounds) - 1])
    out.start()
    outs.append(out)
    for out in outs:
        out.wait()
    for copy in sent:
        copy.wait_send()
    for send_if, recv_if, face in face_copies:

        @pl.when(send_if)
        def _():
            face.wait_send()

def reduce_step(code_parts, rotor_states, velocity, w_in, decay, w_out):
    slab, cross = lax.axis_size("slab"), lax.axis_size("cross")
    rounds = ring_rounds(slab, cross)
    vmem = pl.BlockSpec(memory_space=pltpu.VMEM)
    _, planes, ny, nz = velocity.shape
    return pl.pallas_call(
        lambda *refs: step_kernel(rounds, *refs),
        out_shape=(
            jax.ShapeDtypeStruct(rotor_states.shape, jnp.float32),
            jax.ShapeDtypeStruct(velocity.shape, jnp.float32),
        ),
        in_specs=[vmem] * 8 + [pl.BlockSpec(memory_space=pl.ANY)],
        out_specs=(vmem, pl.BlockSpec(memory_space=pl.ANY)),
        scratch_shapes=[
            pltpu.VMEM((slab,) + rotor_states.shape, jnp.float32),
            *[pltpu.VMEM((R, 3 * TILE), jnp.float32) for _ in range(len(rounds) + 1)],
            pltpu.VMEM((len(rounds), 3, R, 3 * TILE), jnp.float32),
            pltpu.SemaphoreType.DMA((len(rounds), 3)),
            pltpu.SemaphoreType.DMA((len(rounds), 3)),
            pltpu.SemaphoreType.DMA((len(rounds), 3)),
            pltpu.SemaphoreType.DMA((len(rounds), 3)),
            pltpu.VMEM((3, ny, nz), jnp.float32),
            pltpu.VMEM((3, ny, nz), jnp.float32),
            pltpu.VMEM((3, planes, 1, nz), jnp.float32),
            pltpu.VMEM((3, planes, 1, nz), jnp.float32),
            pltpu.SemaphoreType.DMA((4,)),
            pltpu.SemaphoreType.DMA((4,)),
            pltpu.VMEM(w_out.shape, w_out.dtype),
            pltpu.VMEM((slab, w_out.shape[0]), jnp.float32),
            pltpu.SemaphoreType.DMA(()),
            pltpu.VMEM((NSUB * R, TILE), jnp.bfloat16),
            pltpu.SemaphoreType.DMA((2,)),
            pltpu.VMEM((R // 2, 3 * TILE), jnp.float32),
            pltpu.VMEM(velocity.shape, jnp.float32),
            pltpu.SemaphoreType.DMA((len(rounds),)),
            pltpu.VMEM((code_parts[-1].shape[0], NSUB * R), jnp.bfloat16),
            pltpu.VMEM((code_parts[-1].shape[0], planes * ny), jnp.bfloat16),
        ],
        compiler_params=pltpu.CompilerParams(collective_id=0, has_side_effects=True),
    )(*code_parts, rotor_states, velocity, w_in, decay.reshape(1, -1), w_out)

def stencil_plane(x, planes, vel_ref, xlo_ref, xhi_ref, ylo_ref, yhi_ref):
    _, _, ny, nz = vel_ref.shape
    rows = lax.broadcasted_iota(jnp.int32, (ny, nz), 0)
    lanes = lax.broadcasted_iota(jnp.int32, (ny, nz), 1)
    here = [vel_ref[c, x] for c in range(3)]
    results = []
    for c in range(3):
        u = here[c]
        west = jnp.where(x == 0, xlo_ref[c].astype(jnp.float32), vel_ref[c, jnp.maximum(x - 1, 0)])
        east = jnp.where(x == planes - 1, xhi_ref[c].astype(jnp.float32), vel_ref[c, jnp.minimum(x + 1, planes - 1)])
        south = jnp.where(rows == 0, ylo_ref[c, x].astype(jnp.float32), pltpu.roll(u, 1, 0))
        north = jnp.where(rows == ny - 1, yhi_ref[c, x].astype(jnp.float32), pltpu.roll(u, ny - 1, 0))
        lower = jnp.where(lanes == 0, 0.0, pltpu.roll(u, 1, 1))
        upper = jnp.where(lanes == nz - 1, 0.0, pltpu.roll(u, nz - 1, 1))
        laplace = east + west + north + south + upper + lower - 6.0 * u
        advect = (
            here[0] * ((east - west) * 0.5)
            + here[1] * ((north - south) * 0.5)
            + here[2] * ((upper - lower) * 0.5)
        )
        results.append(u + time_step * (viscosity * laplace - advect))
    return results


def stencil_kernel(vel_ref, xlo_ref, xhi_ref, ylo_ref, yhi_ref, force_ref, out_ref):
    planes = vel_ref.shape[1]

    def body(x, carry):
        results = stencil_plane(x, planes, vel_ref, xlo_ref, xhi_ref, ylo_ref, yhi_ref)
        out_ref[0, x] = results[0] - force_scale * force_ref[x]
        out_ref[1, x] = results[1]
        out_ref[2, x] = results[2]
        return carry

    lax.fori_loop(0, planes, body, 0)


def stencil(velocity, halos, forcing):
    vmem = pl.BlockSpec(memory_space=pltpu.VMEM)
    return pl.pallas_call(
        stencil_kernel,
        out_shape=jax.ShapeDtypeStruct(velocity.shape, velocity.dtype),
        in_specs=[vmem] * 6,
        out_specs=vmem,
    )(velocity, *halos, forcing)


def halo_faces(velocity):
    faces = []
    for axis, dim in (("slab", 1), ("cross", 2)):
        count = lax.axis_size(axis)
        size = velocity.shape[dim]
        head = lax.slice_in_dim(velocity, 0, 1, axis=dim).astype(jnp.bfloat16)
        tail = lax.slice_in_dim(velocity, size - 1, size, axis=dim).astype(jnp.bfloat16)
        low = lax.ppermute(tail, axis, [(i, i + 1) for i in range(count - 1)])
        high = lax.ppermute(head, axis, [(i + 1, i) for i in range(count - 1)])
        faces += [jnp.squeeze(low, dim), jnp.squeeze(high, dim)] if dim == 1 else [low, high]
    return faces


def extended(cells, sides, width):
    for axis, dim in sides:
        count = lax.axis_size(axis)
        ends = count - 1
        head = lax.slice_in_dim(cells, 0, width, axis=dim)
        tail = lax.slice_in_dim(cells, cells.shape[dim] - width, cells.shape[dim], axis=dim)
        cells = jnp.concatenate(
            [
                lax.ppermute(tail, axis, [(i, (i + 1) % count) for i in range(ends)]),
                cells,
                lax.ppermute(head, axis, [((i + 1) % count, i) for i in range(ends)]),
            ],
            axis=dim,
        )
    return cells


def combine_terms(velocity, east, west, north, south, upper, lower):
    laplace = east + west + north + south + upper + lower - 6.0 * velocity
    advect = (
        velocity[0:1] * ((east - west) * 0.5)
        + velocity[1:2] * ((north - south) * 0.5)
        + velocity[2:3] * ((upper - lower) * 0.5)
    )
    return velocity + time_step * (viscosity * laplace - advect)


def on_device(
    velocity,
    shape_weight,
    w_in,
    w_out,
    decay,
    rotor_states,
    slot_of_rotor,
    entry_rotor,
    entry_tile,
    entry_sub,
):
    local_x, local_y, local_z = (velocity.shape[1], velocity.shape[2], velocity.shape[3])
    tile_count = local_x * local_y * local_z // TILE
    rotor_hot = (entry_rotor == jnp.arange(R, dtype=jnp.int32)[None, :]).astype(jnp.int32)
    slots = jnp.sum(rotor_hot * slot_of_rotor[None, :], axis=1)
    high = lax.reduce_precision(shape_weight, exponent_bits=8, mantissa_bits=7)
    rest = shape_weight - high
    middle = lax.reduce_precision(rest, exponent_bits=8, mantissa_bits=7)
    low = rest - middle
    parts = tuple(part.astype(jnp.bfloat16) for part in (high, middle, low))
    halves = local_z // TILE
    code = (((entry_tile // halves) * NSUB + entry_sub) * R + slots) * halves + entry_tile % halves
    new_states, advanced = reduce_step(parts + (code[:, None],), rotor_states, velocity, w_in, decay, w_out)
    return (advanced, new_states)


def solution(mesh):
    in_specs = (
        P(None, "slab", "cross", None),
        P(),
        P(),
        P(),
        P(),
        P("slab", None),
        P(),
        P(("slab", "cross"), None),
        P(("slab", "cross")),
        P(("slab", "cross")),
    )
    out_specs = (P(None, "slab", "cross", None), P("slab", None))
    return jax.shard_map(
        on_device, mesh=mesh, in_specs=in_specs, out_specs=out_specs, check_vma=False
    )
```

```python
import jax
import jax.numpy as jnp
from jax import lax
from jax.experimental import pallas as pl
from jax.experimental.pallas import tpu as pltpu
from jax.sharding import PartitionSpec as P

MESH = pl.DeviceIdType.MESH

TILE = 128
R = 32
NSUB = 32


time_step = 0.1
viscosity = 0.3
pool_scale = 1.0 / 64.0
state_step = 0.5
force_scale = 0.5


def ring_perm(size, stride, n, shift):
    pairs = []
    for s in range(size):
        base = (s // (stride * n)) * stride * n + s % stride
        pos = (s // stride) % n
        pairs.append((s, base + ((pos + shift) % n) * stride))
    return pairs


def ring_sum(value, axis, stride, n):
    size = lax.axis_size(axis)
    if n == 2:
        return value + lax.ppermute(value, axis, ring_perm(size, stride, n, 1))
    got = [lax.ppermute(value, axis, ring_perm(size, stride, n, j)) for j in (1, 2, 3)]
    return (value + got[1]) + (got[0] + got[2])


def ring_gather(value, axis, stride, n):
    size = lax.axis_size(axis)
    pos = (lax.axis_index(axis) // stride) % n
    got = [value] + [lax.ppermute(value, axis, ring_perm(size, stride, n, j)) for j in range(1, n)]
    parts = []
    for p in range(n):
        pick = got[0]
        for j in range(1, n):
            pick = jnp.where((pos - j) % n == p, got[j], pick)
        parts.append(jnp.where(pos == p, got[0], pick))
    return jnp.concatenate(parts, axis=0)


def mesh_rings():
    slab = lax.axis_size("slab")
    rings = [("slab", 1, 2), ("slab", 2, 4), ("slab", 8, slab // 8)]
    return rings


def all_sum(value):
    for axis, stride, n in mesh_rings() + [("cross", 1, lax.axis_size("cross"))]:
        value = ring_sum(value, axis, stride, n)
    return value


def slab_gather(value):
    parts = value
    for axis, stride, n in mesh_rings():
        parts = ring_gather(parts, axis, stride, n)
    return parts


def ring_rounds(slab, cross):
    return [(0, 1, 2), (0, 2, 4), (0, 8, slab // 8), (1, 1, cross)]


def partner(me, stride, n, shift):
    pos = (me // stride) % n
    return me - pos * stride + ((pos + shift) % n) * stride


def unpack(code_ref):
    code = code_ref[...]
    half = code % 2
    slot = (code // 2) % R
    sub = (code // (2 * R)) % NSUB
    pos = code // (2 * R * NSUB)
    return pos, sub, slot, half


def pool_samples(vel_ref, parts_ref, code_ref, emit):
    _, planes, ny, nz = vel_ref.shape
    entries = code_ref.shape[0]
    cells_xy = planes * ny
    pos, sub, slot, half = unpack(code_ref)
    sub_hot = (sub == lax.broadcasted_iota(jnp.int32, (entries, parts_ref.shape[1]), 1)).astype(jnp.bfloat16)
    gains = [jnp.dot(sub_hot, parts_ref[k], preferred_element_type=jnp.float32) for k in range(3)]
    gains = (gains[0] + gains[1]) + gains[2]
    pick_hot = (pos == lax.broadcasted_iota(jnp.int32, (entries, cells_xy), 1)).astype(jnp.bfloat16)
    slot_hot = (slot == lax.broadcasted_iota(jnp.int32, (entries, R), 1)).astype(jnp.float32)
    pooled = []
    for c in range(3):
        cells = vel_ref[c].reshape(cells_xy, nz).astype(jnp.bfloat16)
        both = jnp.dot(pick_hot, cells, preferred_element_type=jnp.float32)
        picked = both[:, :TILE]
        for h in range(1, nz // TILE):
            picked = jnp.where(half == h, both[:, h * TILE:(h + 1) * TILE], picked)
        weighted = gains[:, c * TILE:(c + 1) * TILE] * picked
        pooled.append(
            lax.dot_general(
                slot_hot, weighted, (((0,), (0,)), ((), ())),
                precision=lax.Precision.HIGHEST, preferred_element_type=jnp.float32,
            )
        )
        emit(c, pooled[-1])
    return pooled


def place_forcing(src, code_ref, flat_ref, adv_ref, row_hot_ref, pick_ref):
    _, planes, ny, nz = adv_ref.shape
    pos, sub, slot, half = unpack(code_ref)
    for j in range(NSUB):
        flat_ref[j * R:(j + 1) * R, :] = src[:, j * TILE:(j + 1) * TILE]
    rows = jnp.dot(row_hot_ref[...], flat_ref[...], preferred_element_type=jnp.float32)
    wide = jnp.concatenate(
        [jnp.where(half == h, rows, 0.0) for h in range(nz // TILE)], axis=1
    ).astype(jnp.bfloat16)
    pick_hot = pick_ref[...]
    forcing = lax.dot_general(pick_hot, wide, (((0,), (0,)), ((), ())), preferred_element_type=jnp.float32)
    adv_ref[0] = adv_ref[0] - force_scale * forcing.reshape(planes, ny, nz)

def step_kernel(rounds, parts_ref, code_ref, st_ref, vel_ref, w_in_ref, decay_ref,
                w_out_hbm, own_ref, adv_hbm,
                states_ref, p0, p1, p2, p3, p4, held, sends, recvs, st_sends, st_recvs, xlo, xhi, ylo, yhi, face_sends,
                face_recvs, w_out_ref, new_ref, w_sem, flat_ref, swap_sems, swap_ref, adv_ref, adv_sems, row_hot_ref, pick_ref):
    here = (lax.axis_index("slab"), lax.axis_index("cross"))
    slab, cross = lax.axis_size("slab"), lax.axis_size("cross")
    planes = vel_ref.shape[1]
    ny = vel_ref.shape[2]
    s, c = here

    def device(axis, other):
        return (other, here[1]) if axis == 0 else (here[0], other)

    extra = s - 1 + 2 * (s % 2)
    barrier = pltpu.get_barrier_semaphore()
    count = 0
    for axis, stride, n in rounds:
        for j in range(1, n):
            pl.semaphore_signal(barrier, inc=1, device_id=device(axis, partner(here[axis], stride, n, j)), device_id_type=MESH)
            count += 1
    pl.semaphore_signal(barrier, inc=1, device_id=((extra + slab) % slab, c), device_id_type=MESH)
    w_copy = pltpu.make_async_copy(w_out_hbm, w_out_ref, w_sem)
    w_copy.start()
    states_ref[pl.ds(s, 1)] = st_ref[...][None]
    first_round = []

    def emit(k, value):
        columns = pl.ds(k * TILE, TILE)
        p0[:, columns] = value
        if k == 0:
            pl.semaphore_wait(barrier, count + 1)
        part = pltpu.make_async_remote_copy(
            src_ref=p0.at[:, columns],
            dst_ref=held.at[0, 0, :, columns],
            send_sem=sends.at[0, k],
            recv_sem=recvs.at[0, k],
            device_id=(s + 1 - 2 * (s % 2), c),
            device_id_type=MESH,
        )
        part.start()
        first_round.append(part)

    pool_samples(vel_ref, parts_ref, code_ref, emit)

    faces = [
        (s > 0, s < slab - 1, vel_ref.at[:, 0], xhi, ((s + slab - 1) % slab, c)),
        (s < slab - 1, s > 0, vel_ref.at[:, planes - 1], xlo, ((s + 1) % slab, c)),
        (c > 0, c < cross - 1, vel_ref.at[:, :, pl.ds(0, 1)], yhi, (s, (c + cross - 1) % cross)),
        (c < cross - 1, c > 0, vel_ref.at[:, :, pl.ds(ny - 1, 1)], ylo, (s, (c + 1) % cross)),
    ]
    face_copies = []
    for k, (send_if, recv_if, src, dst, dev) in enumerate(faces):
        copy = pltpu.make_async_remote_copy(
            src_ref=src, dst_ref=dst, send_sem=face_sends.at[k], recv_sem=face_recvs.at[k],
            device_id=dev, device_id_type=MESH,
        )

        @pl.when(send_if)
        def _():
            copy.start()

        @pl.when(jnp.logical_not(recv_if))
        def _():
            dst[...] = jnp.zeros(dst.shape, dst.dtype)

        face_copies.append((send_if, recv_if, copy))


    chunks = [None, (0, 6), (6, 11), (11, planes)]
    share = R // 2
    mine = pl.ds(pl.multiple_of((s % 2) * share, share), share)
    final = len(rounds)
    bufs = [p0, p1, p2, p3, p4]
    outs = []
    sent = []
    for r, (axis, stride, n) in enumerate(rounds):
        copies = list(first_round) if r == 0 else []
        for j in range(1, n):
            dev = device(axis, partner(here[axis], stride, n, j))
            copy = pltpu.make_async_remote_copy(
                src_ref=bufs[0] if r == 0 else bufs[r].at[mine],
                dst_ref=held.at[r, j - 1] if r == 0 else held.at[r, j - 1, pl.ds(0, share)],
                send_sem=sends.at[r, j - 1],
                recv_sem=recvs.at[r, j - 1],
                device_id=dev,
                device_id_type=MESH,
            )
            if r > 0:
                copy.start()
                copies.append(copy)
            if axis == 0:
                rows = pl.ds(s - s % stride, stride)
                block = pltpu.make_async_remote_copy(
                    src_ref=states_ref.at[rows],
                    dst_ref=states_ref.at[rows],
                    send_sem=st_sends.at[r, j - 1],
                    recv_sem=st_recvs.at[r, j - 1],
                    device_id=dev,
                    device_id_type=MESH,
                )
                block.start()
                copies.append(block)
        if r == 1:
            for send_if, recv_if, face in face_copies:


                @pl.when(recv_if)
                def _():
                    face.wait_recv()
        if chunks[r] is not None:
            first, last = chunks[r]

            def body(x, carry):
                results = stencil_plane(x, planes, vel_ref, xlo, xhi, ylo, yhi)
                for k in range(3):
                    adv_ref[k, x] = results[k]
                return carry

            lax.fori_loop(first, last, body, 0)
            out = pltpu.make_async_copy(
                adv_ref.at[pl.ds(1, 2), pl.ds(first, last - first)],
                adv_hbm.at[pl.ds(1, 2), pl.ds(first, last - first)],
                adv_sems.at[r - 1],
            )
            out.start()
            outs.append(out)
            if r == len(rounds) - 1:
                pos, sub, slot, half = unpack(code_ref)
                entries = code_ref.shape[0]
                row_hot_ref[...] = (
                    (sub * R + slot) == lax.broadcasted_iota(jnp.int32, (entries, NSUB * R), 1)
                ).astype(jnp.bfloat16)
                pick_ref[...] = (pos == lax.broadcasted_iota(jnp.int32, (entries, planes * ny), 1)).astype(jnp.bfloat16)
        for copy in copies:
            copy.wait_recv()
        sent += copies
        if r == 0:
            bufs[r + 1][mine, :] = bufs[r][mine, :] + held[r, 0, mine, :]
        elif n == 2:
            bufs[r + 1][mine, :] = bufs[r][mine, :] + held[r, 0, pl.ds(0, share)]
        else:
            got = [held[r, k, pl.ds(0, share)] for k in range(3)]
            bufs[r + 1][mine, :] = (bufs[r][mine, :] + got[1]) + (got[0] + got[2])
    swap = pltpu.make_async_remote_copy(
        src_ref=bufs[final].at[mine],
        dst_ref=swap_ref,
        send_sem=swap_sems.at[0],
        recv_sem=swap_sems.at[1],
        device_id=(s + 1 - 2 * (s % 2), c),
        device_id_type=MESH,
    )
    swap.start()
    swap.wait()
    bufs[final][pl.ds(pl.multiple_of((1 - s % 2) * share, share), share), :] = swap_ref[...]

    pooled_b = (bufs[final][...] * pool_scale).astype(jnp.bfloat16)
    drive = jnp.dot(pooled_b, w_in_ref[...], preferred_element_type=jnp.float32)
    decay = decay_ref[...]
    for k in range(states_ref.shape[0]):
        row = states_ref[k]
        new_ref[pl.ds(k, 1), :] = row + state_step * (drive[k:k + 1] - decay * row)
    slot_rows = lax.broadcasted_iota(jnp.int32, drive.shape, 0)
    own_drive = jnp.sum(jnp.where(slot_rows == s, drive, 0.0), axis=0, keepdims=True)
    own = st_ref[...]
    own_ref[...] = own + state_step * (own_drive - decay * own)
    w_copy.wait()
    src = jnp.dot(
        new_ref[...].astype(jnp.bfloat16), w_out_ref[...], preferred_element_type=jnp.float32
    ).astype(jnp.bfloat16)
    place_forcing(src, code_ref, flat_ref, adv_ref, row_hot_ref, pick_ref)
    out = pltpu.make_async_copy(adv_ref.at[0], adv_hbm.at[0], adv_sems.at[len(rounds) - 1])
    out.start()
    outs.append(out)
    for out in outs:
        out.wait()
    for copy in sent:
        copy.wait_send()
    for send_if, recv_if, face in face_copies:

        @pl.when(send_if)
        def _():
            face.wait_send()

def reduce_step(code_parts, rotor_states, velocity, w_in, decay, w_out):
    slab, cross = lax.axis_size("slab"), lax.axis_size("cross")
    rounds = ring_rounds(slab, cross)
    vmem = pl.BlockSpec(memory_space=pltpu.VMEM)
    _, planes, ny, nz = velocity.shape
    return pl.pallas_call(
        lambda *refs: step_kernel(rounds, *refs),
        out_shape=(
            jax.ShapeDtypeStruct(rotor_states.shape, jnp.float32),
            jax.ShapeDtypeStruct(velocity.shape, jnp.float32),
        ),
        in_specs=[vmem] * 6 + [pl.BlockSpec(memory_space=pl.ANY)],
        out_specs=(vmem, pl.BlockSpec(memory_space=pl.ANY)),
        scratch_shapes=[
            pltpu.VMEM((slab,) + rotor_states.shape, jnp.float32),
            *[pltpu.VMEM((R, 3 * TILE), jnp.float32) for _ in range(len(rounds) + 1)],
            pltpu.VMEM((len(rounds), 3, R, 3 * TILE), jnp.float32),
            pltpu.SemaphoreType.DMA((len(rounds), 3)),
            pltpu.SemaphoreType.DMA((len(rounds), 3)),
            pltpu.SemaphoreType.DMA((len(rounds), 3)),
            pltpu.SemaphoreType.DMA((len(rounds), 3)),
            pltpu.VMEM((3, ny, nz), jnp.float32),
            pltpu.VMEM((3, ny, nz), jnp.float32),
            pltpu.VMEM((3, planes, 1, nz), jnp.float32),
            pltpu.VMEM((3, planes, 1, nz), jnp.float32),
            pltpu.SemaphoreType.DMA((4,)),
            pltpu.SemaphoreType.DMA((4,)),
            pltpu.VMEM(w_out.shape, w_out.dtype),
            pltpu.VMEM((slab, w_out.shape[0]), jnp.float32),
            pltpu.SemaphoreType.DMA(()),
            pltpu.VMEM((NSUB * R, TILE), jnp.bfloat16),
            pltpu.SemaphoreType.DMA((2,)),
            pltpu.VMEM((R // 2, 3 * TILE), jnp.float32),
            pltpu.VMEM(velocity.shape, jnp.float32),
            pltpu.SemaphoreType.DMA((len(rounds),)),
            pltpu.VMEM((code_parts[1].shape[0], NSUB * R), jnp.bfloat16),
            pltpu.VMEM((code_parts[1].shape[0], planes * ny), jnp.bfloat16),
        ],
        compiler_params=pltpu.CompilerParams(collective_id=0, has_side_effects=True),
    )(*code_parts, rotor_states, velocity, w_in, decay.reshape(1, -1), w_out)

def stencil_plane(x, planes, vel_ref, xlo_ref, xhi_ref, ylo_ref, yhi_ref):
    _, _, ny, nz = vel_ref.shape
    rows = lax.broadcasted_iota(jnp.int32, (ny, nz), 0)
    lanes = lax.broadcasted_iota(jnp.int32, (ny, nz), 1)
    here = [vel_ref[c, x] for c in range(3)]
    results = []
    for c in range(3):
        u = here[c]
        west = jnp.where(x == 0, xlo_ref[c].astype(jnp.float32), vel_ref[c, jnp.maximum(x - 1, 0)])
        east = jnp.where(x == planes - 1, xhi_ref[c].astype(jnp.float32), vel_ref[c, jnp.minimum(x + 1, planes - 1)])
        south = jnp.where(rows == 0, ylo_ref[c, x].astype(jnp.float32), pltpu.roll(u, 1, 0))
        north = jnp.where(rows == ny - 1, yhi_ref[c, x].astype(jnp.float32), pltpu.roll(u, ny - 1, 0))
        lower = jnp.where(lanes == 0, 0.0, pltpu.roll(u, 1, 1))
        upper = jnp.where(lanes == nz - 1, 0.0, pltpu.roll(u, nz - 1, 1))
        laplace = east + west + north + south + upper + lower - 6.0 * u
        advect = (
            here[0] * ((east - west) * 0.5)
            + here[1] * ((north - south) * 0.5)
            + here[2] * ((upper - lower) * 0.5)
        )
        results.append(u + time_step * (viscosity * laplace - advect))
    return results


def stencil_kernel(vel_ref, xlo_ref, xhi_ref, ylo_ref, yhi_ref, force_ref, out_ref):
    planes = vel_ref.shape[1]

    def body(x, carry):
        results = stencil_plane(x, planes, vel_ref, xlo_ref, xhi_ref, ylo_ref, yhi_ref)
        out_ref[0, x] = results[0] - force_scale * force_ref[x]
        out_ref[1, x] = results[1]
        out_ref[2, x] = results[2]
        return carry

    lax.fori_loop(0, planes, body, 0)


def stencil(velocity, halos, forcing):
    vmem = pl.BlockSpec(memory_space=pltpu.VMEM)
    return pl.pallas_call(
        stencil_kernel,
        out_shape=jax.ShapeDtypeStruct(velocity.shape, velocity.dtype),
        in_specs=[vmem] * 6,
        out_specs=vmem,
    )(velocity, *halos, forcing)


def halo_faces(velocity):
    faces = []
    for axis, dim in (("slab", 1), ("cross", 2)):
        count = lax.axis_size(axis)
        size = velocity.shape[dim]
        head = lax.slice_in_dim(velocity, 0, 1, axis=dim).astype(jnp.bfloat16)
        tail = lax.slice_in_dim(velocity, size - 1, size, axis=dim).astype(jnp.bfloat16)
        low = lax.ppermute(tail, axis, [(i, i + 1) for i in range(count - 1)])
        high = lax.ppermute(head, axis, [(i + 1, i) for i in range(count - 1)])
        faces += [jnp.squeeze(low, dim), jnp.squeeze(high, dim)] if dim == 1 else [low, high]
    return faces


def extended(cells, sides, width):
    for axis, dim in sides:
        count = lax.axis_size(axis)
        ends = count - 1
        head = lax.slice_in_dim(cells, 0, width, axis=dim)
        tail = lax.slice_in_dim(cells, cells.shape[dim] - width, cells.shape[dim], axis=dim)
        cells = jnp.concatenate(
            [
                lax.ppermute(tail, axis, [(i, (i + 1) % count) for i in range(ends)]),
                cells,
                lax.ppermute(head, axis, [((i + 1) % count, i) for i in range(ends)]),
            ],
            axis=dim,
        )
    return cells


def combine_terms(velocity, east, west, north, south, upper, lower):
    laplace = east + west + north + south + upper + lower - 6.0 * velocity
    advect = (
        velocity[0:1] * ((east - west) * 0.5)
        + velocity[1:2] * ((north - south) * 0.5)
        + velocity[2:3] * ((upper - lower) * 0.5)
    )
    return velocity + time_step * (viscosity * laplace - advect)


def on_device(
    velocity,
    shape_weight,
    w_in,
    w_out,
    decay,
    rotor_states,
    slot_of_rotor,
    entry_rotor,
    entry_tile,
    entry_sub,
):
    local_x, local_y, local_z = (velocity.shape[1], velocity.shape[2], velocity.shape[3])
    tile_count = local_x * local_y * local_z // TILE
    rotor_hot = (entry_rotor == jnp.arange(R, dtype=jnp.int32)[None, :]).astype(jnp.int32)
    slots = jnp.sum(rotor_hot * slot_of_rotor[None, :], axis=1)
    high = lax.reduce_precision(shape_weight, exponent_bits=8, mantissa_bits=7)
    rest = shape_weight - high
    middle = lax.reduce_precision(rest, exponent_bits=8, mantissa_bits=7)
    low = rest - middle
    parts = jnp.stack([high, middle, low]).astype(jnp.bfloat16)
    halves = local_z // TILE
    code = (((entry_tile // halves) * NSUB + entry_sub) * R + slots) * halves + entry_tile % halves
    new_states, advanced = reduce_step((parts, code[:, None]), rotor_states, velocity, w_in, decay, w_out)
    return (advanced, new_states)


def solution(mesh):
    in_specs = (
        P(None, "slab", "cross", None),
        P(),
        P(),
        P(),
        P(),
        P("slab", None),
        P(),
        P(("slab", "cross"), None),
        P(("slab", "cross")),
        P(("slab", "cross")),
    )
    out_specs = (P(None, "slab", "cross", None), P("slab", None))
    return jax.shard_map(
        on_device, mesh=mesh, in_specs=in_specs, out_specs=out_specs, check_vma=False
    )
```

```python
import jax
import jax.numpy as jnp
from jax import lax
from jax.experimental import pallas as pl
from jax.experimental.pallas import tpu as pltpu
from jax.sharding import PartitionSpec as P

MESH = pl.DeviceIdType.MESH

TILE = 128
R = 32
NSUB = 32


time_step = 0.1
viscosity = 0.3
pool_scale = 1.0 / 64.0
state_step = 0.5
force_scale = 0.5


def ring_perm(size, stride, n, shift):
    pairs = []
    for s in range(size):
        base = (s // (stride * n)) * stride * n + s % stride
        pos = (s // stride) % n
        pairs.append((s, base + ((pos + shift) % n) * stride))
    return pairs


def ring_sum(value, axis, stride, n):
    size = lax.axis_size(axis)
    if n == 2:
        return value + lax.ppermute(value, axis, ring_perm(size, stride, n, 1))
    got = [lax.ppermute(value, axis, ring_perm(size, stride, n, j)) for j in (1, 2, 3)]
    return (value + got[1]) + (got[0] + got[2])


def ring_gather(value, axis, stride, n):
    size = lax.axis_size(axis)
    pos = (lax.axis_index(axis) // stride) % n
    got = [value] + [lax.ppermute(value, axis, ring_perm(size, stride, n, j)) for j in range(1, n)]
    parts = []
    for p in range(n):
        pick = got[0]
        for j in range(1, n):
            pick = jnp.where((pos - j) % n == p, got[j], pick)
        parts.append(jnp.where(pos == p, got[0], pick))
    return jnp.concatenate(parts, axis=0)


def mesh_rings():
    slab = lax.axis_size("slab")
    rings = [("slab", 1, 2), ("slab", 2, 4), ("slab", 8, slab // 8)]
    return rings


def all_sum(value):
    for axis, stride, n in mesh_rings() + [("cross", 1, lax.axis_size("cross"))]:
        value = ring_sum(value, axis, stride, n)
    return value


def slab_gather(value):
    parts = value
    for axis, stride, n in mesh_rings():
        parts = ring_gather(parts, axis, stride, n)
    return parts


def ring_rounds(slab, cross):
    return [(0, 1, 2), (0, 2, 4), (0, 8, slab // 8), (1, 1, cross)]


def partner(me, stride, n, shift):
    pos = (me // stride) % n
    return me - pos * stride + ((pos + shift) % n) * stride


def unpack(code_ref):
    code = code_ref[...]
    half = code % 2
    slot = (code // 2) % R
    sub = (code // (2 * R)) % NSUB
    pos = code // (2 * R * NSUB)
    return pos, sub, slot, half


def pool_samples(vel_ref, parts_ref, code_ref):
    _, planes, ny, nz = vel_ref.shape
    entries = code_ref.shape[0]
    cells_xy = planes * ny
    pos, sub, slot, half = unpack(code_ref)
    sub_hot = (sub == lax.broadcasted_iota(jnp.int32, (entries, parts_ref.shape[1]), 1)).astype(jnp.bfloat16)
    gains = [jnp.dot(sub_hot, parts_ref[k], preferred_element_type=jnp.float32) for k in range(3)]
    gains = (gains[0] + gains[1]) + gains[2]
    pick_hot = (pos == lax.broadcasted_iota(jnp.int32, (entries, cells_xy), 1)).astype(jnp.bfloat16)
    slot_hot = (slot == lax.broadcasted_iota(jnp.int32, (entries, R), 1)).astype(jnp.float32)
    pooled = []
    for c in range(3):
        cells = vel_ref[c].reshape(cells_xy, nz).astype(jnp.bfloat16)
        both = jnp.dot(pick_hot, cells, preferred_element_type=jnp.float32)
        picked = both[:, :TILE]
        for h in range(1, nz // TILE):
            picked = jnp.where(half == h, both[:, h * TILE:(h + 1) * TILE], picked)
        weighted = gains[:, c * TILE:(c + 1) * TILE] * picked
        pooled.append(
            lax.dot_general(
                slot_hot, weighted, (((0,), (0,)), ((), ())),
                precision=lax.Precision.HIGHEST, preferred_element_type=jnp.float32,
            )
        )
    return pooled


def place_forcing(src, code_ref, flat_ref, adv_ref, row_hot_ref, pick_ref):
    _, planes, ny, nz = adv_ref.shape
    pos, sub, slot, half = unpack(code_ref)
    for j in range(NSUB):
        flat_ref[j * R:(j + 1) * R, :] = src[:, j * TILE:(j + 1) * TILE]
    rows = jnp.dot(row_hot_ref[...], flat_ref[...], preferred_element_type=jnp.float32)
    wide = jnp.concatenate(
        [jnp.where(half == h, rows, 0.0) for h in range(nz // TILE)], axis=1
    ).astype(jnp.bfloat16)
    pick_hot = pick_ref[...]
    forcing = lax.dot_general(pick_hot, wide, (((0,), (0,)), ((), ())), preferred_element_type=jnp.float32)
    adv_ref[0] = adv_ref[0] - force_scale * forcing.reshape(planes, ny, nz)

def step_kernel(rounds, parts_ref, code_ref, st_ref, vel_ref, w_in_ref, decay_ref,
                w_out_hbm, own_ref, adv_hbm,
                states_ref, p0, p1, p2, p3, p4, held, sends, recvs, st_sends, st_recvs, xlo, xhi, ylo, yhi, face_sends,
                face_recvs, w_out_ref, new_ref, w_sem, flat_ref, swap_sems, swap_ref, adv_ref, adv_sems, row_hot_ref, pick_ref, held2, msends, mrecvs):
    here = (lax.axis_index("slab"), lax.axis_index("cross"))
    slab, cross = lax.axis_size("slab"), lax.axis_size("cross")
    planes = vel_ref.shape[1]
    ny = vel_ref.shape[2]
    s, c = here

    def device(axis, other):
        return (other, here[1]) if axis == 0 else (here[0], other)

    extra = s - 1 + 2 * (s % 2)
    barrier = pltpu.get_barrier_semaphore()
    count = 0
    for axis, stride, n in rounds:
        for j in range(1, n):
            pl.semaphore_signal(barrier, inc=1, device_id=device(axis, partner(here[axis], stride, n, j)), device_id_type=MESH)
            count += 1
    pl.semaphore_signal(barrier, inc=1, device_id=((extra + slab) % slab, c), device_id_type=MESH)
    for dz in range(1, 4):
        for dy in range(1, cross):
            pl.semaphore_signal(barrier, inc=1, device_id=(partner(s, 8, 4, dz), partner(c, 1, cross, dy)), device_id_type=MESH)
            count += 1
    w_copy = pltpu.make_async_copy(w_out_hbm, w_out_ref, w_sem)
    w_copy.start()
    pooled = pool_samples(vel_ref, parts_ref, code_ref)
    for k in range(3):
        p0[:, k * TILE:(k + 1) * TILE] = pooled[k]
    states_ref[pl.ds(s, 1)] = st_ref[...][None]
    pl.semaphore_wait(barrier, count + 1)

    faces = [
        (s > 0, s < slab - 1, vel_ref.at[:, 0], xhi, ((s + slab - 1) % slab, c)),
        (s < slab - 1, s > 0, vel_ref.at[:, planes - 1], xlo, ((s + 1) % slab, c)),
        (c > 0, c < cross - 1, vel_ref.at[:, :, pl.ds(0, 1)], yhi, (s, (c + cross - 1) % cross)),
        (c < cross - 1, c > 0, vel_ref.at[:, :, pl.ds(ny - 1, 1)], ylo, (s, (c + 1) % cross)),
    ]
    face_copies = []
    for k, (send_if, recv_if, src, dst, dev) in enumerate(faces):
        copy = pltpu.make_async_remote_copy(
            src_ref=src, dst_ref=dst, send_sem=face_sends.at[k], recv_sem=face_recvs.at[k],
            device_id=dev, device_id_type=MESH,
        )

        @pl.when(send_if)
        def _():
            copy.start()

        @pl.when(jnp.logical_not(recv_if))
        def _():
            dst[...] = jnp.zeros(dst.shape, dst.dtype)

        face_copies.append((send_if, recv_if, copy))


    chunks = [None, (0, 6), (6, planes), None]
    share = R // 2
    mine = pl.ds(pl.multiple_of((s % 2) * share, share), share)
    final = 3
    bufs = [p0, p1, p2, p3, p4]
    outs = []
    sent = []
    for r, (axis, stride, n) in enumerate(rounds):
        if r == 3:
            continue
        copies = []
        if r == 2:
            for dz in range(4):
                for dy in range(cross):
                    if dz == 0 and dy == 0:
                        continue
                    m = dz * cross + dy - 1
                    dev = (partner(s, 8, 4, dz), partner(c, 1, cross, dy))
                    copy = pltpu.make_async_remote_copy(
                        src_ref=bufs[r].at[mine], dst_ref=held2.at[m], send_sem=msends.at[m],
                        recv_sem=mrecvs.at[m], device_id=dev, device_id_type=MESH,
                    )
                    copy.start()
                    copies.append(copy)
                    if dy == 0:
                        rows = pl.ds(s - s % 8, 8)
                        block = pltpu.make_async_remote_copy(
                            src_ref=states_ref.at[rows], dst_ref=states_ref.at[rows],
                            send_sem=st_sends.at[r, dz - 1], recv_sem=st_recvs.at[r, dz - 1],
                            device_id=dev, device_id_type=MESH,
                        )
                        block.start()
                        copies.append(block)
        for j in range(1, n if r < 2 else 1):
            dev = device(axis, partner(here[axis], stride, n, j))
            copy = pltpu.make_async_remote_copy(
                src_ref=bufs[0] if r == 0 else bufs[r].at[mine],
                dst_ref=held.at[r, j - 1] if r == 0 else held.at[r, j - 1, pl.ds(0, share)],
                send_sem=sends.at[r, j - 1],
                recv_sem=recvs.at[r, j - 1],
                device_id=dev,
                device_id_type=MESH,
            )
            copy.start()
            copies.append(copy)
            if axis == 0:
                rows = pl.ds(s - s % stride, stride)
                block = pltpu.make_async_remote_copy(
                    src_ref=states_ref.at[rows],
                    dst_ref=states_ref.at[rows],
                    send_sem=st_sends.at[r, j - 1],
                    recv_sem=st_recvs.at[r, j - 1],
                    device_id=dev,
                    device_id_type=MESH,
                )
                block.start()
                copies.append(block)
        if r == 1:
            for send_if, recv_if, face in face_copies:


                @pl.when(recv_if)
                def _():
                    face.wait_recv()
        if chunks[r] is not None:
            first, last = chunks[r]

            def body(x, carry):
                results = stencil_plane(x, planes, vel_ref, xlo, xhi, ylo, yhi)
                for k in range(3):
                    adv_ref[k, x] = results[k]
                return carry

            lax.fori_loop(first, last, body, 0)
            out = pltpu.make_async_copy(
                adv_ref.at[pl.ds(1, 2), pl.ds(first, last - first)],
                adv_hbm.at[pl.ds(1, 2), pl.ds(first, last - first)],
                adv_sems.at[r - 1],
            )
            out.start()
            outs.append(out)
            if r == 2:
                pos, sub, slot, half = unpack(code_ref)
                entries = code_ref.shape[0]
                row_hot_ref[...] = (
                    (sub * R + slot) == lax.broadcasted_iota(jnp.int32, (entries, NSUB * R), 1)
                ).astype(jnp.bfloat16)
                pick_ref[...] = (pos == lax.broadcasted_iota(jnp.int32, (entries, planes * ny), 1)).astype(jnp.bfloat16)
        for copy in copies:
            copy.wait_recv()
        sent += copies
        if r == 2:

            def got(dz, dy):
                return bufs[r][mine, :] if dz == 0 and dy == 0 else held2[dz * cross + dy - 1]

            rows_sum = [(got(dz, 0) + got(dz, 2)) + (got(dz, 1) + got(dz, 3)) for dz in range(4)]
            bufs[r + 1][mine, :] = (rows_sum[0] + rows_sum[2]) + (rows_sum[1] + rows_sum[3])
        elif r == 0:
            bufs[r + 1][mine, :] = bufs[r][mine, :] + held[r, 0, mine, :]
        elif n == 2:
            bufs[r + 1][mine, :] = bufs[r][mine, :] + held[r, 0, pl.ds(0, share)]
        else:
            got = [held[r, k, pl.ds(0, share)] for k in range(3)]
            bufs[r + 1][mine, :] = (bufs[r][mine, :] + got[1]) + (got[0] + got[2])
    swap = pltpu.make_async_remote_copy(
        src_ref=bufs[final].at[mine],
        dst_ref=swap_ref,
        send_sem=swap_sems.at[0],
        recv_sem=swap_sems.at[1],
        device_id=(s + 1 - 2 * (s % 2), c),
        device_id_type=MESH,
    )
    swap.start()
    swap.wait()
    bufs[final][pl.ds(pl.multiple_of((1 - s % 2) * share, share), share), :] = swap_ref[...]

    pooled_b = (bufs[final][...] * pool_scale).astype(jnp.bfloat16)
    drive = jnp.dot(pooled_b, w_in_ref[...], preferred_element_type=jnp.float32)
    decay = decay_ref[...]
    for k in range(states_ref.shape[0]):
        row = states_ref[k]
        new_ref[pl.ds(k, 1), :] = row + state_step * (drive[k:k + 1] - decay * row)
    slot_rows = lax.broadcasted_iota(jnp.int32, drive.shape, 0)
    own_drive = jnp.sum(jnp.where(slot_rows == s, drive, 0.0), axis=0, keepdims=True)
    own = st_ref[...]
    own_ref[...] = own + state_step * (own_drive - decay * own)
    w_copy.wait()
    src = jnp.dot(
        new_ref[...].astype(jnp.bfloat16), w_out_ref[...], preferred_element_type=jnp.float32
    ).astype(jnp.bfloat16)
    place_forcing(src, code_ref, flat_ref, adv_ref, row_hot_ref, pick_ref)
    out = pltpu.make_async_copy(adv_ref.at[0], adv_hbm.at[0], adv_sems.at[len(rounds) - 1])
    out.start()
    outs.append(out)
    for out in outs:
        out.wait()
    for copy in sent:
        copy.wait_send()
    for send_if, recv_if, face in face_copies:

        @pl.when(send_if)
        def _():
            face.wait_send()

def reduce_step(code_parts, rotor_states, velocity, w_in, decay, w_out):
    slab, cross = lax.axis_size("slab"), lax.axis_size("cross")
    rounds = ring_rounds(slab, cross)
    vmem = pl.BlockSpec(memory_space=pltpu.VMEM)
    _, planes, ny, nz = velocity.shape
    return pl.pallas_call(
        lambda *refs: step_kernel(rounds, *refs),
        out_shape=(
            jax.ShapeDtypeStruct(rotor_states.shape, jnp.float32),
            jax.ShapeDtypeStruct(velocity.shape, jnp.float32),
        ),
        in_specs=[vmem] * 6 + [pl.BlockSpec(memory_space=pl.ANY)],
        out_specs=(vmem, pl.BlockSpec(memory_space=pl.ANY)),
        scratch_shapes=[
            pltpu.VMEM((slab,) + rotor_states.shape, jnp.float32),
            *[pltpu.VMEM((R, 3 * TILE), jnp.float32) for _ in range(len(rounds) + 1)],
            pltpu.VMEM((len(rounds), 3, R, 3 * TILE), jnp.float32),
            pltpu.SemaphoreType.DMA((len(rounds), 3)),
            pltpu.SemaphoreType.DMA((len(rounds), 3)),
            pltpu.SemaphoreType.DMA((len(rounds), 3)),
            pltpu.SemaphoreType.DMA((len(rounds), 3)),
            pltpu.VMEM((3, ny, nz), jnp.float32),
            pltpu.VMEM((3, ny, nz), jnp.float32),
            pltpu.VMEM((3, planes, 1, nz), jnp.float32),
            pltpu.VMEM((3, planes, 1, nz), jnp.float32),
            pltpu.SemaphoreType.DMA((4,)),
            pltpu.SemaphoreType.DMA((4,)),
            pltpu.VMEM(w_out.shape, w_out.dtype),
            pltpu.VMEM((slab, w_out.shape[0]), jnp.float32),
            pltpu.SemaphoreType.DMA(()),
            pltpu.VMEM((NSUB * R, TILE), jnp.bfloat16),
            pltpu.SemaphoreType.DMA((2,)),
            pltpu.VMEM((R // 2, 3 * TILE), jnp.float32),
            pltpu.VMEM(velocity.shape, jnp.float32),
            pltpu.SemaphoreType.DMA((len(rounds),)),
            pltpu.VMEM((code_parts[1].shape[0], NSUB * R), jnp.bfloat16),
            pltpu.VMEM((code_parts[1].shape[0], planes * ny), jnp.bfloat16),
            pltpu.VMEM((15, R // 2, 3 * TILE), jnp.float32),
            pltpu.SemaphoreType.DMA((15,)),
            pltpu.SemaphoreType.DMA((15,)),
        ],
        compiler_params=pltpu.CompilerParams(collective_id=0, has_side_effects=True),
    )(*code_parts, rotor_states, velocity, w_in, decay.reshape(1, -1), w_out)

def stencil_plane(x, planes, vel_ref, xlo_ref, xhi_ref, ylo_ref, yhi_ref):
    _, _, ny, nz = vel_ref.shape
    rows = lax.broadcasted_iota(jnp.int32, (ny, nz), 0)
    lanes = lax.broadcasted_iota(jnp.int32, (ny, nz), 1)
    here = [vel_ref[c, x] for c in range(3)]
    results = []
    for c in range(3):
        u = here[c]
        west = jnp.where(x == 0, xlo_ref[c].astype(jnp.float32), vel_ref[c, jnp.maximum(x - 1, 0)])
        east = jnp.where(x == planes - 1, xhi_ref[c].astype(jnp.float32), vel_ref[c, jnp.minimum(x + 1, planes - 1)])
        south = jnp.where(rows == 0, ylo_ref[c, x].astype(jnp.float32), pltpu.roll(u, 1, 0))
        north = jnp.where(rows == ny - 1, yhi_ref[c, x].astype(jnp.float32), pltpu.roll(u, ny - 1, 0))
        lower = jnp.where(lanes == 0, 0.0, pltpu.roll(u, 1, 1))
        upper = jnp.where(lanes == nz - 1, 0.0, pltpu.roll(u, nz - 1, 1))
        laplace = east + west + north + south + upper + lower - 6.0 * u
        advect = (
            here[0] * ((east - west) * 0.5)
            + here[1] * ((north - south) * 0.5)
            + here[2] * ((upper - lower) * 0.5)
        )
        results.append(u + time_step * (viscosity * laplace - advect))
    return results


def stencil_kernel(vel_ref, xlo_ref, xhi_ref, ylo_ref, yhi_ref, force_ref, out_ref):
    planes = vel_ref.shape[1]

    def body(x, carry):
        results = stencil_plane(x, planes, vel_ref, xlo_ref, xhi_ref, ylo_ref, yhi_ref)
        out_ref[0, x] = results[0] - force_scale * force_ref[x]
        out_ref[1, x] = results[1]
        out_ref[2, x] = results[2]
        return carry

    lax.fori_loop(0, planes, body, 0)


def stencil(velocity, halos, forcing):
    vmem = pl.BlockSpec(memory_space=pltpu.VMEM)
    return pl.pallas_call(
        stencil_kernel,
        out_shape=jax.ShapeDtypeStruct(velocity.shape, velocity.dtype),
        in_specs=[vmem] * 6,
        out_specs=vmem,
    )(velocity, *halos, forcing)


def halo_faces(velocity):
    faces = []
    for axis, dim in (("slab", 1), ("cross", 2)):
        count = lax.axis_size(axis)
        size = velocity.shape[dim]
        head = lax.slice_in_dim(velocity, 0, 1, axis=dim).astype(jnp.bfloat16)
        tail = lax.slice_in_dim(velocity, size - 1, size, axis=dim).astype(jnp.bfloat16)
        low = lax.ppermute(tail, axis, [(i, i + 1) for i in range(count - 1)])
        high = lax.ppermute(head, axis, [(i + 1, i) for i in range(count - 1)])
        faces += [jnp.squeeze(low, dim), jnp.squeeze(high, dim)] if dim == 1 else [low, high]
    return faces


def extended(cells, sides, width):
    for axis, dim in sides:
        count = lax.axis_size(axis)
        ends = count - 1
        head = lax.slice_in_dim(cells, 0, width, axis=dim)
        tail = lax.slice_in_dim(cells, cells.shape[dim] - width, cells.shape[dim], axis=dim)
        cells = jnp.concatenate(
            [
                lax.ppermute(tail, axis, [(i, (i + 1) % count) for i in range(ends)]),
                cells,
                lax.ppermute(head, axis, [((i + 1) % count, i) for i in range(ends)]),
            ],
            axis=dim,
        )
    return cells


def combine_terms(velocity, east, west, north, south, upper, lower):
    laplace = east + west + north + south + upper + lower - 6.0 * velocity
    advect = (
        velocity[0:1] * ((east - west) * 0.5)
        + velocity[1:2] * ((north - south) * 0.5)
        + velocity[2:3] * ((upper - lower) * 0.5)
    )
    return velocity + time_step * (viscosity * laplace - advect)


def on_device(
    velocity,
    shape_weight,
    w_in,
    w_out,
    decay,
    rotor_states,
    slot_of_rotor,
    entry_rotor,
    entry_tile,
    entry_sub,
):
    local_x, local_y, local_z = (velocity.shape[1], velocity.shape[2], velocity.shape[3])
    tile_count = local_x * local_y * local_z // TILE
    rotor_hot = (entry_rotor == jnp.arange(R, dtype=jnp.int32)[None, :]).astype(jnp.int32)
    slots = jnp.sum(rotor_hot * slot_of_rotor[None, :], axis=1)
    high = lax.reduce_precision(shape_weight, exponent_bits=8, mantissa_bits=7)
    rest = shape_weight - high
    middle = lax.reduce_precision(rest, exponent_bits=8, mantissa_bits=7)
    low = rest - middle
    parts = jnp.stack([high, middle, low]).astype(jnp.bfloat16)
    halves = local_z // TILE
    code = (((entry_tile // halves) * NSUB + entry_sub) * R + slots) * halves + entry_tile % halves
    new_states, advanced = reduce_step((parts, code[:, None]), rotor_states, velocity, w_in, decay, w_out)
    return (advanced, new_states)


def solution(mesh):
    in_specs = (
        P(None, "slab", "cross", None),
        P(),
        P(),
        P(),
        P(),
        P("slab", None),
        P(),
        P(("slab", "cross"), None),
        P(("slab", "cross")),
        P(("slab", "cross")),
    )
    out_specs = (P(None, "slab", "cross", None), P("slab", None))
    return jax.shard_map(
        on_device, mesh=mesh, in_specs=in_specs, out_specs=out_specs, check_vma=False
    )
```

```python
import jax
import jax.numpy as jnp
from jax import lax
from jax.experimental import pallas as pl
from jax.experimental.pallas import tpu as pltpu
from jax.sharding import PartitionSpec as P

MESH = pl.DeviceIdType.MESH

TILE = 128
R = 32
NSUB = 32


time_step = 0.1
viscosity = 0.3
pool_scale = 1.0 / 64.0
state_step = 0.5
force_scale = 0.5


def ring_perm(size, stride, n, shift):
    pairs = []
    for s in range(size):
        base = (s // (stride * n)) * stride * n + s % stride
        pos = (s // stride) % n
        pairs.append((s, base + ((pos + shift) % n) * stride))
    return pairs


def ring_sum(value, axis, stride, n):
    size = lax.axis_size(axis)
    if n == 2:
        return value + lax.ppermute(value, axis, ring_perm(size, stride, n, 1))
    got = [lax.ppermute(value, axis, ring_perm(size, stride, n, j)) for j in (1, 2, 3)]
    return (value + got[1]) + (got[0] + got[2])


def ring_gather(value, axis, stride, n):
    size = lax.axis_size(axis)
    pos = (lax.axis_index(axis) // stride) % n
    got = [value] + [lax.ppermute(value, axis, ring_perm(size, stride, n, j)) for j in range(1, n)]
    parts = []
    for p in range(n):
        pick = got[0]
        for j in range(1, n):
            pick = jnp.where((pos - j) % n == p, got[j], pick)
        parts.append(jnp.where(pos == p, got[0], pick))
    return jnp.concatenate(parts, axis=0)


def mesh_rings():
    slab = lax.axis_size("slab")
    rings = [("slab", 1, 2), ("slab", 2, 4), ("slab", 8, slab // 8)]
    return rings


def all_sum(value):
    for axis, stride, n in mesh_rings() + [("cross", 1, lax.axis_size("cross"))]:
        value = ring_sum(value, axis, stride, n)
    return value


def slab_gather(value):
    parts = value
    for axis, stride, n in mesh_rings():
        parts = ring_gather(parts, axis, stride, n)
    return parts


def ring_rounds(slab, cross):
    return [(0, 1, 2), (0, 2, 4), (0, 8, slab // 8), (1, 1, cross)]


def partner(me, stride, n, shift):
    pos = (me // stride) % n
    return me - pos * stride + ((pos + shift) % n) * stride


def unpack(code_ref):
    code = code_ref[...]
    half = code % 2
    slot = (code // 2) % R
    sub = (code // (2 * R)) % NSUB
    pos = code // (2 * R * NSUB)
    return pos, sub, slot, half


def pool_samples(vel_ref, parts_ref, code_ref):
    _, planes, ny, nz = vel_ref.shape
    entries = code_ref.shape[0]
    cells_xy = planes * ny
    pos, sub, slot, half = unpack(code_ref)
    sub_hot = (sub == lax.broadcasted_iota(jnp.int32, (entries, parts_ref.shape[1]), 1)).astype(jnp.bfloat16)
    gains = [jnp.dot(sub_hot, parts_ref[k], preferred_element_type=jnp.float32) for k in range(3)]
    gains = (gains[0] + gains[1]) + gains[2]
    pick_hot = (pos == lax.broadcasted_iota(jnp.int32, (entries, cells_xy), 1)).astype(jnp.bfloat16)
    slot_hot = (slot == lax.broadcasted_iota(jnp.int32, (entries, R), 1)).astype(jnp.float32)
    pooled = []
    for c in range(3):
        cells = vel_ref[c].reshape(cells_xy, nz).astype(jnp.bfloat16)
        both = jnp.dot(pick_hot, cells, preferred_element_type=jnp.float32)
        picked = both[:, :TILE]
        for h in range(1, nz // TILE):
            picked = jnp.where(half == h, both[:, h * TILE:(h + 1) * TILE], picked)
        weighted = gains[:, c * TILE:(c + 1) * TILE] * picked
        pooled.append(
            lax.dot_general(
                slot_hot, weighted, (((0,), (0,)), ((), ())),
                precision=lax.Precision.HIGHEST, preferred_element_type=jnp.float32,
            )
        )
    return pooled


def place_forcing(src, code_ref, flat_ref, adv_ref, row_hot_ref, pick_ref):
    _, planes, ny, nz = adv_ref.shape
    pos, sub, slot, half = unpack(code_ref)
    for j in range(NSUB):
        flat_ref[j * R:(j + 1) * R, :] = src[:, j * TILE:(j + 1) * TILE]
    rows = jnp.dot(row_hot_ref[...], flat_ref[...], preferred_element_type=jnp.float32)
    wide = jnp.concatenate(
        [jnp.where(half == h, rows, 0.0) for h in range(nz // TILE)], axis=1
    ).astype(jnp.bfloat16)
    pick_hot = pick_ref[...]
    forcing = lax.dot_general(pick_hot, wide, (((0,), (0,)), ((), ())), preferred_element_type=jnp.float32)
    adv_ref[0] = adv_ref[0] - force_scale * forcing.reshape(planes, ny, nz)

def step_kernel(rounds, parts_ref, code_ref, st_ref, vel_ref, w_in_ref, decay_ref,
                w_out_hbm, own_ref, adv_hbm,
                states_ref, p0, p1, p2, p3, p4, held, sends, recvs, st_sends, st_recvs, xlo, xhi, ylo, yhi, face_sends,
                face_recvs, w_out_ref, new_ref, w_sem, flat_ref, swap_sems, swap_ref, adv_ref, adv_sems, row_hot_ref, pick_ref, held2, msends, mrecvs):
    here = (lax.axis_index("slab"), lax.axis_index("cross"))
    slab, cross = lax.axis_size("slab"), lax.axis_size("cross")
    planes = vel_ref.shape[1]
    ny = vel_ref.shape[2]
    s, c = here

    def device(axis, other):
        return (other, here[1]) if axis == 0 else (here[0], other)

    extra = s - 1 + 2 * (s % 2)
    barrier = pltpu.get_barrier_semaphore()
    count = 0
    for axis, stride, n in rounds:
        for j in range(1, n):
            pl.semaphore_signal(barrier, inc=1, device_id=device(axis, partner(here[axis], stride, n, j)), device_id_type=MESH)
            count += 1
    pl.semaphore_signal(barrier, inc=1, device_id=((extra + slab) % slab, c), device_id_type=MESH)
    for dz in range(1, 4):
        for dy in range(1, cross):
            pl.semaphore_signal(barrier, inc=1, device_id=(partner(s, 8, 4, dz), partner(c, 1, cross, dy)), device_id_type=MESH)
            count += 1
    w_copy = pltpu.make_async_copy(w_out_hbm, w_out_ref, w_sem)
    w_copy.start()
    pooled = pool_samples(vel_ref, parts_ref, code_ref)
    for k in range(3):
        p0[:, k * TILE:(k + 1) * TILE] = pooled[k]
    states_ref[pl.ds(s, 1)] = st_ref[...][None]
    pl.semaphore_wait(barrier, count + 1)

    faces = [
        (s > 0, s < slab - 1, vel_ref.at[:, 0], xhi, ((s + slab - 1) % slab, c)),
        (s < slab - 1, s > 0, vel_ref.at[:, planes - 1], xlo, ((s + 1) % slab, c)),
        (c > 0, c < cross - 1, vel_ref.at[:, :, pl.ds(0, 1)], yhi, (s, (c + cross - 1) % cross)),
        (c < cross - 1, c > 0, vel_ref.at[:, :, pl.ds(ny - 1, 1)], ylo, (s, (c + 1) % cross)),
    ]
    face_copies = []
    for k, (send_if, recv_if, src, dst, dev) in enumerate(faces):
        copy = pltpu.make_async_remote_copy(
            src_ref=src, dst_ref=dst, send_sem=face_sends.at[k], recv_sem=face_recvs.at[k],
            device_id=dev, device_id_type=MESH,
        )

        @pl.when(send_if)
        def _():
            copy.start()

        @pl.when(jnp.logical_not(recv_if))
        def _():
            dst[...] = jnp.zeros(dst.shape, dst.dtype)

        face_copies.append((send_if, recv_if, copy))


    chunks = [None, (0, planes // 2), (planes // 2, planes), None]
    share = R // 2
    mine = pl.ds(pl.multiple_of((s % 2) * share, share), share)
    final = 3
    bufs = [p0, p1, p2, p3, p4]
    outs = []
    sent = []
    for r, (axis, stride, n) in enumerate(rounds):
        if r == 3:
            continue
        copies = []
        if r == 2:
            for dz in range(4):
                for dy in range(cross):
                    if dz == 0 and dy == 0:
                        continue
                    m = dz * cross + dy - 1
                    dev = (partner(s, 8, 4, dz), partner(c, 1, cross, dy))
                    copy = pltpu.make_async_remote_copy(
                        src_ref=bufs[r].at[mine], dst_ref=held2.at[m], send_sem=msends.at[m],
                        recv_sem=mrecvs.at[m], device_id=dev, device_id_type=MESH,
                    )
                    copy.start()
                    copies.append(copy)
                    if dy == 0:
                        rows = pl.ds(s - s % 8, 8)
                        block = pltpu.make_async_remote_copy(
                            src_ref=states_ref.at[rows], dst_ref=states_ref.at[rows],
                            send_sem=st_sends.at[r, dz - 1], recv_sem=st_recvs.at[r, dz - 1],
                            device_id=dev, device_id_type=MESH,
                        )
                        block.start()
                        copies.append(block)
        for j in range(1, n if r < 2 else 1):
            dev = device(axis, partner(here[axis], stride, n, j))
            copy = pltpu.make_async_remote_copy(
                src_ref=bufs[0] if r == 0 else bufs[r].at[mine],
                dst_ref=held.at[r, j - 1] if r == 0 else held.at[r, j - 1, pl.ds(0, share)],
                send_sem=sends.at[r, j - 1],
                recv_sem=recvs.at[r, j - 1],
                device_id=dev,
                device_id_type=MESH,
            )
            copy.start()
            copies.append(copy)
            if axis == 0:
                rows = pl.ds(s - s % stride, stride)
                block = pltpu.make_async_remote_copy(
                    src_ref=states_ref.at[rows],
                    dst_ref=states_ref.at[rows],
                    send_sem=st_sends.at[r, j - 1],
                    recv_sem=st_recvs.at[r, j - 1],
                    device_id=dev,
                    device_id_type=MESH,
                )
                block.start()
                copies.append(block)
        if r == 1:
            for send_if, recv_if, face in face_copies:


                @pl.when(recv_if)
                def _():
                    face.wait_recv()
        if chunks[r] is not None:
            first, last = chunks[r]

            def body(x, carry):
                results = stencil_plane(x, planes, vel_ref, xlo, xhi, ylo, yhi)
                for k in range(3):
                    adv_ref[k, x] = results[k]
                return carry

            lax.fori_loop(first, last, body, 0)
            out = pltpu.make_async_copy(
                adv_ref.at[pl.ds(1, 2), pl.ds(first, last - first)],
                adv_hbm.at[pl.ds(1, 2), pl.ds(first, last - first)],
                adv_sems.at[r - 1],
            )
            out.start()
            outs.append(out)
            if r == 2:
                pos, sub, slot, half = unpack(code_ref)
                entries = code_ref.shape[0]
                row_hot_ref[...] = (
                    (sub * R + slot) == lax.broadcasted_iota(jnp.int32, (entries, NSUB * R), 1)
                ).astype(jnp.bfloat16)
                pick_ref[...] = (pos == lax.broadcasted_iota(jnp.int32, (entries, planes * ny), 1)).astype(jnp.bfloat16)
        for copy in copies:
            copy.wait_recv()
        sent += copies
        if r == 2:

            def got(dz, dy):
                return bufs[r][mine, :] if dz == 0 and dy == 0 else held2[dz * cross + dy - 1]

            rows_sum = [(got(dz, 0) + got(dz, 2)) + (got(dz, 1) + got(dz, 3)) for dz in range(4)]
            bufs[r + 1][mine, :] = (rows_sum[0] + rows_sum[2]) + (rows_sum[1] + rows_sum[3])
        elif r == 0:
            bufs[r + 1][mine, :] = bufs[r][mine, :] + held[r, 0, mine, :]
        elif n == 2:
            bufs[r + 1][mine, :] = bufs[r][mine, :] + held[r, 0, pl.ds(0, share)]
        else:
            got = [held[r, k, pl.ds(0, share)] for k in range(3)]
            bufs[r + 1][mine, :] = (bufs[r][mine, :] + got[1]) + (got[0] + got[2])
    swap = pltpu.make_async_remote_copy(
        src_ref=bufs[final].at[mine],
        dst_ref=swap_ref,
        send_sem=swap_sems.at[0],
        recv_sem=swap_sems.at[1],
        device_id=(s + 1 - 2 * (s % 2), c),
        device_id_type=MESH,
    )
    swap.start()
    swap.wait()
    bufs[final][pl.ds(pl.multiple_of((1 - s % 2) * share, share), share), :] = swap_ref[...]

    pooled_b = (bufs[final][...] * pool_scale).astype(jnp.bfloat16)
    drive = jnp.dot(pooled_b, w_in_ref[...], preferred_element_type=jnp.float32)
    decay = decay_ref[...]
    for k in range(states_ref.shape[0]):
        row = states_ref[k]
        new_ref[pl.ds(k, 1), :] = row + state_step * (drive[k:k + 1] - decay * row)
    slot_rows = lax.broadcasted_iota(jnp.int32, drive.shape, 0)
    own_drive = jnp.sum(jnp.where(slot_rows == s, drive, 0.0), axis=0, keepdims=True)
    own = st_ref[...]
    own_ref[...] = own + state_step * (own_drive - decay * own)
    w_copy.wait()
    src = jnp.dot(
        new_ref[...].astype(jnp.bfloat16), w_out_ref[...], preferred_element_type=jnp.float32
    ).astype(jnp.bfloat16)
    place_forcing(src, code_ref, flat_ref, adv_ref, row_hot_ref, pick_ref)
    out = pltpu.make_async_copy(adv_ref.at[0], adv_hbm.at[0], adv_sems.at[len(rounds) - 1])
    out.start()
    outs.append(out)
    for out in outs:
        out.wait()
    for copy in sent:
        copy.wait_send()
    for send_if, recv_if, face in face_copies:

        @pl.when(send_if)
        def _():
            face.wait_send()

def reduce_step(code_parts, rotor_states, velocity, w_in, decay, w_out):
    slab, cross = lax.axis_size("slab"), lax.axis_size("cross")
    rounds = ring_rounds(slab, cross)
    vmem = pl.BlockSpec(memory_space=pltpu.VMEM)
    _, planes, ny, nz = velocity.shape
    return pl.pallas_call(
        lambda *refs: step_kernel(rounds, *refs),
        out_shape=(
            jax.ShapeDtypeStruct(rotor_states.shape, jnp.float32),
            jax.ShapeDtypeStruct(velocity.shape, jnp.float32),
        ),
        in_specs=[vmem] * 6 + [pl.BlockSpec(memory_space=pl.ANY)],
        out_specs=(vmem, pl.BlockSpec(memory_space=pl.ANY)),
        scratch_shapes=[
            pltpu.VMEM((slab,) + rotor_states.shape, jnp.float32),
            *[pltpu.VMEM((R, 3 * TILE), jnp.float32) for _ in range(len(rounds) + 1)],
            pltpu.VMEM((len(rounds), 3, R, 3 * TILE), jnp.float32),
            pltpu.SemaphoreType.DMA((len(rounds), 3)),
            pltpu.SemaphoreType.DMA((len(rounds), 3)),
            pltpu.SemaphoreType.DMA((len(rounds), 3)),
            pltpu.SemaphoreType.DMA((len(rounds), 3)),
            pltpu.VMEM((3, ny, nz), jnp.float32),
            pltpu.VMEM((3, ny, nz), jnp.float32),
            pltpu.VMEM((3, planes, 1, nz), jnp.float32),
            pltpu.VMEM((3, planes, 1, nz), jnp.float32),
            pltpu.SemaphoreType.DMA((4,)),
            pltpu.SemaphoreType.DMA((4,)),
            pltpu.VMEM(w_out.shape, w_out.dtype),
            pltpu.VMEM((slab, w_out.shape[0]), jnp.float32),
            pltpu.SemaphoreType.DMA(()),
            pltpu.VMEM((NSUB * R, TILE), jnp.bfloat16),
            pltpu.SemaphoreType.DMA((2,)),
            pltpu.VMEM((R // 2, 3 * TILE), jnp.float32),
            pltpu.VMEM(velocity.shape, jnp.float32),
            pltpu.SemaphoreType.DMA((len(rounds),)),
            pltpu.VMEM((code_parts[1].shape[0], NSUB * R), jnp.bfloat16),
            pltpu.VMEM((code_parts[1].shape[0], planes * ny), jnp.bfloat16),
            pltpu.VMEM((15, R // 2, 3 * TILE), jnp.float32),
            pltpu.SemaphoreType.DMA((15,)),
            pltpu.SemaphoreType.DMA((15,)),
        ],
        compiler_params=pltpu.CompilerParams(collective_id=0, has_side_effects=True),
    )(*code_parts, rotor_states, velocity, w_in, decay.reshape(1, -1), w_out)

def stencil_plane(x, planes, vel_ref, xlo_ref, xhi_ref, ylo_ref, yhi_ref):
    _, _, ny, nz = vel_ref.shape
    rows = lax.broadcasted_iota(jnp.int32, (ny, nz), 0)
    lanes = lax.broadcasted_iota(jnp.int32, (ny, nz), 1)
    here = [vel_ref[c, x] for c in range(3)]
    results = []
    for c in range(3):
        u = here[c]
        west = jnp.where(x == 0, xlo_ref[c].astype(jnp.float32), vel_ref[c, jnp.maximum(x - 1, 0)])
        east = jnp.where(x == planes - 1, xhi_ref[c].astype(jnp.float32), vel_ref[c, jnp.minimum(x + 1, planes - 1)])
        south = jnp.where(rows == 0, ylo_ref[c, x].astype(jnp.float32), pltpu.roll(u, 1, 0))
        north = jnp.where(rows == ny - 1, yhi_ref[c, x].astype(jnp.float32), pltpu.roll(u, ny - 1, 0))
        lower = jnp.where(lanes == 0, 0.0, pltpu.roll(u, 1, 1))
        upper = jnp.where(lanes == nz - 1, 0.0, pltpu.roll(u, nz - 1, 1))
        laplace = east + west + north + south + upper + lower - 6.0 * u
        advect = (
            here[0] * ((east - west) * 0.5)
            + here[1] * ((north - south) * 0.5)
            + here[2] * ((upper - lower) * 0.5)
        )
        results.append(u + time_step * (viscosity * laplace - advect))
    return results


def stencil_kernel(vel_ref, xlo_ref, xhi_ref, ylo_ref, yhi_ref, force_ref, out_ref):
    planes = vel_ref.shape[1]

    def body(x, carry):
        results = stencil_plane(x, planes, vel_ref, xlo_ref, xhi_ref, ylo_ref, yhi_ref)
        out_ref[0, x] = results[0] - force_scale * force_ref[x]
        out_ref[1, x] = results[1]
        out_ref[2, x] = results[2]
        return carry

    lax.fori_loop(0, planes, body, 0)


def stencil(velocity, halos, forcing):
    vmem = pl.BlockSpec(memory_space=pltpu.VMEM)
    return pl.pallas_call(
        stencil_kernel,
        out_shape=jax.ShapeDtypeStruct(velocity.shape, velocity.dtype),
        in_specs=[vmem] * 6,
        out_specs=vmem,
    )(velocity, *halos, forcing)


def halo_faces(velocity):
    faces = []
    for axis, dim in (("slab", 1), ("cross", 2)):
        count = lax.axis_size(axis)
        size = velocity.shape[dim]
        head = lax.slice_in_dim(velocity, 0, 1, axis=dim).astype(jnp.bfloat16)
        tail = lax.slice_in_dim(velocity, size - 1, size, axis=dim).astype(jnp.bfloat16)
        low = lax.ppermute(tail, axis, [(i, i + 1) for i in range(count - 1)])
        high = lax.ppermute(head, axis, [(i + 1, i) for i in range(count - 1)])
        faces += [jnp.squeeze(low, dim), jnp.squeeze(high, dim)] if dim == 1 else [low, high]
    return faces


def extended(cells, sides, width):
    for axis, dim in sides:
        count = lax.axis_size(axis)
        ends = count - 1
        head = lax.slice_in_dim(cells, 0, width, axis=dim)
        tail = lax.slice_in_dim(cells, cells.shape[dim] - width, cells.shape[dim], axis=dim)
        cells = jnp.concatenate(
            [
                lax.ppermute(tail, axis, [(i, (i + 1) % count) for i in range(ends)]),
                cells,
                lax.ppermute(head, axis, [((i + 1) % count, i) for i in range(ends)]),
            ],
            axis=dim,
        )
    return cells


def combine_terms(velocity, east, west, north, south, upper, lower):
    laplace = east + west + north + south + upper + lower - 6.0 * velocity
    advect = (
        velocity[0:1] * ((east - west) * 0.5)
        + velocity[1:2] * ((north - south) * 0.5)
        + velocity[2:3] * ((upper - lower) * 0.5)
    )
    return velocity + time_step * (viscosity * laplace - advect)


def on_device(
    velocity,
    shape_weight,
    w_in,
    w_out,
    decay,
    rotor_states,
    slot_of_rotor,
    entry_rotor,
    entry_tile,
    entry_sub,
):
    local_x, local_y, local_z = (velocity.shape[1], velocity.shape[2], velocity.shape[3])
    tile_count = local_x * local_y * local_z // TILE
    rotor_hot = (entry_rotor == jnp.arange(R, dtype=jnp.int32)[None, :]).astype(jnp.int32)
    slots = jnp.sum(rotor_hot * slot_of_rotor[None, :], axis=1)
    high = lax.reduce_precision(shape_weight, exponent_bits=8, mantissa_bits=7)
    rest = shape_weight - high
    middle = lax.reduce_precision(rest, exponent_bits=8, mantissa_bits=7)
    low = rest - middle
    parts = jnp.stack([high, middle, low]).astype(jnp.bfloat16)
    halves = local_z // TILE
    code = (((entry_tile // halves) * NSUB + entry_sub) * R + slots) * halves + entry_tile % halves
    new_states, advanced = reduce_step((parts, code[:, None]), rotor_states, velocity, w_in, decay, w_out)
    return (advanced, new_states)


def solution(mesh):
    in_specs = (
        P(None, "slab", "cross", None),
        P(),
        P(),
        P(),
        P(),
        P("slab", None),
        P(),
        P(("slab", "cross"), None),
        P(("slab", "cross")),
        P(("slab", "cross")),
    )
    out_specs = (P(None, "slab", "cross", None), P("slab", None))
    return jax.shard_map(
        on_device, mesh=mesh, in_specs=in_specs, out_specs=out_specs, check_vma=False
    )
```

```python
import jax
import jax.numpy as jnp
from jax import lax
from jax.experimental import pallas as pl
from jax.experimental.pallas import tpu as pltpu
from jax.sharding import PartitionSpec as P

MESH = pl.DeviceIdType.MESH

TILE = 128
R = 32
NSUB = 32


time_step = 0.1
viscosity = 0.3
pool_scale = 1.0 / 64.0
state_step = 0.5
force_scale = 0.5


def ring_perm(size, stride, n, shift):
    pairs = []
    for s in range(size):
        base = (s // (stride * n)) * stride * n + s % stride
        pos = (s // stride) % n
        pairs.append((s, base + ((pos + shift) % n) * stride))
    return pairs


def ring_sum(value, axis, stride, n):
    size = lax.axis_size(axis)
    if n == 2:
        return value + lax.ppermute(value, axis, ring_perm(size, stride, n, 1))
    got = [lax.ppermute(value, axis, ring_perm(size, stride, n, j)) for j in (1, 2, 3)]
    return (value + got[1]) + (got[0] + got[2])


def ring_gather(value, axis, stride, n):
    size = lax.axis_size(axis)
    pos = (lax.axis_index(axis) // stride) % n
    got = [value] + [lax.ppermute(value, axis, ring_perm(size, stride, n, j)) for j in range(1, n)]
    parts = []
    for p in range(n):
        pick = got[0]
        for j in range(1, n):
            pick = jnp.where((pos - j) % n == p, got[j], pick)
        parts.append(jnp.where(pos == p, got[0], pick))
    return jnp.concatenate(parts, axis=0)


def mesh_rings():
    slab = lax.axis_size("slab")
    rings = [("slab", 1, 2), ("slab", 2, 4), ("slab", 8, slab // 8)]
    return rings


def all_sum(value):
    for axis, stride, n in mesh_rings() + [("cross", 1, lax.axis_size("cross"))]:
        value = ring_sum(value, axis, stride, n)
    return value


def slab_gather(value):
    parts = value
    for axis, stride, n in mesh_rings():
        parts = ring_gather(parts, axis, stride, n)
    return parts


def ring_rounds(slab, cross):
    return [(0, 1, 2), (0, 2, 4), (0, 8, slab // 8), (1, 1, cross)]


def partner(me, stride, n, shift):
    pos = (me // stride) % n
    return me - pos * stride + ((pos + shift) % n) * stride


def unpack(code_ref):
    code = code_ref[...]
    half = code % 2
    slot = (code // 2) % R
    sub = (code // (2 * R)) % NSUB
    pos = code // (2 * R * NSUB)
    return pos, sub, slot, half


def pool_samples(vel_ref, parts_ref, code_ref):
    _, planes, ny, nz = vel_ref.shape
    entries = code_ref.shape[0]
    cells_xy = planes * ny
    pos, sub, slot, half = unpack(code_ref)
    sub_hot = (sub == lax.broadcasted_iota(jnp.int32, (entries, parts_ref.shape[1]), 1)).astype(jnp.bfloat16)
    gains = [jnp.dot(sub_hot, parts_ref[k], preferred_element_type=jnp.float32) for k in range(3)]
    gains = (gains[0] + gains[1]) + gains[2]
    pick_hot = (pos == lax.broadcasted_iota(jnp.int32, (entries, cells_xy), 1)).astype(jnp.bfloat16)
    slot_hot = (slot == lax.broadcasted_iota(jnp.int32, (entries, R), 1)).astype(jnp.float32)
    pooled = []
    for c in range(3):
        cells = vel_ref[c].reshape(cells_xy, nz).astype(jnp.bfloat16)
        both = jnp.dot(pick_hot, cells, preferred_element_type=jnp.float32)
        picked = both[:, :TILE]
        for h in range(1, nz // TILE):
            picked = jnp.where(half == h, both[:, h * TILE:(h + 1) * TILE], picked)
        weighted = gains[:, c * TILE:(c + 1) * TILE] * picked
        pooled.append(
            lax.dot_general(
                slot_hot, weighted, (((0,), (0,)), ((), ())),
                precision=lax.Precision.HIGHEST, preferred_element_type=jnp.float32,
            )
        )
    return pooled


def place_forcing(src, code_ref, flat_ref, adv_ref, row_hot_ref, pick_ref):
    _, planes, ny, nz = adv_ref.shape
    pos, sub, slot, half = unpack(code_ref)
    for j in range(NSUB):
        flat_ref[j * R:(j + 1) * R, :] = src[:, j * TILE:(j + 1) * TILE]
    rows = jnp.dot(row_hot_ref[...], flat_ref[...], preferred_element_type=jnp.float32)
    wide = jnp.concatenate(
        [jnp.where(half == h, rows, 0.0) for h in range(nz // TILE)], axis=1
    ).astype(jnp.bfloat16)
    pick_hot = pick_ref[...]
    forcing = lax.dot_general(pick_hot, wide, (((0,), (0,)), ((), ())), preferred_element_type=jnp.float32)
    adv_ref[0] = adv_ref[0] - force_scale * forcing.reshape(planes, ny, nz)

def step_kernel(rounds, parts_ref, code_ref, st_ref, vel_ref, w_in_ref, decay_ref,
                w_out_hbm, own_ref, adv_hbm,
                states_ref, p0, p1, p2, p3, p4, held, sends, recvs, st_sends, st_recvs, xlo, xhi, ylo, yhi, face_sends,
                face_recvs, w_out_ref, new_ref, w_sem, flat_ref, swap_sems, swap_ref, adv_ref, adv_sems, row_hot_ref, pick_ref, held2, msends, mrecvs):
    here = (lax.axis_index("slab"), lax.axis_index("cross"))
    slab, cross = lax.axis_size("slab"), lax.axis_size("cross")
    planes = vel_ref.shape[1]
    ny = vel_ref.shape[2]
    s, c = here

    def device(axis, other):
        return (other, here[1]) if axis == 0 else (here[0], other)

    extra = s - 1 + 2 * (s % 2)
    barrier = pltpu.get_barrier_semaphore()
    count = 0
    for axis, stride, n in rounds:
        for j in range(1, n):
            pl.semaphore_signal(barrier, inc=1, device_id=device(axis, partner(here[axis], stride, n, j)), device_id_type=MESH)
            count += 1
    pl.semaphore_signal(barrier, inc=1, device_id=((extra + slab) % slab, c), device_id_type=MESH)
    for dz in range(1, 4):
        for dy in range(1, cross):
            pl.semaphore_signal(barrier, inc=1, device_id=(partner(s, 8, 4, dz), partner(c, 1, cross, dy)), device_id_type=MESH)
            count += 1
    w_copy = pltpu.make_async_copy(w_out_hbm, w_out_ref, w_sem)
    w_copy.start()
    pooled = pool_samples(vel_ref, parts_ref, code_ref)
    for k in range(3):
        p0[:, k * TILE:(k + 1) * TILE] = pooled[k]
    states_ref[pl.ds(s, 1)] = st_ref[...][None]
    pl.semaphore_wait(barrier, count + 1)

    faces = [
        (s > 0, s < slab - 1, vel_ref.at[:, 0], xhi, ((s + slab - 1) % slab, c)),
        (s < slab - 1, s > 0, vel_ref.at[:, planes - 1], xlo, ((s + 1) % slab, c)),
        (c > 0, c < cross - 1, vel_ref.at[:, :, pl.ds(0, 1)], yhi, (s, (c + cross - 1) % cross)),
        (c < cross - 1, c > 0, vel_ref.at[:, :, pl.ds(ny - 1, 1)], ylo, (s, (c + 1) % cross)),
    ]
    face_copies = []
    for k, (send_if, recv_if, src, dst, dev) in enumerate(faces):
        copy = pltpu.make_async_remote_copy(
            src_ref=src, dst_ref=dst, send_sem=face_sends.at[k], recv_sem=face_recvs.at[k],
            device_id=dev, device_id_type=MESH,
        )

        @pl.when(send_if)
        def _():
            copy.start()

        @pl.when(jnp.logical_not(recv_if))
        def _():
            dst[...] = jnp.zeros(dst.shape, dst.dtype)

        face_copies.append((send_if, recv_if, copy))


    chunks = [None, (0, planes // 2), (planes // 2, planes), None]
    share = R // 2
    mine = pl.ds(pl.multiple_of((s % 2) * share, share), share)
    final = 3
    bufs = [p0, p1, p2, p3, p4]
    outs = []
    sent = []
    for r, (axis, stride, n) in enumerate(rounds):
        if r == 3:
            continue
        copies = []
        if r == 2:
            for dz in range(4):
                for dy in range(cross):
                    if dz == 0 and dy == 0:
                        continue
                    m = dz * cross + dy - 1
                    dev = (partner(s, 8, 4, dz), partner(c, 1, cross, dy))
                    copy = pltpu.make_async_remote_copy(
                        src_ref=bufs[r].at[mine], dst_ref=held2.at[m], send_sem=msends.at[m],
                        recv_sem=mrecvs.at[m], device_id=dev, device_id_type=MESH,
                    )
                    copy.start()
                    copies.append(copy)
                    if dy == 0:
                        rows = pl.ds(s - s % 8, 8)
                        block = pltpu.make_async_remote_copy(
                            src_ref=states_ref.at[rows], dst_ref=states_ref.at[rows],
                            send_sem=st_sends.at[r, dz - 1], recv_sem=st_recvs.at[r, dz - 1],
                            device_id=dev, device_id_type=MESH,
                        )
                        block.start()
                        copies.append(block)
        for j in range(1, n if r < 2 else 1):
            dev = device(axis, partner(here[axis], stride, n, j))
            copy = pltpu.make_async_remote_copy(
                src_ref=bufs[0] if r == 0 else bufs[r].at[mine],
                dst_ref=held.at[r, j - 1] if r == 0 else held.at[r, j - 1, pl.ds(0, share)],
                send_sem=sends.at[r, j - 1],
                recv_sem=recvs.at[r, j - 1],
                device_id=dev,
                device_id_type=MESH,
            )
            copy.start()
            copies.append(copy)
            if axis == 0:
                rows = pl.ds(s - s % stride, stride)
                block = pltpu.make_async_remote_copy(
                    src_ref=states_ref.at[rows],
                    dst_ref=states_ref.at[rows],
                    send_sem=st_sends.at[r, j - 1],
                    recv_sem=st_recvs.at[r, j - 1],
                    device_id=dev,
                    device_id_type=MESH,
                )
                block.start()
                copies.append(block)
        if r == 0:
            pos, sub, slot, half = unpack(code_ref)
            entries = code_ref.shape[0]
            row_hot_ref[...] = (
                (sub * R + slot) == lax.broadcasted_iota(jnp.int32, (entries, NSUB * R), 1)
            ).astype(jnp.bfloat16)
            pick_ref[...] = (pos == lax.broadcasted_iota(jnp.int32, (entries, planes * ny), 1)).astype(jnp.bfloat16)
        if r == 1:
            for send_if, recv_if, face in face_copies:


                @pl.when(recv_if)
                def _():
                    face.wait_recv()
        if chunks[r] is not None:
            first, last = chunks[r]

            def body(x, carry):
                results = stencil_plane(x, planes, vel_ref, xlo, xhi, ylo, yhi)
                for k in range(3):
                    adv_ref[k, x] = results[k]
                return carry

            lax.fori_loop(first, last, body, 0)
            out = pltpu.make_async_copy(
                adv_ref.at[pl.ds(1, 2), pl.ds(first, last - first)],
                adv_hbm.at[pl.ds(1, 2), pl.ds(first, last - first)],
                adv_sems.at[r - 1],
            )
            out.start()
            outs.append(out)
        for copy in copies:
            copy.wait_recv()
        sent += copies
        if r == 2:

            def got(dz, dy):
                return bufs[r][mine, :] if dz == 0 and dy == 0 else held2[dz * cross + dy - 1]

            rows_sum = [(got(dz, 0) + got(dz, 2)) + (got(dz, 1) + got(dz, 3)) for dz in range(4)]
            bufs[r + 1][mine, :] = (rows_sum[0] + rows_sum[2]) + (rows_sum[1] + rows_sum[3])
        elif r == 0:
            bufs[r + 1][mine, :] = bufs[r][mine, :] + held[r, 0, mine, :]
        elif n == 2:
            bufs[r + 1][mine, :] = bufs[r][mine, :] + held[r, 0, pl.ds(0, share)]
        else:
            got = [held[r, k, pl.ds(0, share)] for k in range(3)]
            bufs[r + 1][mine, :] = (bufs[r][mine, :] + got[1]) + (got[0] + got[2])
    swap = pltpu.make_async_remote_copy(
        src_ref=bufs[final].at[mine],
        dst_ref=swap_ref,
        send_sem=swap_sems.at[0],
        recv_sem=swap_sems.at[1],
        device_id=(s + 1 - 2 * (s % 2), c),
        device_id_type=MESH,
    )
    swap.start()
    swap.wait()
    bufs[final][pl.ds(pl.multiple_of((1 - s % 2) * share, share), share), :] = swap_ref[...]

    pooled_b = (bufs[final][...] * pool_scale).astype(jnp.bfloat16)
    drive = jnp.dot(pooled_b, w_in_ref[...], preferred_element_type=jnp.float32)
    decay = decay_ref[...]
    for k in range(states_ref.shape[0]):
        row = states_ref[k]
        new_ref[pl.ds(k, 1), :] = row + state_step * (drive[k:k + 1] - decay * row)
    slot_rows = lax.broadcasted_iota(jnp.int32, drive.shape, 0)
    own_drive = jnp.sum(jnp.where(slot_rows == s, drive, 0.0), axis=0, keepdims=True)
    own = st_ref[...]
    own_ref[...] = own + state_step * (own_drive - decay * own)
    w_copy.wait()
    src = jnp.dot(
        new_ref[...].astype(jnp.bfloat16), w_out_ref[...], preferred_element_type=jnp.float32
    ).astype(jnp.bfloat16)
    place_forcing(src, code_ref, flat_ref, adv_ref, row_hot_ref, pick_ref)
    out = pltpu.make_async_copy(adv_ref.at[0], adv_hbm.at[0], adv_sems.at[len(rounds) - 1])
    out.start()
    outs.append(out)
    for out in outs:
        out.wait()
    for copy in sent:
        copy.wait_send()
    for send_if, recv_if, face in face_copies:

        @pl.when(send_if)
        def _():
            face.wait_send()

def reduce_step(code_parts, rotor_states, velocity, w_in, decay, w_out):
    slab, cross = lax.axis_size("slab"), lax.axis_size("cross")
    rounds = ring_rounds(slab, cross)
    vmem = pl.BlockSpec(memory_space=pltpu.VMEM)
    _, planes, ny, nz = velocity.shape
    return pl.pallas_call(
        lambda *refs: step_kernel(rounds, *refs),
        out_shape=(
            jax.ShapeDtypeStruct(rotor_states.shape, jnp.float32),
            jax.ShapeDtypeStruct(velocity.shape, jnp.float32),
        ),
        in_specs=[vmem] * 6 + [pl.BlockSpec(memory_space=pl.ANY)],
        out_specs=(vmem, pl.BlockSpec(memory_space=pl.ANY)),
        scratch_shapes=[
            pltpu.VMEM((slab,) + rotor_states.shape, jnp.float32),
            *[pltpu.VMEM((R, 3 * TILE), jnp.float32) for _ in range(len(rounds) + 1)],
            pltpu.VMEM((len(rounds), 3, R, 3 * TILE), jnp.float32),
            pltpu.SemaphoreType.DMA((len(rounds), 3)),
            pltpu.SemaphoreType.DMA((len(rounds), 3)),
            pltpu.SemaphoreType.DMA((len(rounds), 3)),
            pltpu.SemaphoreType.DMA((len(rounds), 3)),
            pltpu.VMEM((3, ny, nz), jnp.float32),
            pltpu.VMEM((3, ny, nz), jnp.float32),
            pltpu.VMEM((3, planes, 1, nz), jnp.float32),
            pltpu.VMEM((3, planes, 1, nz), jnp.float32),
            pltpu.SemaphoreType.DMA((4,)),
            pltpu.SemaphoreType.DMA((4,)),
            pltpu.VMEM(w_out.shape, w_out.dtype),
            pltpu.VMEM((slab, w_out.shape[0]), jnp.float32),
            pltpu.SemaphoreType.DMA(()),
            pltpu.VMEM((NSUB * R, TILE), jnp.bfloat16),
            pltpu.SemaphoreType.DMA((2,)),
            pltpu.VMEM((R // 2, 3 * TILE), jnp.float32),
            pltpu.VMEM(velocity.shape, jnp.float32),
            pltpu.SemaphoreType.DMA((len(rounds),)),
            pltpu.VMEM((code_parts[1].shape[0], NSUB * R), jnp.bfloat16),
            pltpu.VMEM((code_parts[1].shape[0], planes * ny), jnp.bfloat16),
            pltpu.VMEM((15, R // 2, 3 * TILE), jnp.float32),
            pltpu.SemaphoreType.DMA((15,)),
            pltpu.SemaphoreType.DMA((15,)),
        ],
        compiler_params=pltpu.CompilerParams(collective_id=0, has_side_effects=True),
    )(*code_parts, rotor_states, velocity, w_in, decay.reshape(1, -1), w_out)

def stencil_plane(x, planes, vel_ref, xlo_ref, xhi_ref, ylo_ref, yhi_ref):
    _, _, ny, nz = vel_ref.shape
    rows = lax.broadcasted_iota(jnp.int32, (ny, nz), 0)
    lanes = lax.broadcasted_iota(jnp.int32, (ny, nz), 1)
    here = [vel_ref[c, x] for c in range(3)]
    results = []
    for c in range(3):
        u = here[c]
        west = jnp.where(x == 0, xlo_ref[c].astype(jnp.float32), vel_ref[c, jnp.maximum(x - 1, 0)])
        east = jnp.where(x == planes - 1, xhi_ref[c].astype(jnp.float32), vel_ref[c, jnp.minimum(x + 1, planes - 1)])
        south = jnp.where(rows == 0, ylo_ref[c, x].astype(jnp.float32), pltpu.roll(u, 1, 0))
        north = jnp.where(rows == ny - 1, yhi_ref[c, x].astype(jnp.float32), pltpu.roll(u, ny - 1, 0))
        lower = jnp.where(lanes == 0, 0.0, pltpu.roll(u, 1, 1))
        upper = jnp.where(lanes == nz - 1, 0.0, pltpu.roll(u, nz - 1, 1))
        laplace = east + west + north + south + upper + lower - 6.0 * u
        advect = (
            here[0] * ((east - west) * 0.5)
            + here[1] * ((north - south) * 0.5)
            + here[2] * ((upper - lower) * 0.5)
        )
        results.append(u + time_step * (viscosity * laplace - advect))
    return results


def stencil_kernel(vel_ref, xlo_ref, xhi_ref, ylo_ref, yhi_ref, force_ref, out_ref):
    planes = vel_ref.shape[1]

    def body(x, carry):
        results = stencil_plane(x, planes, vel_ref, xlo_ref, xhi_ref, ylo_ref, yhi_ref)
        out_ref[0, x] = results[0] - force_scale * force_ref[x]
        out_ref[1, x] = results[1]
        out_ref[2, x] = results[2]
        return carry

    lax.fori_loop(0, planes, body, 0)


def stencil(velocity, halos, forcing):
    vmem = pl.BlockSpec(memory_space=pltpu.VMEM)
    return pl.pallas_call(
        stencil_kernel,
        out_shape=jax.ShapeDtypeStruct(velocity.shape, velocity.dtype),
        in_specs=[vmem] * 6,
        out_specs=vmem,
    )(velocity, *halos, forcing)


def halo_faces(velocity):
    faces = []
    for axis, dim in (("slab", 1), ("cross", 2)):
        count = lax.axis_size(axis)
        size = velocity.shape[dim]
        head = lax.slice_in_dim(velocity, 0, 1, axis=dim).astype(jnp.bfloat16)
        tail = lax.slice_in_dim(velocity, size - 1, size, axis=dim).astype(jnp.bfloat16)
        low = lax.ppermute(tail, axis, [(i, i + 1) for i in range(count - 1)])
        high = lax.ppermute(head, axis, [(i + 1, i) for i in range(count - 1)])
        faces += [jnp.squeeze(low, dim), jnp.squeeze(high, dim)] if dim == 1 else [low, high]
    return faces


def extended(cells, sides, width):
    for axis, dim in sides:
        count = lax.axis_size(axis)
        ends = count - 1
        head = lax.slice_in_dim(cells, 0, width, axis=dim)
        tail = lax.slice_in_dim(cells, cells.shape[dim] - width, cells.shape[dim], axis=dim)
        cells = jnp.concatenate(
            [
                lax.ppermute(tail, axis, [(i, (i + 1) % count) for i in range(ends)]),
                cells,
                lax.ppermute(head, axis, [((i + 1) % count, i) for i in range(ends)]),
            ],
            axis=dim,
        )
    return cells


def combine_terms(velocity, east, west, north, south, upper, lower):
    laplace = east + west + north + south + upper + lower - 6.0 * velocity
    advect = (
        velocity[0:1] * ((east - west) * 0.5)
        + velocity[1:2] * ((north - south) * 0.5)
        + velocity[2:3] * ((upper - lower) * 0.5)
    )
    return velocity + time_step * (viscosity * laplace - advect)


def on_device(
    velocity,
    shape_weight,
    w_in,
    w_out,
    decay,
    rotor_states,
    slot_of_rotor,
    entry_rotor,
    entry_tile,
    entry_sub,
):
    local_x, local_y, local_z = (velocity.shape[1], velocity.shape[2], velocity.shape[3])
    tile_count = local_x * local_y * local_z // TILE
    rotor_hot = (entry_rotor == jnp.arange(R, dtype=jnp.int32)[None, :]).astype(jnp.int32)
    slots = jnp.sum(rotor_hot * slot_of_rotor[None, :], axis=1)
    high = lax.reduce_precision(shape_weight, exponent_bits=8, mantissa_bits=7)
    rest = shape_weight - high
    middle = lax.reduce_precision(rest, exponent_bits=8, mantissa_bits=7)
    low = rest - middle
    parts = jnp.stack([high, middle, low]).astype(jnp.bfloat16)
    halves = local_z // TILE
    code = (((entry_tile // halves) * NSUB + entry_sub) * R + slots) * halves + entry_tile % halves
    new_states, advanced = reduce_step((parts, code[:, None]), rotor_states, velocity, w_in, decay, w_out)
    return (advanced, new_states)


def solution(mesh):
    in_specs = (
        P(None, "slab", "cross", None),
        P(),
        P(),
        P(),
        P(),
        P("slab", None),
        P(),
        P(("slab", "cross"), None),
        P(("slab", "cross")),
        P(("slab", "cross")),
    )
    out_specs = (P(None, "slab", "cross", None), P("slab", None))
    return jax.shard_map(
        on_device, mesh=mesh, in_specs=in_specs, out_specs=out_specs, check_vma=False
    )
```
